32 devices in a mesh: section: 4 (over y, x), ctx: 8 (over z, core).
Axes of the slice: x: 2, y: 2, z: 4, core: 2. Of those that a mesh axis runs over, the one named last changes fastest.
Arguments:
- resid: bfloat16 [4, 1024, 6144], P('section', 'ctx'), may hold values from -6 to 6
- queries: bfloat16 [4, 1024, 6144], P('section', 'ctx'), may hold values from -6 to 6
- keys: bfloat16 [4, 1024, 6144], P('section', 'ctx'), may hold values from -6 to 6
- values: bfloat16 [4, 1024, 6144], P('section', 'ctx'), may hold values from -6 to 6
- log_decay: float32 [4, 1024, 48], P('section', 'ctx'), may hold values from -3 to 0
- attn_gain: float32 [4, 6144], P('section'), may hold values from 0.25 to 1.75
- moe_gain: float32 [4, 6144], P('section'), may hold values from 0.25 to 1.75
- experts: int32 [4, 1024, 2], P('section', 'ctx'), may hold values from 0 to 31, all different within a row; in each aligned block of 128 rows (0 to 127, 128 to 255, ..., all dimensions but the last counted through in order) at most 16 rows name the same one
- combine_weight: float32 [4, 1024, 2], P('section', 'ctx'), may hold values from 0.2 to 1
- w_up: bfloat16 [4, 6144, 5120], P('section', None, 'ctx'), may hold values from -0.078125 to 0.078125
- w_down: bfloat16 [4, 5120, 6144], P('section', 'ctx'), may hold values from -0.078125 to 0.078125
Outputs:
- received: bfloat16 [4, 1024, 6144], P('section', 'ctx')
The draws below stay inside these ranges and needn't reach their ends.
Inputs may be any that keep to these rules, and one draw needn't show every extreme that they name: In the rows of one device each expert is named at most 16 times, and the two experts of a token differ.
All inputs are finite; a program needn't handle non-finite values.
Results may differ from the reference program's by a relative error of at most 0.002.
Values may be sent and summed in bfloat16 or wider, within the bound.
No kernel may reach another device: no remote copies, remote signals or barrier semaphores. Data moves between devices by JAX's collectives and lax.ppermute only.
A program may use at most 256 MiB of HBM per device.

```python
import math
import jax
import jax.numpy as jnp
import numpy as np
from jax import lax

D = 6144
LINEAR_HEADS = 48
HEAD = 128
EXPERTS = 32
FF = 5120
SHARDS = 8
CAP_SRC = 16
TOK_DEV = 128
SECTION_TOKENS = 1024
RELAY_SECTIONS = 4
EXP_FLY = 1
FF_DEV = 640


def draw_log_decay(key, part):
    random_parts_key = jax.random.split(key, 7)
    fraction = 0.5
    quick_heads = jax.random.uniform(random_parts_key[0], (RELAY_SECTIONS, 1, LINEAR_HEADS)) < fraction
    slow_rate = jax.random.uniform(random_parts_key[1], (RELAY_SECTIONS, 1, LINEAR_HEADS), minval=0.2, maxval=0.6) / SECTION_TOKENS
    fast_rate = jax.random.uniform(random_parts_key[2], (RELAY_SECTIONS, 1, LINEAR_HEADS), minval=2.5, maxval=4.2) / TOK_DEV
    baseline_rate = jnp.where(quick_heads, fast_rate, slow_rate)
    block_count = SECTION_TOKENS // TOK_DEV
    processor_rate = jax.random.uniform(random_parts_key[3], (RELAY_SECTIONS, block_count, 1, LINEAR_HEADS), minval=0.6, maxval=1.5)
    processor_rate = jnp.broadcast_to(processor_rate, (RELAY_SECTIONS, block_count, TOK_DEV, LINEAR_HEADS)).reshape(RELAY_SECTIONS, SECTION_TOKENS, LINEAR_HEADS)
    jaggedness = jax.random.uniform(random_parts_key[4], (RELAY_SECTIONS, SECTION_TOKENS, LINEAR_HEADS), minval=0.5, maxval=1.5)
    spike_positions = jax.random.randint(random_parts_key[5], (RELAY_SECTIONS, 1, 4), 0, SECTION_TOKENS)
    spike_struck = jnp.any(jnp.arange(SECTION_TOKENS)[None, :, None] == spike_positions, axis=2)[:, :, None]
    spike_penalty = jax.random.uniform(random_parts_key[6], (RELAY_SECTIONS, SECTION_TOKENS, LINEAR_HEADS), minval=0.2, maxval=0.4)
    final_result = -baseline_rate * processor_rate * jaggedness + jnp.where(spike_struck, jnp.log1p(-spike_penalty), 0.0)
    return final_result.astype(jnp.float32)


def block_levels(rng, dims, cuts, smallest, high):
    def one(axis_at, blocks):
        heights = jax.random.uniform(jax.random.fold_in(jax.random.fold_in(rng, 6), axis_at), (blocks,), jnp.float32, smallest / len(cuts), high / len(cuts))
        return jnp.repeat(jnp.exp(heights), dims[axis_at] // blocks).reshape((-1,) + (1,) * (len(dims) - axis_at - 1))

    loudness = one(*cuts[0])
    for cut in cuts[1:]:
        loudness = loudness * one(*cut)
    return loudness


def assign_block(rng, own, number, rows, count, top, reach, skew):
    order = jax.random.permutation(rng, count)
    crowded, usual = portions_of(count, rows * top, reach, skew, True), portions_of(count, rows * top, reach, skew, False)
    places = jnp.arange(count)

    def named(tallies, offset_by):
        used = int((tallies > 0).sum())
        fixed = max(1, used // 4)
        shifted = fixed + (places - fixed + offset_by * (used - fixed)) % max(1, count - fixed)
        return jnp.zeros((count,), jnp.int32).at[order[jnp.where(places < fixed, places, shifted)]].set(jnp.asarray(tallies, jnp.int32))

    tallies = jnp.where(number % 4 == 0, named(crowded, number // 4), named(usual, number - number // 4 - 1))
    mixed = jax.random.permutation(jax.random.fold_in(own, 3), count)
    source_of, taker = mixed[0:count // 2 * 2:2], mixed[1:count // 2 * 2:2]
    slack = jnp.minimum(tallies[source_of] - 1, reach - tallies[taker]) // 2
    slack = jnp.where((source_of == order[0]) | (taker == order[0]) | (tallies[taker] == 0), 0, jnp.maximum(slack, 0))
    shifted = jax.random.randint(jax.random.fold_in(own, 4), (count // 2,), 0, 1 << 20) % (slack + 1)
    tallies = tallies.at[source_of].add(-shifted).at[taker].add(shifted)
    items = jnp.searchsorted(jnp.cumsum(tallies), jnp.arange(rows * top), side="right").astype(jnp.int32)
    table = items.reshape(top, rows).T
    table = table[jax.random.permutation(jax.random.fold_in(own, 1), rows)]
    offset_by = jax.random.randint(jax.random.fold_in(own, 2), (rows, 1), 0, top)
    return jnp.take_along_axis(table, (jnp.arange(top)[None, :] + offset_by) % top, axis=1)


def portions_of(count, total, most, skew, full):
    loads = [(1 << 20) // math.isqrt(rank ** skew) + 1 for rank in range(1, count + 1)]
    largest = most if full else min(most, max(-(-total // count), total * loads[0] // sum(loads)))
    least = 1 if total - largest >= count - 1 else 0
    holding, rest = [largest] + [least] * (count - 1), total - largest - least * (count - 1)
    while rest > 0:
        movable = [i for i in range(1, count) if holding[i] < largest] or [i for i in range(1, count) if holding[i] < most]
        mass, remaining = sum([loads[i] for i in movable]), rest
        for i in movable:
            more = min(most - holding[i], max(1, remaining * loads[i] // mass), rest)
            holding[i] = holding[i] + more
            rest = rest - more
    return np.array(holding)


def bell_draw(stream_key, shape, scale, bound, shards=(), held_as=jnp.bfloat16):
    result = scale * jax.random.normal(stream_key, shape, jnp.float32)
    if shards:
        result = result * block_levels(stream_key, shape, shards, -0.22, 0.18)
    return jnp.clip(result, -bound, bound).astype(held_as)


def setup_inputs(seed: int = 0) -> dict:
    key_of = jax.random.split(jax.random.key(seed), 12)
    resid = bell_draw(key_of[0], (RELAY_SECTIONS, SECTION_TOKENS, D), 1.0, 6.0, ((0, 4), (1, 8)))
    queries = bell_draw(key_of[1], (RELAY_SECTIONS, SECTION_TOKENS, D), 1.0, 6.0, ((0, 4), (1, 8)))
    keys = bell_draw(key_of[2], (RELAY_SECTIONS, SECTION_TOKENS, D), 1.0, 6.0, ((0, 4), (1, 8)))
    values = bell_draw(key_of[3], (RELAY_SECTIONS, SECTION_TOKENS, D), 1.0, 6.0, ((0, 4), (1, 8)))
    log_decay = draw_log_decay(jax.random.fold_in(key_of[11], 71), 0)
    attn_gain = jnp.clip(1.0 + 0.15 * jax.random.normal(key_of[5], (RELAY_SECTIONS, D), jnp.float32), 0.25, 1.75)
    moe_gain = jnp.clip(1.0 + 0.15 * jax.random.normal(key_of[6], (RELAY_SECTIONS, D), jnp.float32), 0.25, 1.75)
    experts_keys = jax.random.split(jax.random.fold_in(key_of[7], 1), RELAY_SECTIONS * SECTION_TOKENS // TOK_DEV)
    experts_turns = jax.random.permutation(jax.random.fold_in(key_of[7], 3), RELAY_SECTIONS * SECTION_TOKENS // TOK_DEV)
    experts = jax.vmap(lambda own, number: assign_block(jax.random.fold_in(key_of[7], 2), own, number, TOK_DEV, EXPERTS, 2, CAP_SRC, 2))(experts_keys, experts_turns).reshape((RELAY_SECTIONS, SECTION_TOKENS, 2))
    combine_weight = jnp.clip(0.2 + 0.8 * jax.random.uniform(key_of[8], (RELAY_SECTIONS, SECTION_TOKENS, 2), jnp.float32) ** block_levels(key_of[8], (RELAY_SECTIONS, SECTION_TOKENS, 2), ((0, 4), (1, 8)), -0.2, 0.2), 0.2, 1.0)
    w_up = bell_draw(key_of[9], (RELAY_SECTIONS, D, EXP_FLY * FF), D ** -0.5, 0.078125, ((0, 4), (2, 8)))
    w_down = bell_draw(key_of[10], (RELAY_SECTIONS, EXP_FLY * FF, D), FF ** -0.5, 0.078125, ((0, 4), (1, 8)))
    return dict(resid=resid, queries=queries, keys=keys, values=values, log_decay=log_decay, attn_gain=attn_gain, moe_gain=moe_gain, experts=experts, combine_weight=combine_weight, w_up=w_up, w_down=w_down)


HIGH = lax.Precision.HIGHEST

def block_attention(query, keyrows, valrows, log_rate):
    cumul = jnp.cumsum(log_rate, axis=0)
    scores = jnp.einsum('thd,shd->hts', query, keyrows, precision=HIGH)
    spread = cumul.T[:, :, None] - cumul.T[:, None, :]
    length = log_rate.shape[0]
    lower = jnp.arange(length)[:, None] >= jnp.arange(length)[None, :]
    weights = jnp.exp(jnp.where(lower[None], spread, -1e+30))
    intra = jnp.einsum('hts,shd->thd', scores * weights, valrows, precision=HIGH)
    tail_decay = jnp.exp(cumul[-1][None, :] - cumul)
    state = jnp.einsum('thd,the->hde', keyrows * tail_decay[:, :, None], valrows, precision=HIGH)
    return (intra, cumul, jnp.exp(cumul[-1]), state)

def attention_section(queries, keys, values, log_decay):
    blocks = SECTION_TOKENS // TOK_DEV
    qrows = queries.astype(jnp.float32).reshape(blocks, TOK_DEV, LINEAR_HEADS, HEAD)
    krows = keys.astype(jnp.float32).reshape(blocks, TOK_DEV, LINEAR_HEADS, HEAD)
    vrows = values.astype(jnp.float32).reshape(blocks, TOK_DEV, LINEAR_HEADS, HEAD)
    lrows = log_decay.reshape(blocks, TOK_DEV, LINEAR_HEADS)

    def advance(carry, inputs):
        query, keyrows, valrows, log_rate = inputs
        intra, cumul, decay, state = block_attention(query, keyrows, valrows, log_rate)
        inter = jnp.exp(cumul)[:, :, None] * jnp.einsum('thd,hde->the', query, carry, precision=HIGH)
        carry = decay[:, None, None] * carry + state
        return (carry, (intra + inter).reshape(TOK_DEV, D))
    start_state = jnp.zeros((LINEAR_HEADS, HEAD, HEAD), jnp.float32)
    _, outputs = lax.scan(advance, start_state, (qrows, krows, vrows, lrows))
    return outputs.reshape(SECTION_TOKENS, D)

def rms_scale(values_in, gain):
    return values_in * lax.rsqrt(lax.optimization_barrier(jnp.mean(values_in * values_in, axis=-1, keepdims=True)) + 1e-06) * gain

def slots_of(chosen):
    onehot = (chosen[:, None] == jnp.arange(EXPERTS)[None, :]).astype(jnp.int32)
    before = jnp.cumsum(onehot, axis=0) - onehot
    return lax.optimization_barrier(jnp.sum(before * onehot, axis=1)).astype(jnp.int32)

def moe_section(normed, experts, combine_weight, w_up, w_down):
    blocks = SECTION_TOKENS // TOK_DEV
    chosen = experts.reshape(blocks, 2 * TOK_DEV)
    slot = jax.vmap(slots_of)(chosen)
    source = jnp.arange(blocks, dtype=jnp.int32)[:, None]
    token_of = (source * TOK_DEV + jnp.arange(2 * TOK_DEV, dtype=jnp.int32)[None, :] // 2).reshape(-1)
    total_rows = blocks * CAP_SRC
    gathered = jnp.zeros((2 * SECTION_TOKENS, D), jnp.float32)
    for expert_id in range(EXP_FLY):
        taken = (chosen == expert_id).reshape(-1)
        target = jnp.where(taken, (source * CAP_SRC + slot).reshape(-1), total_rows).astype(jnp.int32)
        rows = jnp.zeros((total_rows, D), jnp.bfloat16).at[target].set(normed[token_of], mode='drop')
        summed = jnp.zeros((total_rows, D), jnp.float32)
        for shard in range(SHARDS):
            first = expert_id * FF + shard * FF_DEV
            hidden = jax.nn.gelu(jnp.dot(rows, w_up[:, first:first + FF_DEV], preferred_element_type=jnp.float32), approximate=True).astype(jnp.bfloat16)
            part = jnp.dot(hidden, w_down[first:first + FF_DEV, :], preferred_element_type=jnp.float32).astype(jnp.bfloat16)
            summed = summed + part.astype(jnp.float32)
        picked = jnp.take(summed, jnp.clip(target, 0, total_rows - 1), axis=0)
        gathered = gathered + jnp.where(taken[:, None], picked, 0.0)
    weighted = gathered * combine_weight.reshape(-1)[:, None]
    return weighted.reshape(SECTION_TOKENS, 2, D).sum(axis=1)

def reference(resid, queries, keys, values, log_decay, attn_gain, moe_gain, experts, combine_weight, w_up, w_down):
    outputs = []
    for section_id in range(RELAY_SECTIONS):
        attn_raw = attention_section(queries[section_id], keys[section_id], values[section_id], log_decay[section_id])
        hres = resid[section_id].astype(jnp.float32) + rms_scale(attn_raw, attn_gain[section_id])
        normed = rms_scale(hres, moe_gain[section_id]).astype(jnp.bfloat16)
        mixed = moe_section(normed, experts[section_id], combine_weight[section_id], w_up[section_id], w_down[section_id])
        outputs.append((hres + mixed).astype(jnp.bfloat16))
    layer_out = jnp.stack(outputs)
    return jnp.roll(layer_out, 1, axis=0)
```

```python
import jax
import jax.numpy as jnp
from jax import lax
from jax.sharding import PartitionSpec as P

HEAD = 128
EXPERTS = 32
SHARDS = 8
CAP_SRC = 16
CHUNKS = 6
LAG = 2

HIGH = lax.Precision.HIGHEST


def passed_along(value, axis, steps):
    count = lax.axis_size(axis)
    pairs = [(source, (source + steps) % count) for source in range(count)]
    return lax.ppermute(value, axis, pairs)


def swapped(value):
    count = lax.axis_size("ctx")
    return lax.ppermute(value, "ctx", [(i, i ^ 1) for i in range(count)])


def rms_scale(values_in, gain):
    return (
        values_in
        * lax.rsqrt(jnp.mean(values_in * values_in, axis=-1, keepdims=True) + 1e-06)
        * gain
    )


def slots_of(chosen):
    onehot = (chosen[:, None] == jnp.arange(EXPERTS)[None, :]).astype(jnp.int32)
    before = jnp.cumsum(onehot, axis=0) - onehot
    return jnp.sum(before * onehot, axis=1)


def chain_prefix(total, decay, chip, chips, scale):
    heads = total.shape[0]
    per = heads // CHUNKS
    received = []
    for step in range(CHUNKS + LAG * (chips - 2)):
        place = jnp.clip(step - LAG * chip, 0, CHUNKS - 1) * per
        gone = lax.dynamic_slice_in_dim(total, place, per, 0)
        if step >= LAG:
            before = received[step - LAG].astype(jnp.float32)
            gone = lax.dynamic_slice_in_dim(decay, place, per, 0)[:, None, None] * before + gone * scale
        else:
            gone = gone * scale
        gone = gone.astype(jnp.float16)
        arrived = None
        for parity in range(2):
            active = [
                z for z in range(parity, chips - 1, 2) if 0 <= step - LAG * z < CHUNKS
            ]
            if active:
                pairs = [(2 * z + core, 2 * z + 2 + core) for z in active for core in range(2)]
                moved = lax.ppermute(gone, "ctx", pairs)
                arrived = moved if arrived is None else arrived + moved
        received.append(arrived)
    row = jnp.concatenate(received, axis=0)
    first = jnp.maximum(chip - 1, 0) * LAG * per
    mine = lax.dynamic_slice_in_dim(row, first, heads, 0).astype(jnp.float32) / scale
    return jnp.where(chip > 0, mine, 0.0)


def state_prefix(decay, state):
    count = lax.axis_size("ctx")
    me = lax.axis_index("ctx")
    chips, chip, core = count // 2, me // 2, me % 2
    half = state.shape[0] // 2
    tokens = count * 128
    scale = 1.0
    while 36.0 * tokens * scale > 65000.0:
        scale = scale / 2
    mine = lax.dynamic_slice_in_dim(state, core * half, half, 0)
    other = lax.dynamic_slice_in_dim(state, (1 - core) * half, half, 0)
    partner = swapped(other)
    partner_decay = lax.dynamic_slice_in_dim(swapped(decay), core * half, half, 0)
    my_decay = lax.dynamic_slice_in_dim(decay, core * half, half, 0)
    first = core == 0
    state0, state1 = jnp.where(first, mine, partner), jnp.where(first, partner, mine)
    decay0, decay1 = jnp.where(first, my_decay, partner_decay), jnp.where(first, partner_decay, my_decay)
    total = decay1[:, None, None] * state0 + state1
    prefix = chain_prefix(total, decay0 * decay1, chip, chips, scale)
    after0 = decay0[:, None, None] * prefix + state0
    give = jnp.where(first, after0, prefix)
    keep = jnp.where(first, prefix, after0)
    got = swapped(give)
    return jnp.where(first, jnp.concatenate([keep, got]), jnp.concatenate([got, keep]))


def local(
    resid,
    queries,
    keys,
    values,
    log_decay,
    attn_gain,
    moe_gain,
    experts,
    combine_weight,
    w_up,
    w_down,
):
    length, width = queries.shape[1:]
    heads = width // HEAD
    query = queries[0].astype(jnp.float32).reshape(length, heads, HEAD)
    keyrows = keys[0].astype(jnp.float32).reshape(length, heads, HEAD)
    valrows = values[0].astype(jnp.float32).reshape(length, heads, HEAD)
    log_rate = log_decay[0]
    cumul = jnp.cumsum(log_rate, axis=0)
    tail_decay = jnp.exp(cumul[-1][None, :] - cumul)
    state = jnp.einsum("thd,the->hde", keyrows * tail_decay[:, :, None], valrows, precision=HIGH)
    prefix = state_prefix(jnp.exp(cumul[-1]), state)
    scores = jnp.einsum("thd,shd->hts", query, keyrows, precision=HIGH)
    spread = cumul.T[:, :, None] - cumul.T[:, None, :]
    lower = jnp.arange(length)[:, None] >= jnp.arange(length)[None, :]
    weights = jnp.exp(jnp.where(lower[None], spread, -1e30))
    intra = jnp.einsum("hts,shd->thd", scores * weights, valrows, precision=HIGH)
    inter = jnp.exp(cumul)[:, :, None] * jnp.einsum(
        "thd,hde->the", query, prefix, precision=HIGH
    )
    attn_raw = (intra + inter).reshape(length, width)
    hres = resid[0].astype(jnp.float32) + rms_scale(attn_raw, attn_gain[0])
    normed = rms_scale(hres, moe_gain[0]).astype(jnp.bfloat16)

    count = lax.axis_size("ctx")
    flying = count // SHARDS
    me = lax.axis_index("ctx")
    chosen = experts[0].reshape(-1)
    slot = slots_of(chosen)
    target = chosen * CAP_SRC + slot
    in_window = chosen < flying
    slots = flying * CAP_SRC
    hot = (target[None, :] == jnp.arange(slots)[:, None]) & in_window[None, :]
    hot = hot.reshape(slots, length, 2)
    select = hot.any(axis=2)
    weight_of = jnp.where(hot, combine_weight[0][None], 0.0).sum(axis=2)
    up_local, down_local = w_up[0], w_down[0]

    def expert(rows):
        hidden = jax.nn.gelu(
            jnp.dot(rows, up_local, preferred_element_type=jnp.float32), approximate=True
        ).astype(jnp.bfloat16)
        return jnp.dot(hidden, down_local, preferred_element_type=jnp.float32).astype(jnp.bfloat16)

    outbox = jnp.dot(
        select.astype(jnp.bfloat16), normed, preferred_element_type=jnp.float32
    ).astype(jnp.bfloat16)
    if flying == 1:
        early = passed_along(hres.astype(jnp.bfloat16), "section", 1)
        place = passed_along(
            jnp.where(select.any(axis=0), select.astype(jnp.float32).T @ jnp.arange(slots, dtype=jnp.float32), -1.0)[None],
            "section",
            1,
        )
        chips = count // 2
        core = me % 2
        own = [outbox] + [
            lax.ppermute(outbox, "ctx", [(i, (i + 2 * d) % count) for i in range(count)])
            for d in range(1, chips)
        ]
        own = jnp.stack(own)
        both = jnp.concatenate([own, swapped(own)])
        part = expert(both.reshape(2 * chips * CAP_SRC, width)).reshape(2, chips, CAP_SRC, width)
        pair = part[0].astype(jnp.float32) + swapped(part[1]).astype(jnp.float32)
        pair = pair.astype(jnp.bfloat16)
        summed = pair[0].astype(jnp.float32)
        for d in range(1, chips):
            back = lax.ppermute(pair[d], "ctx", [(i, (i - 2 * d) % count) for i in range(count)])
            summed = summed + back.astype(jnp.float32)
        picked = jnp.dot(select.astype(jnp.float32), hres, precision=HIGH)
        late = (picked + weight_of.sum(axis=1)[:, None] * summed).astype(jnp.bfloat16)
        late = passed_along(late, "section", 1)
        found = (place == jnp.arange(slots, dtype=jnp.float32)[:, None]).astype(jnp.bfloat16)
        spread_rows = lax.dot_general(
            found, late, (((0,), (0,)), ((), ())), preferred_element_type=jnp.float32
        ).astype(jnp.bfloat16)
        return jnp.where(place[0][:, None] >= 0, spread_rows, early)[None]
    my_expert = me // SHARDS
    outbox = outbox.reshape(flying, CAP_SRC, width)
    mine = lax.dynamic_index_in_dim(
        lax.all_gather(outbox[None], "ctx", axis=0, tiled=True), my_expert, 1, False
    )
    part = expert(mine.reshape(count * CAP_SRC, width)).reshape(count, CAP_SRC, width)
    returned = lax.all_to_all(part, "ctx", split_axis=0, concat_axis=0, tiled=True)
    summed = returned.reshape(flying, SHARDS, CAP_SRC, width).astype(jnp.float32).sum(axis=1)
    mixed = lax.dot_general(
        weight_of, summed.reshape(slots, width), (((0,), (0,)), ((), ())), precision=HIGH
    )
    layer_out = (hres + mixed).astype(jnp.bfloat16)
    return passed_along(layer_out[None], "section", 1)


def solution(mesh):
    return jax.shard_map(
        local,
        mesh=mesh,
        in_specs=(
            P("section", "ctx", None),
            P("section", "ctx", None),
            P("section", "ctx", None),
            P("section", "ctx", None),
            P("section", "ctx", None),
            P("section", None),
            P("section", None),
            P("section", "ctx", None),
            P("section", "ctx", None),
            P("section", None, "ctx"),
            P("section", "ctx", None),
        ),
        out_specs=P("section", "ctx", None),
        check_vma=False,
    )
```

```python
import jax
import jax.numpy as jnp
from jax import lax
from jax.experimental import pallas as pl
from jax.experimental.pallas import tpu as pltpu
from jax.sharding import PartitionSpec as P

HEAD = 128
SHARDS = 8
CAP_SRC = 16
GROUP = 8
CHUNKS = 4

F32, BF16 = jnp.float32, jnp.bfloat16


def dot(a, b, dims=((1,), (0,))):
    return lax.dot_general(a, b, (dims, ((), ())), preferred_element_type=F32)


def split(a):
    hi = a.astype(BF16)
    return hi, (a - hi.astype(F32)).astype(BF16)


def cumul_rows(rate, cum_ref):
    length = rate.shape[0]
    upper = (
        lax.broadcasted_iota(jnp.int32, (length, length), 0)
        <= lax.broadcasted_iota(jnp.int32, (length, length), 1)
    ).astype(F32)
    cum_ref[...] = lax.dot_general(
        rate, upper, (((0,), (0,)), ((), ())), precision=lax.Precision.HIGHEST,
        preferred_element_type=F32,
    )


def state_kernel(half_ref, rate_ref, k_ref, v_ref, state_ref, decay_ref, cum_ref):
    step = pl.program_id(0)
    length = rate_ref.shape[0]

    @pl.when(step == 0)
    def _():
        cumul_rows(rate_ref[...], cum_ref)
        last = cum_ref[:, length - 1 :]
        decay_ref[...] = jnp.broadcast_to(jnp.exp(last), decay_ref.shape)

    row = (half_ref[0] * pl.num_programs(0) + step) * GROUP
    cum = cum_ref[pl.ds(pl.multiple_of(row, GROUP), GROUP), :]
    tail = jnp.exp(cum[:, length - 1 :] - cum)
    for j in range(GROUP):
        cols = slice(j * HEAD, (j + 1) * HEAD)
        turned = k_ref[:, cols].astype(F32).T * tail[j : j + 1, :]
        hi, lo = split(turned)
        v = v_ref[:, cols]
        state_ref[j] = dot(hi, v) + dot(lo, v)


def half_state(half, rate, keys, values):
    length, width = keys.shape
    heads = width // HEAD
    steps = heads // 2 // GROUP
    block = pl.BlockSpec((length, GROUP * HEAD), lambda i, h: (0, h[0] * steps + i))
    return pl.pallas_call(
        state_kernel,
        grid_spec=pltpu.PrefetchScalarGridSpec(
            num_scalar_prefetch=1,
            grid=(steps,),
            in_specs=[pl.BlockSpec((length, heads), lambda i, h: (0, 0)), block, block],
            out_specs=[
                pl.BlockSpec((GROUP, HEAD, HEAD), lambda i, h: (i, 0, 0)),
                pl.BlockSpec((heads, HEAD), lambda i, h: (0, 0)),
            ],
            scratch_shapes=[pltpu.VMEM((heads, length), F32)],
        ),
        out_shape=[
            jax.ShapeDtypeStruct((heads // 2, HEAD, HEAD), F32),
            jax.ShapeDtypeStruct((heads, HEAD), F32),
        ],
        name="half_state",
    )(half, rate, keys, values)


def intra_kernel(rate_ref, q_ref, k_ref, v_ref, out_ref, cum_ref):
    step = pl.program_id(0)
    length = rate_ref.shape[0]

    @pl.when(step == 0)
    def _():
        cumul_rows(rate_ref[...], cum_ref)

    lower = lax.broadcasted_iota(jnp.int32, (length, length), 0) >= lax.broadcasted_iota(
        jnp.int32, (length, length), 1
    )
    cum = cum_ref[pl.ds(pl.multiple_of(step * GROUP, GROUP), GROUP), :]
    for j in range(GROUP):
        cols = slice(j * HEAD, (j + 1) * HEAD)
        across = jnp.broadcast_to(cum[j : j + 1, :], (length, length))
        weights = jnp.exp(jnp.where(lower, across.T - across, -1e30))
        scores = dot(q_ref[:, cols], k_ref[:, cols], ((1,), (1,)))
        hi, lo = split(scores * weights)
        v = v_ref[:, cols]
        out_ref[:, cols] = dot(hi, v) + dot(lo, v)


def intra_attention(rate, queries, keys, values):
    length, width = keys.shape
    heads = width // HEAD
    block = pl.BlockSpec((length, GROUP * HEAD), lambda i: (0, i))
    return pl.pallas_call(
        intra_kernel,
        grid=(heads // GROUP,),
        in_specs=[pl.BlockSpec((length, heads), lambda i: (0, 0)), block, block, block],
        out_specs=block,
        out_shape=jax.ShapeDtypeStruct((length, width), F32),
        scratch_shapes=[pltpu.VMEM((heads, length), F32)],
        name="intra_attention",
    )(rate, queries, keys, values)


def finish_kernel(
    core_ref, rate_ref, q_ref, intra_ref, keep_ref, got_ref, resid_ref, again_ref, mgain_ref,
    experts_ref, weight_ref, early_ref, outbox_ref, picked_ref, wcol_ref, place_ref,
    cum_ref, attn_ref, normed_ref,
):
    step = pl.program_id(0)
    steps = pl.num_programs(0)
    length, width = resid_ref.shape

    @pl.when(step == 0)
    def _():
        cumul_rows(rate_ref[...], cum_ref)

    place = lax.rem(step + core_ref[0] * (steps // 2), steps)
    cum = cum_ref[pl.ds(pl.multiple_of(place * GROUP, GROUP), GROUP), :]

    def inter(prefix_ref):
        for j in range(GROUP):
            cols = slice(j * HEAD, (j + 1) * HEAD)
            across = jnp.broadcast_to(jnp.exp(cum[j : j + 1, :]), (length, length))
            hi, lo = split(prefix_ref[j])
            q = q_ref[:, cols]
            value = intra_ref[:, cols] + across.T * (dot(q, hi) + dot(q, lo))
            column = pl.multiple_of(place * (GROUP * HEAD) + j * HEAD, HEAD)
            attn_ref[:, pl.ds(column, HEAD)] = value

    @pl.when(step < steps // 2)
    def _():
        inter(keep_ref)

    @pl.when(step >= steps // 2)
    def _():
        inter(got_ref)

    @pl.when(step == steps - 1)
    def _():
        rows = 16

        def norm(r, carry):
            at = pl.ds(pl.multiple_of(r * rows, rows), rows)
            x = attn_ref[at, :]
            scale = lax.rsqrt(jnp.mean(x * x, axis=-1, keepdims=True) + 1e-06)
            hres = resid_ref[at, :].astype(F32) + x * scale * again_ref[...]
            attn_ref[at, :] = hres
            early_ref[at, :] = hres.astype(BF16)
            scale = lax.rsqrt(jnp.mean(hres * hres, axis=-1, keepdims=True) + 1e-06)
            normed_ref[at, :] = (hres * scale * mgain_ref[...]).astype(BF16)
            return carry

        lax.fori_loop(0, length // rows, norm, 0)
        slots = outbox_ref.shape[0]
        before = (
            lax.broadcasted_iota(jnp.int32, (length, length), 0)
            < lax.broadcasted_iota(jnp.int32, (length, length), 1)
        ).astype(BF16)
        named = experts_ref[...] == 0
        taken = jnp.max(named.astype(F32), axis=0, keepdims=True)
        slot = dot(jnp.broadcast_to(taken, (8, length)).astype(BF16), before)[0:1, :]
        slot = jnp.where(taken > 0, slot, -1.0)
        place_ref[...] = jnp.broadcast_to(slot, place_ref.shape)
        hot = lax.broadcasted_iota(jnp.int32, (slots, length), 0).astype(F32) == slot
        weight = jnp.sum(jnp.where(named, weight_ref[...], 0.0), axis=0, keepdims=True)
        weight = jnp.sum(jnp.where(hot, weight, 0.0), axis=1, keepdims=True)
        wcol_ref[...] = jnp.broadcast_to(weight, wcol_ref.shape)
        hot = hot.astype(BF16)
        outbox_ref[...] = dot(hot, normed_ref[...]).astype(BF16)
        for c in range(width // 512):
            cols = slice(c * 512, (c + 1) * 512)
            x = attn_ref[:, cols]
            hi, rest = x.astype(BF16), None
            rest = x - hi.astype(F32)
            mid, low = split(rest)
            picked_ref[:, cols] = dot(hot, hi) + dot(hot, mid) + dot(hot, low)


def finish(core, rate, queries, intra, keep, got, resid, attn_gain, moe_gain, experts, weight):
    length, width = queries.shape
    heads = width // HEAD
    steps = heads // GROUP
    half = steps // 2

    def whole(shape):
        return pl.BlockSpec(shape, lambda i, c: (0,) * len(shape))

    block = pl.BlockSpec((length, GROUP * HEAD), lambda i, c: (0, lax.rem(i + c[0] * half, steps)))
    states = (GROUP, HEAD, HEAD)
    outs = [
        ((length, width), BF16),
        ((CAP_SRC, width), BF16),
        ((CAP_SRC, width), F32),
        ((CAP_SRC, 128), F32),
        ((8, length), F32),
    ]
    return pl.pallas_call(
        finish_kernel,
        grid_spec=pltpu.PrefetchScalarGridSpec(
            num_scalar_prefetch=1,
            grid=(steps,),
            in_specs=[
                whole((length, heads)),
                block,
                block,
                pl.BlockSpec(states, lambda i, c: (jnp.minimum(i, half - 1), 0, 0)),
                pl.BlockSpec(states, lambda i, c: (jnp.maximum(i - half, 0), 0, 0)),
                whole((length, width)),
                whole((1, width)),
                whole((1, width)),
                whole((2, length)),
                whole((2, length)),
            ],
            out_specs=[whole(shape) for shape, _ in outs],
            scratch_shapes=[
                pltpu.VMEM((heads, length), F32),
                pltpu.VMEM((length, width), F32),
                pltpu.VMEM((length, width), BF16),
            ],
        ),
        out_shape=[jax.ShapeDtypeStruct(*out) for out in outs],
        name="finish",
    )(core, rate, queries, intra, keep, got, resid, attn_gain, moe_gain, experts, weight)


def expert_kernel(count, *refs):
    row_refs, (up_ref, down_ref, mine_ref, other_ref, acc_ref, hidden_ref) = refs[:count], refs[count:]
    step = pl.program_id(0)
    steps = pl.num_programs(0) // 2
    block = up_ref.shape[0]

    @pl.when(step < steps)
    def _():
        cols = pl.ds(pl.multiple_of(step * block, block), block)
        rows = jnp.concatenate([ref[:, cols] for ref in row_refs], axis=0)
        part = dot(rows, up_ref[...])

        @pl.when(step == 0)
        def _():
            acc_ref[...] = part

        @pl.when(step > 0)
        def _():
            acc_ref[...] += part

    @pl.when(step == steps - 1)
    def _():
        hidden_ref[...] = jax.nn.gelu(acc_ref[...], approximate=True).astype(BF16)

    @pl.when(step >= steps)
    def _():
        half = hidden_ref.shape[0] // 2
        part = dot(hidden_ref[...], down_ref[...]).astype(BF16)
        mine_ref[...] = part[:half]
        other_ref[...] = part[half:]


def expert_rows(rows, up, down):
    width, units = up.shape
    steps = 4
    block = width // steps
    total = sum(r.shape[0] for r in rows)

    def part(i):
        return jnp.maximum(i - steps, 0)

    out = pl.BlockSpec((total // 2, block), lambda i: (0, part(i)))
    return pl.pallas_call(
        lambda *refs: expert_kernel(len(rows), *refs),
        grid=(2 * steps,),
        in_specs=[pl.BlockSpec(r.shape, lambda i: (0, 0)) for r in rows]
        + [
            pl.BlockSpec((block, units), lambda i: (jnp.minimum(i, steps - 1), 0)),
            pl.BlockSpec((units, block), lambda i: (0, part(i))),
        ],
        out_specs=[out, out],
        out_shape=[jax.ShapeDtypeStruct((total // 2, width), BF16)] * 2,
        scratch_shapes=[pltpu.VMEM((total, units), F32), pltpu.VMEM((total, units), BF16)],
        name="expert_rows",
    )(*rows, up, down)


def passed_along(value, axis, steps):
    count = lax.axis_size(axis)
    pairs = [(source, (source + steps) % count) for source in range(count)]
    return lax.ppermute(value, axis, pairs)


def swapped(value):
    count = lax.axis_size("ctx")
    return lax.ppermute(value, "ctx", [(i, i ^ 1) for i in range(count)])


def chain_prefix(total, decay, chip, chips, scale):
    heads = total.shape[0]
    per = heads // CHUNKS
    received = []
    for step in range(CHUNKS + chips - 2):
        place = jnp.clip(step - chip, 0, CHUNKS - 1) * per
        gone = lax.dynamic_slice_in_dim(total, place, per, 0) * scale
        if step >= 1:
            before = received[step - 1].astype(F32)
            gone = lax.dynamic_slice_in_dim(decay, place, per, 0)[:, None, :] * before + gone
        pairs = [
            (2 * z + core, 2 * z + 2 + core)
            for z in range(chips - 1)
            if 0 <= step - z < CHUNKS
            for core in range(2)
        ]
        received.append(lax.ppermute(gone.astype(jnp.float16), "ctx", pairs))
    row = jnp.concatenate(received, axis=0)
    first = jnp.maximum(chip - 1, 0) * per
    mine = lax.dynamic_slice_in_dim(row, first, heads, 0).astype(F32) * (1.0 / scale)
    return jnp.where(chip > 0, mine, 0.0)


def local(
    resid,
    queries,
    keys,
    values,
    log_decay,
    attn_gain,
    moe_gain,
    experts,
    combine_weight,
    w_up,
    w_down,
):
    return layer(
        resid[0], queries[0], keys[0], values[0], log_decay[0], attn_gain, moe_gain,
        experts[0], combine_weight[0], w_up[0], w_down[0],
    )


def layer(resid, queries, keys, values, rate, attn_gain, moe_gain, experts, weight, up, down):
    length, width = queries.shape
    count = lax.axis_size("ctx")
    me = lax.axis_index("ctx")
    chips, chip, core = count // 2, me // 2, me % 2
    half = width // HEAD // 2
    first = core == 0
    core1 = core.astype(jnp.int32)[None]

    other, decay = half_state(1 - core1, rate, keys, values)
    partner = swapped(other)
    decay_partner = swapped(decay)
    mine, _ = half_state(core1, rate, keys, values)
    decay = lax.dynamic_slice_in_dim(decay, core * half, half, 0)
    decay_partner = lax.dynamic_slice_in_dim(decay_partner, core * half, half, 0)
    state0, state1 = jnp.where(first, mine, partner), jnp.where(first, partner, mine)
    decay0, decay1 = (
        jnp.where(first, decay, decay_partner),
        jnp.where(first, decay_partner, decay),
    )
    scale = 1.0
    while 36.0 * count * length * scale > 65000.0:
        scale = scale / 2
    total = decay1[:, None, :] * state0 + state1
    prefix = chain_prefix(total, decay0 * decay1, chip, chips, scale)
    after0 = decay0[:, None, :] * prefix + state0
    keep = jnp.where(first, prefix, after0)
    got = swapped(jnp.where(first, after0, prefix))
    intra = intra_attention(rate, queries, keys, values)
    flying = count // SHARDS
    if flying > 1:
        prefix = jnp.where(first, jnp.concatenate([keep, got]), jnp.concatenate([got, keep]))
        return many_experts(
            flying, rate, queries, intra, prefix, resid, attn_gain, moe_gain, experts, weight, up, down
        )
    early, outbox, picked, wcol, place = finish(
        core1, rate, queries, intra, keep, got, resid, attn_gain, moe_gain, experts.T, weight.T
    )
    early = passed_along(early, "section", 1)
    place = passed_along(place, "section", 1)
    own = [outbox] + [
        lax.ppermute(outbox, "ctx", [(i, (i + 2 * d) % count) for i in range(count)])
        for d in range(1, chips)
    ]
    others = [swapped(r) for r in own]
    mine, other = expert_rows(own + others, up, down)
    pair = (mine.astype(F32) + swapped(other).astype(F32)).astype(BF16)
    pair = pair.reshape(chips, CAP_SRC, width)
    summed = pair[0].astype(F32)
    for d in range(1, chips):
        back = lax.ppermute(pair[d], "ctx", [(i, (i - 2 * d) % count) for i in range(count)])
        summed = summed + back.astype(F32)
    late = (picked + wcol[:, :1] * summed).astype(BF16)
    late = passed_along(late, "section", 1)
    found = (place[:1] == jnp.arange(CAP_SRC, dtype=F32)[:, None]).astype(BF16)
    rows = lax.dot_general(
        found, late, (((0,), (0,)), ((), ())), preferred_element_type=F32
    ).astype(BF16)
    return jnp.where(place[0][:, None] >= 0, rows, early)[None]


def rms_scale(values_in, gain):
    return (
        values_in
        * lax.rsqrt(jnp.mean(values_in * values_in, axis=-1, keepdims=True) + 1e-06)
        * gain
    )


def many_experts(
    flying, rate, queries, intra, prefix, resid, attn_gain, moe_gain, experts, weight, up, down
):
    length, width = queries.shape
    heads = width // HEAD
    count = lax.axis_size("ctx")
    inter = jnp.exp(jnp.cumsum(rate, axis=0))[:, :, None] * jnp.einsum(
        "thd,hde->the",
        queries.astype(F32).reshape(length, heads, HEAD),
        prefix,
        precision=lax.Precision.HIGHEST,
    )
    hres = resid.astype(F32) + rms_scale(intra + inter.reshape(length, width), attn_gain)
    normed = rms_scale(hres, moe_gain).astype(BF16)
    slots = flying * CAP_SRC
    chosen = experts.reshape(-1)
    onehot = (chosen[:, None] == jnp.arange(flying)[None, :]).astype(jnp.int32)
    slot = jnp.sum((jnp.cumsum(onehot, axis=0) - onehot) * onehot, axis=1)
    target = jnp.where(chosen < flying, chosen * CAP_SRC + slot, -1)
    hot = (target[None, :] == jnp.arange(slots)[:, None]).reshape(slots, length, 2)
    outbox = dot(hot.any(axis=2).astype(BF16), normed).astype(BF16)
    outbox = outbox.reshape(1, flying, CAP_SRC, width)
    mine = lax.dynamic_index_in_dim(
        lax.all_gather(outbox, "ctx", axis=0, tiled=True), lax.axis_index("ctx") // SHARDS, 1, False
    )
    hidden = jax.nn.gelu(dot(mine.reshape(count * CAP_SRC, width), up), approximate=True)
    part = dot(hidden.astype(BF16), down).astype(BF16).reshape(count, CAP_SRC, width)
    returned = lax.all_to_all(part, "ctx", split_axis=0, concat_axis=0, tiled=True)
    summed = returned.reshape(flying, SHARDS, CAP_SRC, width).astype(F32).sum(axis=1)
    mixed = lax.dot_general(
        jnp.where(hot, weight[None], 0.0).sum(axis=2),
        summed.reshape(slots, width),
        (((0,), (0,)), ((), ())),
        precision=lax.Precision.HIGHEST,
    )
    return passed_along((hres + mixed).astype(BF16)[None], "section", 1)


def solution(mesh):
    return jax.shard_map(
        local,
        mesh=mesh,
        in_specs=(
            P("section", "ctx", None),
            P("section", "ctx", None),
            P("section", "ctx", None),
            P("section", "ctx", None),
            P("section", "ctx", None),
            P("section", None),
            P("section", None),
            P("section", "ctx", None),
            P("section", "ctx", None),
            P("section", None, "ctx"),
            P("section", "ctx", None),
        ),
        out_specs=P("section", "ctx", None),
        check_vma=False,
    )
```

```python
import jax
import jax.numpy as jnp
from jax import lax
from jax.experimental import pallas as pl
from jax.experimental.pallas import tpu as pltpu
from jax.sharding import PartitionSpec as P

HEAD = 128
SHARDS = 8
CAP_SRC = 16
GROUP = 8
CHUNKS = 4
PARTS = 3

F32, BF16 = jnp.float32, jnp.bfloat16


def dot(a, b, dims=((1,), (0,))):
    return lax.dot_general(a, b, (dims, ((), ())), preferred_element_type=F32)


def split(a):
    hi = a.astype(BF16)
    return hi, (a - hi.astype(F32)).astype(BF16)


def cumul_rows(rate_ref):
    length = rate_ref.shape[1]
    upper = (
        lax.broadcasted_iota(jnp.int32, (length, length), 0)
        <= lax.broadcasted_iota(jnp.int32, (length, length), 1)
    ).astype(F32)
    return lax.dot_general(
        rate_ref[...], upper, (((1,), (0,)), ((), ())), precision=lax.Precision.HIGHEST,
        preferred_element_type=F32,
    )


def in_vmem(x):
    return pltpu.with_memory_space_constraint(x, pltpu.VMEM)


VMEM_SPEC = pl.BlockSpec(memory_space=pltpu.VMEM)
HBM_SPEC = pl.BlockSpec(memory_space=pltpu.HBM)
ANY_SPEC = pl.BlockSpec(memory_space=pl.ANY)
SMEM_SPEC = pl.BlockSpec(memory_space=pltpu.SMEM)


def state_kernel(
    half_ref, rate_ref, k_hbm, v_hbm, state_hbm, decay_ref, k_ref, v_ref, state_ref, cum_ref, sems
):
    groups = sems.shape[1]
    length = rate_ref.shape[1]
    span = GROUP * HEAD

    def fetch(kind, g):
        source, target = ((k_hbm, k_ref), (v_hbm, v_ref))[kind]
        column = pl.multiple_of((half_ref[0] * groups + g) * span, span)
        return pltpu.make_async_copy(
            source.at[:, pl.ds(column, span)], target.at[g], sems.at[kind, g]
        )

    def store(g):
        at = pl.ds(g * GROUP, GROUP)
        return pltpu.make_async_copy(state_ref.at[at], state_hbm.at[at], sems.at[2, g])

    for g in range(groups):
        for kind in range(2):
            fetch(kind, g).start()
    cum_ref[...] = cumul_rows(rate_ref)
    decay_ref[...] = jnp.broadcast_to(jnp.exp(cum_ref[:, length - 1 :]), decay_ref.shape)
    for g in range(groups):
        row = pl.multiple_of((half_ref[0] * groups + g) * GROUP, GROUP)
        cum = cum_ref[pl.ds(row, GROUP), :]
        tail = jnp.exp(cum[:, length - 1 :] - cum)
        for kind in range(2):
            fetch(kind, g).wait()
        for j in range(GROUP):
            cols = slice(j * HEAD, (j + 1) * HEAD)
            turned = k_ref[g, :, cols].astype(F32).T * tail[j : j + 1, :]
            hi, lo = split(turned)
            v = v_ref[g, :, cols]
            state_ref[g * GROUP + j] = dot(hi, v) + dot(lo, v)
        store(g).start()
    for g in range(groups):
        store(g).wait()


def half_state(half, rate, keys, values):
    length, width = keys.shape
    heads = width // HEAD
    groups = heads // 2 // GROUP
    return pl.pallas_call(
        state_kernel,
        in_specs=[SMEM_SPEC, VMEM_SPEC, HBM_SPEC, HBM_SPEC],
        out_specs=[HBM_SPEC, VMEM_SPEC],
        out_shape=[
            jax.ShapeDtypeStruct((heads // 2, HEAD, HEAD), F32),
            jax.ShapeDtypeStruct((heads, HEAD), F32),
        ],
        scratch_shapes=[
            pltpu.VMEM((groups, length, GROUP * HEAD), BF16),
            pltpu.VMEM((groups, length, GROUP * HEAD), BF16),
            pltpu.VMEM((heads // 2, HEAD, HEAD), F32),
            pltpu.VMEM((heads, length), F32),
            pltpu.SemaphoreType.DMA((3, groups)),
        ],
        name="half_state",
    )(half, rate, keys, values)


def intra_kernel(first, rate_ref, q_hbm, k_hbm, v_hbm, out_hbm, q_ref, k_ref, v_ref, out_ref, sems):
    groups = sems.shape[1]
    length = rate_ref.shape[1]
    span = GROUP * HEAD

    def fetch(kind, g):
        source, target = ((q_hbm, q_ref), (k_hbm, k_ref), (v_hbm, v_ref))[kind]
        return pltpu.make_async_copy(
            source.at[:, pl.ds((first + g) * span, span)], target.at[g], sems.at[kind, g]
        )

    def store(g):
        at = pl.ds(g * span, span)
        return pltpu.make_async_copy(out_ref.at[g], out_hbm.at[:, at], sems.at[3, g])

    for g in range(groups):
        for kind in range(3):
            fetch(kind, g).start()
    cumul = cumul_rows(rate_ref)
    lower = lax.broadcasted_iota(jnp.int32, (length, length), 0) >= lax.broadcasted_iota(
        jnp.int32, (length, length), 1
    )
    for g in range(groups):
        for kind in range(3):
            fetch(kind, g).wait()
        for j in range(GROUP):
            head = (first + g) * GROUP + j
            cols = slice(j * HEAD, (j + 1) * HEAD)
            across = jnp.broadcast_to(cumul[head : head + 1, :], (length, length))
            weights = jnp.exp(jnp.where(lower, across.T - across, -1e30))
            scores = dot(q_ref[g, :, cols], k_ref[g, :, cols], ((1,), (1,)))
            hi, lo = split(scores * weights)
            v = v_ref[g, :, cols]
            out_ref[g, :, cols] = dot(hi, v) + dot(lo, v)
        store(g).start()
    for g in range(groups):
        store(g).wait()


def intra_attention(part, parts, rate, queries, keys, values):
    length, width = keys.shape
    groups = width // HEAD // GROUP // parts
    piece = (groups, length, GROUP * HEAD)
    return pl.pallas_call(
        lambda *refs: intra_kernel(part * groups, *refs),
        in_specs=[VMEM_SPEC] + [HBM_SPEC] * 3,
        out_specs=HBM_SPEC,
        out_shape=jax.ShapeDtypeStruct((length, width // parts), F32),
        scratch_shapes=[pltpu.VMEM(piece, BF16)] * 3
        + [pltpu.VMEM(piece, F32), pltpu.SemaphoreType.DMA((4, groups))],
        name="intra_attention",
    )(rate, queries, keys, values)


def finish_kernel(parts, core_ref, rate_ref, q_hbm, *refs):
    intra_hbm = refs[:parts]
    (
        keep_hbm, got_hbm, resid_hbm, again_ref, mgain_ref, experts_ref, weight_ref,
        early_ref, outbox_ref, picked_ref, wcol_ref, place_ref,
        attn_ref, normed_ref, q_ref, intra_ref, state_ref, resid_ref, scale_ref, sems,
    ) = refs[parts:]
    length, width = resid_ref.shape
    heads = width // HEAD
    groups = heads // GROUP
    span = GROUP * HEAD

    def copies(g):
        at = pl.ds(g * span, span)
        part, place = divmod(g * parts, groups)
        place = place // parts
        return [
            pltpu.make_async_copy(q_hbm.at[:, at], q_ref.at[g], sems.at[0, g]),
            pltpu.make_async_copy(
                intra_hbm[part].at[:, pl.ds(place * span, span)], intra_ref.at[g], sems.at[1, g]
            ),
        ]

    half = heads // 2
    for g in range(groups):
        for copy in copies(g):
            copy.start()

    def states(n):
        place = pl.multiple_of(lax.rem(core_ref[0] + n, 2) * half, half)
        return pltpu.make_async_copy(
            (keep_hbm, got_hbm)[n], state_ref.at[pl.ds(place, half)], sems.at[2, n]
        )

    states(0).start()
    states(1).start()
    rest = pltpu.make_async_copy(resid_hbm, resid_ref, sems.at[2, 2])
    rest.start()
    growth = jnp.exp(cumul_rows(rate_ref))
    for head in range(heads):
        across = jnp.broadcast_to(growth[head : head + 1, :], (length, length))
        scale_ref[:, head * HEAD : (head + 1) * HEAD] = across.T
    states(0).wait()
    states(1).wait()
    for g in range(groups):
        for copy in copies(g):
            copy.wait()
        for j in range(GROUP):
            head = g * GROUP + j
            mine = slice(j * HEAD, (j + 1) * HEAD)
            cols = slice(head * HEAD, (head + 1) * HEAD)
            hi, lo = split(state_ref[head])
            q = q_ref[g, :, mine]
            value = dot(q, hi) + dot(q, lo)
            attn_ref[:, cols] = intra_ref[g, :, mine] + scale_ref[:, cols] * value
    rest.wait()

    rows = 16

    def norm(r, carry):
        at = pl.ds(pl.multiple_of(r * rows, rows), rows)
        x = attn_ref[at, :]
        scale = lax.rsqrt(jnp.mean(x * x, axis=-1, keepdims=True) + 1e-06)
        hres = resid_ref[at, :].astype(F32) + x * scale * again_ref[...]
        attn_ref[at, :] = hres
        early_ref[at, :] = hres.astype(BF16)
        scale = lax.rsqrt(jnp.mean(hres * hres, axis=-1, keepdims=True) + 1e-06)
        normed_ref[at, :] = (hres * scale * mgain_ref[...]).astype(BF16)
        return carry

    lax.fori_loop(0, length // rows, norm, 0)
    slots = outbox_ref.shape[0]
    before = (
        lax.broadcasted_iota(jnp.int32, (length, length), 0)
        < lax.broadcasted_iota(jnp.int32, (length, length), 1)
    ).astype(BF16)
    named = experts_ref[...] == 0
    taken = jnp.max(named.astype(F32), axis=0, keepdims=True)
    slot = dot(jnp.broadcast_to(taken, (8, length)).astype(BF16), before)[0:1, :]
    slot = jnp.where(taken > 0, slot, -1.0)
    place_ref[...] = jnp.broadcast_to(slot, place_ref.shape)
    hot = lax.broadcasted_iota(jnp.int32, (slots, length), 0).astype(F32) == slot
    weight = jnp.sum(jnp.where(named, weight_ref[...], 0.0), axis=0, keepdims=True)
    weight = jnp.sum(jnp.where(hot, weight, 0.0), axis=1, keepdims=True)
    wcol_ref[...] = jnp.broadcast_to(weight, wcol_ref.shape)
    hot = hot.astype(BF16)
    outbox_ref[...] = dot(hot, normed_ref[...]).astype(BF16)
    for c in range(width // 512):
        cols = slice(c * 512, (c + 1) * 512)
        x = attn_ref[:, cols]
        hi = x.astype(BF16)
        mid, low = split(x - hi.astype(F32))
        picked_ref[:, cols] = dot(hot, hi) + dot(hot, mid) + dot(hot, low)


def finish(core, rate, queries, intra, keep, got, resid, attn_gain, moe_gain, experts, weight):
    length, width = queries.shape
    heads = width // HEAD
    groups = heads // GROUP
    parts = len(intra)
    args = [rate, queries, *intra, keep, got, resid, attn_gain, moe_gain, experts, weight]
    return pl.pallas_call(
        lambda *refs: finish_kernel(parts, *refs),
        in_specs=[SMEM_SPEC, VMEM_SPEC]
        + [HBM_SPEC] * (1 + parts)
        + [ANY_SPEC] * 2
        + [HBM_SPEC]
        + [VMEM_SPEC] * 4,
        out_specs=[VMEM_SPEC] * 5,
        out_shape=[
            pltpu.VMEM((length, width), BF16),
            pltpu.VMEM((CAP_SRC, width), BF16),
            pltpu.VMEM((CAP_SRC, width), F32),
            pltpu.VMEM((CAP_SRC, 128), F32),
            pltpu.VMEM((8, length), F32),
        ],
        scratch_shapes=[
            pltpu.VMEM((length, width), F32),
            pltpu.VMEM((length, width), BF16),
            pltpu.VMEM((groups, length, GROUP * HEAD), BF16),
            pltpu.VMEM((groups, length, GROUP * HEAD), F32),
            pltpu.VMEM((heads, HEAD, HEAD), F32),
            pltpu.VMEM((length, width), BF16),
            pltpu.VMEM((length, width), F32),
            pltpu.SemaphoreType.DMA((3, groups)),
        ],
        compiler_params=pltpu.CompilerParams(vmem_limit_bytes=32 << 20),
        name="finish",
    )(core, *args)


def expert_kernel(count, *refs):
    row_refs = refs[:count]
    (
        up_hbm, down_hbm, mine_ref, other_ref,
        up_ref, down_ref, rows_ref, hidden_ref, sems,
    ) = refs[count:]
    parts = sems.shape[1]
    depth, length = up_ref.shape[0] // parts, down_ref.shape[1] // parts
    half = mine_ref.shape[0]

    def fetch(kind, i):
        if kind == 0:
            at = pl.ds(i * depth, depth)
            return pltpu.make_async_copy(up_hbm.at[at], up_ref.at[at], sems.at[0, i])
        at = pl.ds(i * length, length)
        return pltpu.make_async_copy(down_hbm.at[:, at], down_ref.at[:, at], sems.at[1, i])

    for kind in range(2):
        for i in range(parts):
            fetch(kind, i).start()
    each = row_refs[0].shape[0]
    for n, ref in enumerate(row_refs):
        rows_ref[n * each : (n + 1) * each, :] = ref[...]
    acc = None
    for i in range(parts):
        fetch(0, i).wait()
        at = slice(i * depth, (i + 1) * depth)
        part = dot(rows_ref[:, at], up_ref[at, :])
        acc = part if acc is None else acc + part
    hidden_ref[...] = jax.nn.gelu(acc, approximate=True).astype(BF16)
    for i in range(parts):
        fetch(1, i).wait()
        at = slice(i * length, (i + 1) * length)
        part = dot(hidden_ref[...], down_ref[:, at]).astype(BF16)
        mine_ref[:, at] = part[:half]
        other_ref[:, at] = part[half:]


def expert_rows(rows, up, down):
    width, units = up.shape
    parts = 6
    total = sum(r.shape[0] for r in rows)
    return pl.pallas_call(
        lambda *refs: expert_kernel(len(rows), *refs),
        in_specs=[VMEM_SPEC] * len(rows) + [HBM_SPEC] * 2,
        out_specs=[VMEM_SPEC] * 2,
        out_shape=[pltpu.VMEM((total // 2, width), BF16)] * 2,
        scratch_shapes=[
            pltpu.VMEM((width, units), BF16),
            pltpu.VMEM((units, width), BF16),
            pltpu.VMEM((total, width), BF16),
            pltpu.VMEM((total, units), BF16),
            pltpu.SemaphoreType.DMA((2, parts)),
        ],
        compiler_params=pltpu.CompilerParams(vmem_limit_bytes=32 << 20),
        name="expert_rows",
    )(*[in_vmem(r) for r in rows], up, down)


def expert_kernel(count, *refs):
    row_refs = refs[:count]
    up_ref, down_ref, mine_ref, other_ref, rows_ref, hidden_ref = refs[count:]
    half = mine_ref.shape[0]
    each = row_refs[0].shape[0]
    for n, ref in enumerate(row_refs):
        rows_ref[n * each : (n + 1) * each, :] = ref[...]
    hidden = dot(rows_ref[...], up_ref[...])
    hidden_ref[...] = jax.nn.gelu(hidden, approximate=True).astype(BF16)
    parts = 4
    length = down_ref.shape[1] // parts
    for i in range(parts):
        at = slice(i * length, (i + 1) * length)
        part = dot(hidden_ref[...], down_ref[:, at]).astype(BF16)
        mine_ref[:, at] = part[:half]
        other_ref[:, at] = part[half:]


def expert_rows(rows, up, down):
    width, units = up.shape
    total = sum(r.shape[0] for r in rows)
    return pl.pallas_call(
        lambda *refs: expert_kernel(len(rows), *refs),
        in_specs=[VMEM_SPEC] * (len(rows) + 2),
        out_specs=[VMEM_SPEC] * 2,
        out_shape=[pltpu.VMEM((total // 2, width), BF16)] * 2,
        scratch_shapes=[pltpu.VMEM((total, width), BF16), pltpu.VMEM((total, units), BF16)],
        compiler_params=pltpu.CompilerParams(vmem_limit_bytes=12 << 20),
        name="expert_rows",
    )(*[in_vmem(r) for r in rows], in_vmem(up), in_vmem(down))


def passed_along(value, axis, steps):
    count = lax.axis_size(axis)
    pairs = [(source, (source + steps) % count) for source in range(count)]
    return lax.ppermute(value, axis, pairs)


def swapped(value):
    count = lax.axis_size("ctx")
    return lax.ppermute(value, "ctx", [(i, i ^ 1) for i in range(count)])


def chain_prefix(total, decay, chip, chips, scale):
    heads = total.shape[0]
    per = heads // CHUNKS
    received = []
    for step in range(CHUNKS + chips - 2):
        place = jnp.clip(step - chip, 0, CHUNKS - 1) * per
        gone = lax.dynamic_slice_in_dim(total, place, per, 0) * scale
        if step >= 1:
            before = received[step - 1].astype(F32)
            gone = lax.dynamic_slice_in_dim(decay, place, per, 0)[:, None, :] * before + gone
        pairs = [
            (2 * z + core, 2 * z + 2 + core)
            for z in range(chips - 1)
            if 0 <= step - z < CHUNKS
            for core in range(2)
        ]
        received.append(lax.ppermute(gone.astype(jnp.float16), "ctx", pairs))
    row = jnp.concatenate(received, axis=0)
    first = jnp.maximum(chip - 1, 0) * per
    mine = lax.dynamic_slice_in_dim(row, first, heads, 0).astype(F32) * (1.0 / scale)
    return jnp.where(chip > 0, mine, 0.0)


def local(
    resid,
    queries,
    keys,
    values,
    log_decay,
    attn_gain,
    moe_gain,
    experts,
    combine_weight,
    w_up,
    w_down,
):
    return layer(
        resid[0], queries[0], keys[0], values[0], log_decay[0], attn_gain, moe_gain,
        experts[0], combine_weight[0], w_up[0], w_down[0],
    )


def layer(resid, queries, keys, values, rate, attn_gain, moe_gain, experts, weight, up, down):
    length, width = queries.shape
    count = lax.axis_size("ctx")
    me = lax.axis_index("ctx")
    chips, chip, core = count // 2, me // 2, me % 2
    half = width // HEAD // 2
    first = core == 0
    core1 = core.astype(jnp.int32)[None]
    turned = rate.T

    other, decay = half_state(1 - core1, turned, keys, values)
    partner = swapped(other)
    decay_partner = swapped(decay)
    mine, _ = half_state(core1, turned, keys, values)
    decay = lax.dynamic_slice_in_dim(decay, core * half, half, 0)
    decay_partner = lax.dynamic_slice_in_dim(decay_partner, core * half, half, 0)
    state0, state1 = jnp.where(first, mine, partner), jnp.where(first, partner, mine)
    decay0, decay1 = (
        jnp.where(first, decay, decay_partner),
        jnp.where(first, decay_partner, decay),
    )
    scale = 1.0
    while 36.0 * count * length * scale > 65000.0:
        scale = scale / 2
    total = decay1[:, None, :] * state0 + state1
    prefix = chain_prefix(total, decay0 * decay1, chip, chips, scale)
    after0 = decay0[:, None, :] * prefix + state0
    keep = jnp.where(first, prefix, after0)
    got = swapped(jnp.where(first, after0, prefix))
    intra = []
    for part in range(PARTS):
        intra.append(intra_attention(part, PARTS, turned, queries, keys, values))
    flying = count // SHARDS
    if flying > 1:
        prefix = jnp.where(first, jnp.concatenate([keep, got]), jnp.concatenate([got, keep]))
        return many_experts(
            flying, rate, queries, jnp.concatenate(intra, axis=1), prefix, resid, attn_gain, moe_gain, experts, weight, up, down
        )
    early, outbox, picked, wcol, place = finish(
        core1, turned, queries, intra, keep, got, resid, attn_gain, moe_gain, experts.T, weight.T
    )
    early = passed_along(early, "section", 1)
    place = passed_along(place, "section", 1)
    own = [outbox] + [
        lax.ppermute(outbox, "ctx", [(i, (i + 2 * d) % count) for i in range(count)])
        for d in range(1, chips)
    ]
    others = [swapped(r) for r in own]
    mine, other = expert_rows(own + others, up, down)
    pair = (mine.astype(F32) + swapped(other).astype(F32)).astype(BF16)
    pair = pair.reshape(chips, CAP_SRC, width)
    summed = pair[0].astype(F32)
    for d in range(1, chips):
        back = lax.ppermute(pair[d], "ctx", [(i, (i - 2 * d) % count) for i in range(count)])
        summed = summed + back.astype(F32)
    late = (picked + wcol[:, :1] * summed).astype(BF16)
    late = passed_along(late, "section", 1)
    found = (place[:1] == jnp.arange(CAP_SRC, dtype=F32)[:, None]).astype(BF16)
    rows = lax.dot_general(
        found, late, (((0,), (0,)), ((), ())), preferred_element_type=F32
    ).astype(BF16)
    return jnp.where(place[0][:, None] >= 0, rows, early)[None]


def rms_scale(values_in, gain):
    return (
        values_in
        * lax.rsqrt(jnp.mean(values_in * values_in, axis=-1, keepdims=True) + 1e-06)
        * gain
    )


def many_experts(
    flying, rate, queries, intra, prefix, resid, attn_gain, moe_gain, experts, weight, up, down
):
    length, width = queries.shape
    heads = width // HEAD
    count = lax.axis_size("ctx")
    inter = jnp.exp(jnp.cumsum(rate, axis=0))[:, :, None] * jnp.einsum(
        "thd,hde->the",
        queries.astype(F32).reshape(length, heads, HEAD),
        prefix,
        precision=lax.Precision.HIGHEST,
    )
    hres = resid.astype(F32) + rms_scale(intra + inter.reshape(length, width), attn_gain)
    normed = rms_scale(hres, moe_gain).astype(BF16)
    slots = flying * CAP_SRC
    chosen = experts.reshape(-1)
    onehot = (chosen[:, None] == jnp.arange(flying)[None, :]).astype(jnp.int32)
    slot = jnp.sum((jnp.cumsum(onehot, axis=0) - onehot) * onehot, axis=1)
    target = jnp.where(chosen < flying, chosen * CAP_SRC + slot, -1)
    hot = (target[None, :] == jnp.arange(slots)[:, None]).reshape(slots, length, 2)
    outbox = dot(hot.any(axis=2).astype(BF16), normed).astype(BF16)
    outbox = outbox.reshape(1, flying, CAP_SRC, width)
    mine = lax.dynamic_index_in_dim(
        lax.all_gather(outbox, "ctx", axis=0, tiled=True), lax.axis_index("ctx") // SHARDS, 1, False
    )
    hidden = jax.nn.gelu(dot(mine.reshape(count * CAP_SRC, width), up), approximate=True)
    part = dot(hidden.astype(BF16), down).astype(BF16).reshape(count, CAP_SRC, width)
    returned = lax.all_to_all(part, "ctx", split_axis=0, concat_axis=0, tiled=True)
    summed = returned.reshape(flying, SHARDS, CAP_SRC, width).astype(F32).sum(axis=1)
    mixed = lax.dot_general(
        jnp.where(hot, weight[None], 0.0).sum(axis=2),
        summed.reshape(slots, width),
        (((0,), (0,)), ((), ())),
        precision=lax.Precision.HIGHEST,
    )
    return passed_along((hres + mixed).astype(BF16)[None], "section", 1)


def solution(mesh):
    return jax.shard_map(
        local,
        mesh=mesh,
        in_specs=(
            P("section", "ctx", None),
            P("section", "ctx", None),
            P("section", "ctx", None),
            P("section", "ctx", None),
            P("section", "ctx", None),
            P("section", None),
            P("section", None),
            P("section", "ctx", None),
            P("section", "ctx", None),
            P("section", None, "ctx"),
            P("section", "ctx", None),
        ),
        out_specs=P("section", "ctx", None),
        check_vma=False,
    )
```

```python
import jax
import jax.numpy as jnp
from jax import lax
from jax.experimental import pallas as pl
from jax.experimental.pallas import tpu as pltpu
from jax.sharding import PartitionSpec as P

HEAD = 128
SHARDS = 8
CAP_SRC = 16
GROUP = 8
CHUNKS = 4
PARTS = 3
FETCH_MIB = 42

F32, BF16 = jnp.float32, jnp.bfloat16


def dot(a, b, dims=((1,), (0,))):
    return lax.dot_general(a, b, (dims, ((), ())), preferred_element_type=F32)


def split(a):
    hi = a.astype(BF16)
    return hi, (a - hi.astype(F32)).astype(BF16)


def cumul_rows(rate_ref):
    length = rate_ref.shape[1]
    upper = (
        lax.broadcasted_iota(jnp.int32, (length, length), 0)
        <= lax.broadcasted_iota(jnp.int32, (length, length), 1)
    ).astype(F32)
    return lax.dot_general(
        rate_ref[...], upper, (((1,), (0,)), ((), ())), precision=lax.Precision.HIGHEST,
        preferred_element_type=F32,
    )


def in_vmem(x):
    return pltpu.with_memory_space_constraint(x, pltpu.VMEM)


VMEM_SPEC = pl.BlockSpec(memory_space=pltpu.VMEM)
HBM_SPEC = pl.BlockSpec(memory_space=pltpu.HBM)
ANY_SPEC = pl.BlockSpec(memory_space=pl.ANY)
SMEM_SPEC = pl.BlockSpec(memory_space=pltpu.SMEM)


def state_kernel(
    half_ref, rate_ref, k_hbm, v_hbm, state_hbm, decay_ref, k_ref, v_ref, state_ref, cum_ref, sems
):
    groups = sems.shape[1]
    length = rate_ref.shape[1]
    span = GROUP * HEAD

    def fetch(kind, g):
        source, target = ((k_hbm, k_ref), (v_hbm, v_ref))[kind]
        column = pl.multiple_of((half_ref[0] * groups + g) * span, span)
        return pltpu.make_async_copy(
            source.at[:, pl.ds(column, span)], target.at[g], sems.at[kind, g]
        )

    def store(g):
        at = pl.ds(g * GROUP, GROUP)
        return pltpu.make_async_copy(state_ref.at[at], state_hbm.at[at], sems.at[2, g])

    for g in range(groups):
        for kind in range(2):
            fetch(kind, g).start()
    eye = (
        lax.broadcasted_iota(jnp.int32, (HEAD, HEAD), 0)
        == lax.broadcasted_iota(jnp.int32, (HEAD, HEAD), 1)
    ).astype(BF16)
    cum_ref[...] = cumul_rows(rate_ref)
    decay_ref[...] = jnp.broadcast_to(jnp.exp(cum_ref[:, length - 1 :]), decay_ref.shape)
    for g in range(groups):
        row = pl.multiple_of((half_ref[0] * groups + g) * GROUP, GROUP)
        cum = cum_ref[pl.ds(row, GROUP), :]
        tail = jnp.exp(cum[:, length - 1 :] - cum)
        for kind in range(2):
            fetch(kind, g).wait()
        for j in range(GROUP):
            cols = slice(j * HEAD, (j + 1) * HEAD)
            turned = dot(eye, k_ref[g, :, cols], ((1,), (1,))) * tail[j : j + 1, :]
            hi, lo = split(turned)
            v = v_ref[g, :, cols]
            state_ref[g * GROUP + j] = dot(hi, v) + dot(lo, v)
        store(g).start()
    for g in range(groups):
        store(g).wait()


def half_state(half, rate, keys, values):
    length, width = keys.shape
    heads = width // HEAD
    groups = heads // 2 // GROUP
    return pl.pallas_call(
        state_kernel,
        in_specs=[SMEM_SPEC, VMEM_SPEC, HBM_SPEC, HBM_SPEC],
        out_specs=[HBM_SPEC, VMEM_SPEC],
        out_shape=[
            jax.ShapeDtypeStruct((heads // 2, HEAD, HEAD), F32),
            jax.ShapeDtypeStruct((heads, HEAD), F32),
        ],
        scratch_shapes=[
            pltpu.VMEM((groups, length, GROUP * HEAD), BF16),
            pltpu.VMEM((groups, length, GROUP * HEAD), BF16),
            pltpu.VMEM((heads // 2, HEAD, HEAD), F32),
            pltpu.VMEM((heads, length), F32),
            pltpu.SemaphoreType.DMA((3, groups)),
        ],
        name="half_state",
    )(half, rate, keys, values)


def intra_kernel(first, rate_ref, q_hbm, k_hbm, v_hbm, out_hbm, q_ref, k_ref, v_ref, out_ref, sems):
    groups = sems.shape[1]
    length = rate_ref.shape[1]
    span = GROUP * HEAD

    def fetch(kind, g):
        source, target = ((q_hbm, q_ref), (k_hbm, k_ref), (v_hbm, v_ref))[kind]
        return pltpu.make_async_copy(
            source.at[:, pl.ds((first + g) * span, span)], target.at[g], sems.at[kind, g]
        )

    def store(g):
        at = pl.ds(g * span, span)
        return pltpu.make_async_copy(out_ref.at[g], out_hbm.at[:, at], sems.at[3, g])

    for g in range(groups):
        for kind in range(3):
            fetch(kind, g).start()
    cumul = cumul_rows(rate_ref)
    lower = lax.broadcasted_iota(jnp.int32, (length, length), 0) >= lax.broadcasted_iota(
        jnp.int32, (length, length), 1
    )
    for g in range(groups):
        for kind in range(3):
            fetch(kind, g).wait()
        for j in range(GROUP):
            head = (first + g) * GROUP + j
            cols = slice(j * HEAD, (j + 1) * HEAD)
            across = jnp.broadcast_to(cumul[head : head + 1, :], (length, length))
            weights = jnp.exp(jnp.where(lower, across.T - across, -1e30))
            scores = dot(q_ref[g, :, cols], k_ref[g, :, cols], ((1,), (1,)))
            hi, lo = split(scores * weights)
            v = v_ref[g, :, cols]
            out_ref[g, :, cols] = dot(hi, v) + dot(lo, v)
        store(g).start()
    for g in range(groups):
        store(g).wait()


def intra_attention(part, parts, rate, queries, keys, values):
    length, width = keys.shape
    groups = width // HEAD // GROUP // parts
    piece = (groups, length, GROUP * HEAD)
    return pl.pallas_call(
        lambda *refs: intra_kernel(part * groups, *refs),
        in_specs=[VMEM_SPEC] + [HBM_SPEC] * 3,
        out_specs=HBM_SPEC,
        out_shape=jax.ShapeDtypeStruct((length, width // parts), F32),
        scratch_shapes=[pltpu.VMEM(piece, BF16)] * 3
        + [pltpu.VMEM(piece, F32), pltpu.SemaphoreType.DMA((4, groups))],
        name="intra_attention",
    )(rate, queries, keys, values)


def route_kernel(experts_ref, weight_ref, place_ref, wcol_ref, token_ref):
    slots = wcol_ref.shape[0]
    length = experts_ref.shape[1]
    before = (
        lax.broadcasted_iota(jnp.int32, (length, length), 0)
        < lax.broadcasted_iota(jnp.int32, (length, length), 1)
    ).astype(BF16)
    named = experts_ref[...] == 0
    taken = jnp.max(named.astype(F32), axis=0, keepdims=True)
    slot = dot(jnp.broadcast_to(taken, (8, length)).astype(BF16), before)[0:1, :]
    slot = jnp.where(taken > 0, slot, -1.0)
    place_ref[...] = jnp.broadcast_to(slot, place_ref.shape)
    hot = lax.broadcasted_iota(jnp.int32, (slots, length), 0).astype(F32) == slot
    weight = jnp.sum(jnp.where(named, weight_ref[...], 0.0), axis=0, keepdims=True)
    weight = jnp.sum(jnp.where(hot, weight, 0.0), axis=1, keepdims=True)
    wcol_ref[...] = jnp.broadcast_to(weight, wcol_ref.shape)
    at = lax.broadcasted_iota(jnp.int32, (slots, length), 1).astype(F32)
    token = jnp.sum(jnp.where(hot, at, 0.0), axis=1, keepdims=True)
    token_ref[...] = jnp.broadcast_to(token, token_ref.shape).astype(jnp.int32)


def route(experts, weight):
    length = experts.shape[1]
    return pl.pallas_call(
        route_kernel,
        in_specs=[VMEM_SPEC] * 2,
        out_specs=[VMEM_SPEC] * 3,
        out_shape=[
            jax.ShapeDtypeStruct((8, length), F32),
            jax.ShapeDtypeStruct((CAP_SRC, 128), F32),
            jax.ShapeDtypeStruct((CAP_SRC, 128), jnp.int32),
        ],
        name="route",
    )(experts, weight)


def finish_kernel(parts, chunks, steps, core_ref, token_ref, rate_ref, q_hbm, *refs):
    intra_hbm, refs = refs[:parts], refs[parts:]
    keeps, gots, refs = refs[:steps], refs[steps : 2 * steps], refs[2 * steps :]
    (
        resid_hbm, again_ref, mgain_ref, early_ref, outbox_ref, picked_ref,
        attn_ref, q_ref, intra_ref, state_ref, resid_ref, scale_ref, sems,
    ) = refs
    length, width = resid_ref.shape
    heads = width // HEAD
    groups = heads // GROUP
    span = GROUP * HEAD

    def copies(g):
        at = pl.ds(g * span, span)
        part, place = divmod(g * parts, groups)
        place = place // parts
        return [
            pltpu.make_async_copy(q_hbm.at[:, at], q_ref.at[g], sems.at[0, g]),
            pltpu.make_async_copy(
                intra_hbm[part].at[:, pl.ds(place * span, span)], intra_ref.at[g], sems.at[1, g]
            ),
        ]

    for g in range(groups):
        for copy in copies(g):
            copy.start()
    half = heads // 2
    per = half // chunks

    def states(n, c, late):
        place = pl.multiple_of(lax.rem(core_ref[0] + n, 2) * half + c * per, per)
        source = (keeps, gots)[n][c + late]
        return pltpu.make_async_copy(source, state_ref.at[pl.ds(place, per)], sems.at[2 + n, c])

    for late in range(steps - chunks + 1):

        @pl.when(core_ref[1] == late)
        def _():
            for c in range(chunks):
                for n in range(2):
                    states(n, c, late).start()

    rest = pltpu.make_async_copy(resid_hbm, resid_ref, sems.at[4, 0])
    rest.start()
    growth = jnp.exp(cumul_rows(rate_ref))
    for head in range(heads):
        across = jnp.broadcast_to(growth[head : head + 1, :], (length, length))
        scale_ref[:, head * HEAD : (head + 1) * HEAD] = across.T
    for c in range(chunks):
        for n in range(2):
            states(n, c, 0).wait()
    for g in range(groups):
        for copy in copies(g):
            copy.wait()
        for j in range(GROUP):
            head = g * GROUP + j
            mine = slice(j * HEAD, (j + 1) * HEAD)
            cols = slice(head * HEAD, (head + 1) * HEAD)
            hi, lo = split(state_ref[head])
            q = q_ref[g, :, mine]
            value = dot(q, hi) + dot(q, lo)
            attn_ref[:, cols] = intra_ref[g, :, mine] + scale_ref[:, cols] * value
    rest.wait()
    rows = 16

    def norm(r, carry):
        at = pl.ds(pl.multiple_of(r * rows, rows), rows)
        x = attn_ref[at, :]
        scale = lax.rsqrt(jnp.mean(x * x, axis=-1, keepdims=True) + 1e-06)
        hres = resid_ref[at, :].astype(F32) + x * scale * again_ref[...]
        attn_ref[at, :] = hres
        early_ref[at, :] = hres.astype(BF16)
        return carry

    lax.fori_loop(0, length // rows, norm, 0)
    for s in range(picked_ref.shape[0]):
        picked_ref[s : s + 1, :] = attn_ref[pl.ds(token_ref[s], 1), :]
    x = picked_ref[...]
    scale = lax.rsqrt(jnp.mean(x * x, axis=-1, keepdims=True) + 1e-06)
    outbox_ref[...] = (x * scale * mgain_ref[...]).astype(BF16)


def finish(core, token, rate, queries, intra, keeps, gots, resid, attn_gain, moe_gain):
    length, width = queries.shape
    heads = width // HEAD
    groups = heads // GROUP
    parts, steps = len(intra), len(keeps)
    args = [rate, queries, *intra, *keeps, *gots, resid, attn_gain, moe_gain]
    return pl.pallas_call(
        lambda *refs: finish_kernel(parts, CHUNKS, steps, *refs),
        in_specs=[SMEM_SPEC, SMEM_SPEC, VMEM_SPEC]
        + [HBM_SPEC] * (1 + parts)
        + [ANY_SPEC] * (2 * steps)
        + [HBM_SPEC]
        + [VMEM_SPEC] * 2,
        out_specs=[VMEM_SPEC] * 3,
        out_shape=[
            pltpu.VMEM((length, width), BF16),
            pltpu.VMEM((CAP_SRC, width), BF16),
            pltpu.VMEM((CAP_SRC, width), F32),
        ],
        scratch_shapes=[
            pltpu.VMEM((length, width), F32),
            pltpu.VMEM((groups, length, GROUP * HEAD), BF16),
            pltpu.VMEM((groups, length, GROUP * HEAD), F32),
            pltpu.VMEM((heads, HEAD, HEAD), F32),
            pltpu.VMEM((length, width), BF16),
            pltpu.VMEM((length, width), F32),
            pltpu.SemaphoreType.DMA((5, max(groups, CHUNKS))),
        ],
        compiler_params=pltpu.CompilerParams(vmem_limit_bytes=32 << 20),
        name="finish",
    )(core, token, *args)


def fetch_kernel(up_hbm, down_hbm, up_ref, down_ref, sems):
    copies = [
        pltpu.make_async_copy(up_hbm, up_ref, sems.at[0]),
        pltpu.make_async_copy(down_hbm, down_ref, sems.at[1]),
    ]
    for copy in copies:
        copy.start()
    for copy in copies:
        copy.wait()


def fetch(up, down):
    return pl.pallas_call(
        fetch_kernel,
        in_specs=[HBM_SPEC] * 2,
        out_specs=[VMEM_SPEC] * 2,
        out_shape=[pltpu.VMEM(up.shape, BF16), pltpu.VMEM(down.shape, BF16)],
        scratch_shapes=[pltpu.SemaphoreType.DMA((2,))],
        compiler_params=pltpu.CompilerParams(vmem_limit_bytes=FETCH_MIB << 20),
        name="fetch",
    )(up, down)


def expert_kernel(count, *refs):
    row_refs = refs[:count]
    up_ref, down_ref, mine_ref, other_ref, rows_ref, hidden_ref = refs[count:]
    half = mine_ref.shape[0]
    each = row_refs[0].shape[0]
    for n, ref in enumerate(row_refs):
        rows_ref[n * each : (n + 1) * each, :] = ref[...]
    hidden = dot(rows_ref[...], up_ref[...])
    hidden_ref[...] = jax.nn.gelu(hidden, approximate=True).astype(BF16)
    parts = 4
    length = down_ref.shape[1] // parts
    for i in range(parts):
        at = slice(i * length, (i + 1) * length)
        part = dot(hidden_ref[...], down_ref[:, at]).astype(BF16)
        mine_ref[:, at] = part[:half]
        other_ref[:, at] = part[half:]


def expert_rows(rows, up, down):
    width, units = up.shape
    total = sum(r.shape[0] for r in rows)
    return pl.pallas_call(
        lambda *refs: expert_kernel(len(rows), *refs),
        in_specs=[VMEM_SPEC] * (len(rows) + 2),
        out_specs=[VMEM_SPEC] * 2,
        out_shape=[pltpu.VMEM((total // 2, width), BF16)] * 2,
        scratch_shapes=[pltpu.VMEM((total, width), BF16), pltpu.VMEM((total, units), BF16)],
        compiler_params=pltpu.CompilerParams(vmem_limit_bytes=12 << 20),
        name="expert_rows",
    )(*[in_vmem(r) for r in rows], up, down)


def passed_along(value, axis, steps):
    count = lax.axis_size(axis)
    pairs = [(source, (source + steps) % count) for source in range(count)]
    return lax.ppermute(value, axis, pairs)


def swapped(value):
    count = lax.axis_size("ctx")
    return lax.ppermute(value, "ctx", [(i, i ^ 1) for i in range(count)])


def chain_prefix(mine, partner, decay, decay_partner, chip, chips, first, scale):
    heads = mine.shape[0]
    per = heads // CHUNKS
    keeps, gots, before = [], [], None

    def chunk(index):
        place = jnp.clip(index, 0, CHUNKS - 1) * per
        cut = [
            lax.dynamic_slice_in_dim(a, place, per, 0)
            for a in (mine, partner, decay, decay_partner)
        ]
        state0, state1 = jnp.where(first, cut[0], cut[1]), jnp.where(first, cut[1], cut[0])
        decay0, decay1 = jnp.where(first, cut[2], cut[3]), jnp.where(first, cut[3], cut[2])
        return state0, state1, decay0[:, None, :], decay1[:, None, :]

    for step in range(CHUNKS + chips - 2):
        state0, state1, decay0, decay1 = chunk(step - chip)
        gone = (decay1 * state0 + state1) * scale
        if before is not None:
            gone = (decay0 * decay1) * before.astype(F32) + gone
        pairs = [
            (2 * z + core, 2 * z + 2 + core)
            for z in range(chips - 1)
            if 0 <= step - z < CHUNKS
            for core in range(2)
        ]
        before = lax.ppermute(gone.astype(jnp.float16), "ctx", pairs)
        if step > 0:
            before, keep, give = lax.optimization_barrier((before, keep, give))
            keeps.append(keep)
            gots.append(swapped(give))
        state0, _, decay0, _ = chunk(step - jnp.maximum(chip - 1, 0))
        prefix = lax.optimization_barrier(before).astype(F32) * (1.0 / scale)
        after0 = decay0 * prefix + state0
        keep, give = jnp.where(first, prefix, after0), jnp.where(first, after0, prefix)
    keeps.append(keep)
    gots.append(swapped(give))
    return keeps, gots


def local(
    resid,
    queries,
    keys,
    values,
    log_decay,
    attn_gain,
    moe_gain,
    experts,
    combine_weight,
    w_up,
    w_down,
):
    return layer(
        resid[0], queries[0], keys[0], values[0], log_decay[0], attn_gain, moe_gain,
        experts[0], combine_weight[0], w_up[0], w_down[0],
    )


def layer(resid, queries, keys, values, rate, attn_gain, moe_gain, experts, weight, up, down):
    length, width = queries.shape
    count = lax.axis_size("ctx")
    me = lax.axis_index("ctx")
    chips, chip, core = count // 2, me // 2, me % 2
    half = width // HEAD // 2
    first = core == 0
    core1 = core.astype(jnp.int32)[None]
    turned = rate.T

    other, decay = half_state(1 - core1, turned, keys, values)
    partner = swapped(other)
    decay_partner = swapped(decay)
    mine, _ = half_state(core1, turned, keys, values)
    decay = lax.dynamic_slice_in_dim(decay, core * half, half, 0)
    decay_partner = lax.dynamic_slice_in_dim(decay_partner, core * half, half, 0)
    scale = 1.0
    while 36.0 * count * length * scale > 65000.0:
        scale = scale / 2
    keeps, gots = chain_prefix(
        mine, partner, decay, decay_partner, chip, chips, first, scale
    )
    late_by = jnp.maximum(chip - 1, 0)
    intra = []
    for part in range(PARTS):
        intra.append(intra_attention(part, PARTS, turned, queries, keys, values))
    flying = count // SHARDS
    if flying > 1:
        keep, got = (
            lax.dynamic_slice_in_dim(jnp.concatenate(a), late_by * (half // CHUNKS), half, 0)
            for a in (keeps, gots)
        )
        prefix = jnp.where(first, jnp.concatenate([keep, got]), jnp.concatenate([got, keep]))
        return many_experts(
            flying, rate, queries, jnp.concatenate(intra, axis=1), prefix, resid,
            attn_gain, moe_gain, experts, weight, up, down,
        )
    place, wcol, token = route(experts.T, weight.T)
    early, outbox, picked = finish(
        jnp.stack([core, late_by]).astype(jnp.int32), token[:, 0], turned, queries, intra,
        keeps, gots, resid, attn_gain, moe_gain,
    )
    early = passed_along(early, "section", 1)
    place = passed_along(place, "section", 1)
    own = [outbox] + [
        lax.ppermute(outbox, "ctx", [(i, (i + 2 * d) % count) for i in range(count)])
        for d in range(1, chips)
    ]
    others = [swapped(r) for r in own]
    up, down = fetch(up, down)
    mine, other = expert_rows(own + others, up, down)
    pair = (mine.astype(F32) + swapped(other).astype(F32)).astype(BF16)
    pair = pair.reshape(chips, CAP_SRC, width)
    summed = pair[0].astype(F32)
    for d in range(1, chips):
        back = lax.ppermute(pair[d], "ctx", [(i, (i - 2 * d) % count) for i in range(count)])
        summed = summed + back.astype(F32)
    late = (picked + wcol[:, :1] * summed).astype(BF16)
    late = passed_along(late, "section", 1)
    found = (place[:1] == jnp.arange(CAP_SRC, dtype=F32)[:, None]).astype(BF16)
    rows = lax.dot_general(
        found, late, (((0,), (0,)), ((), ())), preferred_element_type=F32
    ).astype(BF16)
    return jnp.where(place[0][:, None] >= 0, rows, early)[None]


def rms_scale(values_in, gain):
    return (
        values_in
        * lax.rsqrt(jnp.mean(values_in * values_in, axis=-1, keepdims=True) + 1e-06)
        * gain
    )


def many_experts(
    flying, rate, queries, intra, prefix, resid, attn_gain, moe_gain, experts, weight, up, down
):
    length, width = queries.shape
    heads = width // HEAD
    count = lax.axis_size("ctx")
    inter = jnp.exp(jnp.cumsum(rate, axis=0))[:, :, None] * jnp.einsum(
        "thd,hde->the",
        queries.astype(F32).reshape(length, heads, HEAD),
        prefix,
        precision=lax.Precision.HIGHEST,
    )
    hres = resid.astype(F32) + rms_scale(intra + inter.reshape(length, width), attn_gain)
    normed = rms_scale(hres, moe_gain).astype(BF16)
    slots = flying * CAP_SRC
    chosen = experts.reshape(-1)
    onehot = (chosen[:, None] == jnp.arange(flying)[None, :]).astype(jnp.int32)
    slot = jnp.sum((jnp.cumsum(onehot, axis=0) - onehot) * onehot, axis=1)
    target = jnp.where(chosen < flying, chosen * CAP_SRC + slot, -1)
    hot = (target[None, :] == jnp.arange(slots)[:, None]).reshape(slots, length, 2)
    outbox = dot(hot.any(axis=2).astype(BF16), normed).astype(BF16)
    outbox = outbox.reshape(1, flying, CAP_SRC, width)
    mine = lax.dynamic_index_in_dim(
        lax.all_gather(outbox, "ctx", axis=0, tiled=True), lax.axis_index("ctx") // SHARDS, 1, False
    )
    hidden = jax.nn.gelu(dot(mine.reshape(count * CAP_SRC, width), up), approximate=True)
    part = dot(hidden.astype(BF16), down).astype(BF16).reshape(count, CAP_SRC, width)
    returned = lax.all_to_all(part, "ctx", split_axis=0, concat_axis=0, tiled=True)
    summed = returned.reshape(flying, SHARDS, CAP_SRC, width).astype(F32).sum(axis=1)
    mixed = lax.dot_general(
        jnp.where(hot, weight[None], 0.0).sum(axis=2),
        summed.reshape(slots, width),
        (((0,), (0,)), ((), ())),
        precision=lax.Precision.HIGHEST,
    )
    return passed_along((hres + mixed).astype(BF16)[None], "section", 1)


def solution(mesh):
    return jax.shard_map(
        local,
        mesh=mesh,
        in_specs=(
            P("section", "ctx", None),
            P("section", "ctx", None),
            P("section", "ctx", None),
            P("section", "ctx", None),
            P("section", "ctx", None),
            P("section", None),
            P("section", None),
            P("section", "ctx", None),
            P("section", "ctx", None),
            P("section", None, "ctx"),
            P("section", "ctx", None),
        ),
        out_specs=P("section", "ctx", None),
        check_vma=False,
    )
```

```python
import jax
import jax.numpy as jnp
from jax import lax
from jax.experimental import pallas as pl
from jax.experimental.pallas import tpu as pltpu
from jax.sharding import PartitionSpec as P

HEAD = 128
SHARDS = 8
CAP_SRC = 16
GROUP = 8
CHUNKS = 4
PARTS = 3
FETCH_MIB = 42

F32, BF16 = jnp.float32, jnp.bfloat16


def dot(a, b, dims=((1,), (0,))):
    return lax.dot_general(a, b, (dims, ((), ())), preferred_element_type=F32)


def split(a):
    hi = a.astype(BF16)
    return hi, (a - hi.astype(F32)).astype(BF16)


def cumul_rows(rate_ref):
    length = rate_ref.shape[1]
    upper = (
        lax.broadcasted_iota(jnp.int32, (length, length), 0)
        <= lax.broadcasted_iota(jnp.int32, (length, length), 1)
    ).astype(F32)
    return lax.dot_general(
        rate_ref[...], upper, (((1,), (0,)), ((), ())), precision=lax.Precision.HIGHEST,
        preferred_element_type=F32,
    )


def in_vmem(x):
    return pltpu.with_memory_space_constraint(x, pltpu.VMEM)


VMEM_SPEC = pl.BlockSpec(memory_space=pltpu.VMEM)
HBM_SPEC = pl.BlockSpec(memory_space=pltpu.HBM)
ANY_SPEC = pl.BlockSpec(memory_space=pl.ANY)
SMEM_SPEC = pl.BlockSpec(memory_space=pltpu.SMEM)


def state_kernel(
    half_ref, rate_hbm, k_hbm, v_hbm, state_hbm, decay_hbm,
    rate_ref, k_ref, v_ref, state_ref, decay_ref, cum_ref, sems,
):
    groups = k_ref.shape[0]
    length = rate_ref.shape[1]
    span = GROUP * HEAD
    rates = pltpu.make_async_copy(rate_hbm, rate_ref, sems.at[3, 0])
    rates.start()

    def fetch(kind, g):
        source, target = ((k_hbm, k_ref), (v_hbm, v_ref))[kind]
        column = pl.multiple_of((half_ref[0] * groups + g) * span, span)
        return pltpu.make_async_copy(
            source.at[:, pl.ds(column, span)], target.at[g], sems.at[kind, g]
        )

    def store(g):
        at = pl.ds(g * GROUP, GROUP)
        return pltpu.make_async_copy(state_ref.at[at], state_hbm.at[at], sems.at[2, g])

    for g in range(groups):
        for kind in range(2):
            fetch(kind, g).start()
    rates.wait()
    cum_ref[...] = cumul_rows(rate_ref)
    decay_ref[...] = jnp.broadcast_to(jnp.exp(cum_ref[:, length - 1 :]), decay_ref.shape)
    decays = pltpu.make_async_copy(decay_ref, decay_hbm, sems.at[3, 1])
    decays.start()
    for g in range(groups):
        row = pl.multiple_of((half_ref[0] * groups + g) * GROUP, GROUP)
        cum = cum_ref[pl.ds(row, GROUP), :]
        tail = jnp.exp(cum[:, length - 1 :] - cum)
        for kind in range(2):
            fetch(kind, g).wait()
        for j in range(GROUP):
            cols = slice(j * HEAD, (j + 1) * HEAD)
            turned = k_ref[g, :, cols].T.astype(F32) * tail[j : j + 1, :]
            hi, lo = split(turned)
            v = v_ref[g, :, cols]
            state_ref[g * GROUP + j] = dot(hi, v) + dot(lo, v)
        store(g).start()
    for g in range(groups):
        store(g).wait()
    decays.wait()


def half_state(half, rate, keys, values):
    length, width = keys.shape
    heads = width // HEAD
    groups = heads // 2 // GROUP
    return pl.pallas_call(
        state_kernel,
        in_specs=[SMEM_SPEC, HBM_SPEC, HBM_SPEC, HBM_SPEC],
        out_specs=[HBM_SPEC, HBM_SPEC],
        out_shape=[
            jax.ShapeDtypeStruct((heads // 2, HEAD, HEAD), F32),
            jax.ShapeDtypeStruct((heads, HEAD), F32),
        ],
        scratch_shapes=[
            pltpu.VMEM((heads, length), F32),
            pltpu.VMEM((groups, length, GROUP * HEAD), BF16),
            pltpu.VMEM((groups, length, GROUP * HEAD), BF16),
            pltpu.VMEM((heads // 2, HEAD, HEAD), F32),
            pltpu.VMEM((heads, HEAD), F32),
            pltpu.VMEM((heads, length), F32),
            pltpu.SemaphoreType.DMA((4, max(groups, 2))),
        ],
        name="half_state",
    )(half, rate, keys, values)


def intra_kernel(first, rate_ref, q_hbm, k_hbm, v_hbm, out_hbm, q_ref, k_ref, v_ref, out_ref, sems):
    groups = sems.shape[1]
    length = rate_ref.shape[1]
    span = GROUP * HEAD

    def fetch(kind, g):
        source, target = ((q_hbm, q_ref), (k_hbm, k_ref), (v_hbm, v_ref))[kind]
        return pltpu.make_async_copy(
            source.at[:, pl.ds((first + g) * span, span)], target.at[g], sems.at[kind, g]
        )

    def store(g):
        at = pl.ds(g * span, span)
        return pltpu.make_async_copy(out_ref.at[g], out_hbm.at[:, at], sems.at[3, g])

    for g in range(groups):
        for kind in range(3):
            fetch(kind, g).start()
    cumul = cumul_rows(rate_ref)
    lower = lax.broadcasted_iota(jnp.int32, (length, length), 0) >= lax.broadcasted_iota(
        jnp.int32, (length, length), 1
    )
    for g in range(groups):
        for kind in range(3):
            fetch(kind, g).wait()
        for j in range(GROUP):
            head = (first + g) * GROUP + j
            cols = slice(j * HEAD, (j + 1) * HEAD)
            across = jnp.broadcast_to(cumul[head : head + 1, :], (length, length))
            weights = jnp.exp(jnp.where(lower, across.T - across, -1e30))
            scores = dot(q_ref[g, :, cols], k_ref[g, :, cols], ((1,), (1,)))
            hi, lo = split(scores * weights)
            v = v_ref[g, :, cols]
            out_ref[g, :, cols] = dot(hi, v) + dot(lo, v)
        store(g).start()
    for g in range(groups):
        store(g).wait()


def intra_attention(part, parts, rate, queries, keys, values):
    length, width = keys.shape
    groups = width // HEAD // GROUP // parts
    piece = (groups, length, GROUP * HEAD)
    return pl.pallas_call(
        lambda *refs: intra_kernel(part * groups, *refs),
        in_specs=[VMEM_SPEC] + [HBM_SPEC] * 3,
        out_specs=HBM_SPEC,
        out_shape=jax.ShapeDtypeStruct((length, width // parts), F32),
        scratch_shapes=[pltpu.VMEM(piece, BF16)] * 3
        + [pltpu.VMEM(piece, F32), pltpu.SemaphoreType.DMA((4, groups))],
        name="intra_attention",
    )(rate, queries, keys, values)


def select_kernel(
    parts, experts_ref, weight_ref, rate_ref, q_ref, resid_ref, *refs
):
    intra_refs = refs[:parts]
    wcol_ref, token_ref, growth_ref, q_out, resid_out, intra_out, at_ref, at_smem, sem = refs[parts:]
    slots = wcol_ref.shape[0]
    length = experts_ref.shape[1]
    before = (
        lax.broadcasted_iota(jnp.int32, (length, length), 0)
        < lax.broadcasted_iota(jnp.int32, (length, length), 1)
    ).astype(BF16)
    named = experts_ref[...] == 0
    taken = jnp.max(named.astype(F32), axis=0, keepdims=True)
    slot = dot(jnp.broadcast_to(taken, (8, length)).astype(BF16), before)[0:1, :]
    slot = jnp.where(taken > 0, slot, -1.0)
    hot = lax.broadcasted_iota(jnp.int32, (slots, length), 0).astype(F32) == slot
    weight = jnp.sum(jnp.where(named, weight_ref[...], 0.0), axis=0, keepdims=True)
    weight = jnp.sum(jnp.where(hot, weight, 0.0), axis=1, keepdims=True)
    wcol_ref[...] = jnp.broadcast_to(weight, wcol_ref.shape)
    at = lax.broadcasted_iota(jnp.int32, (slots, length), 1).astype(F32) + 1.0
    token = jnp.sum(jnp.where(hot, at, 0.0), axis=1, keepdims=True) - 1.0
    token_ref[...] = jnp.broadcast_to(token, token_ref.shape)
    at_ref[...] = jnp.broadcast_to(jnp.maximum(token, 0.0), at_ref.shape).astype(jnp.int32)
    known = pltpu.make_async_copy(at_ref, at_smem, sem)
    known.start()
    growth_ref[...] = lax.dot_general(
        hot.astype(F32), jnp.exp(cumul_rows(rate_ref)), (((1,), (1,)), ((), ())),
        precision=lax.Precision.HIGHEST, preferred_element_type=F32,
    )
    hot = hot.astype(BF16)
    q_out[...] = dot(hot, q_ref[...]).astype(BF16)
    resid_out[...] = dot(hot, resid_ref[...])
    known.wait()
    for s in range(slots):
        row = pl.ds(at_smem[s, 0], 1)
        for part, ref in enumerate(intra_refs):
            cols = slice(part * ref.shape[1], (part + 1) * ref.shape[1])
            intra_out[s : s + 1, cols] = ref[row, :]


def select(experts, weight, rate, queries, resid, intra):
    _, width = queries.shape
    heads = width // HEAD
    parts = len(intra)
    return pl.pallas_call(
        lambda *refs: select_kernel(parts, *refs),
        in_specs=[VMEM_SPEC] * (5 + parts),
        out_specs=[VMEM_SPEC] * 6,
        out_shape=[
            jax.ShapeDtypeStruct((CAP_SRC, 128), F32),
            jax.ShapeDtypeStruct((CAP_SRC, 128), F32),
            jax.ShapeDtypeStruct((CAP_SRC, heads), F32),
            jax.ShapeDtypeStruct((CAP_SRC, width), BF16),
            jax.ShapeDtypeStruct((CAP_SRC, width), F32),
            jax.ShapeDtypeStruct((CAP_SRC, width), F32),
        ],
        scratch_shapes=[
            pltpu.VMEM((CAP_SRC, 128), jnp.int32),
            pltpu.SMEM((CAP_SRC, 128), jnp.int32),
            pltpu.SemaphoreType.DMA,
        ],
        name="select",
    )(experts, weight, rate, queries, resid, *intra)


def prefix_copies(core_ref, keeps, gots, state_ref, sems, chunks):
    steps = len(keeps)
    half = state_ref.shape[0] // 2
    per = half // chunks

    def states(n, c, late):
        place = pl.multiple_of(lax.rem(core_ref[0] + n, 2) * half + c * per, per)
        source = (keeps, gots)[n][c + late]
        return pltpu.make_async_copy(source, state_ref.at[pl.ds(place, per)], sems.at[n, c])

    for late in range(steps - chunks + 1):

        @pl.when(core_ref[1] == late)
        def _():
            for c in range(chunks):
                for n in range(2):
                    states(n, c, late).start()

    def wait(c):
        for n in range(2):
            states(n, c, 0).wait()

    return wait


def rows_kernel(chunks, steps, core_ref, growth_ref, q_ref, resid_ref, intra_ref, *refs):
    keeps, gots, refs = refs[:steps], refs[steps : 2 * steps], refs[2 * steps :]
    again_ref, mgain_ref, outbox_ref, picked_ref, state_ref, sems = refs
    _, width = picked_ref.shape
    heads = width // HEAD
    half = heads // 2
    per = half // chunks
    wait = prefix_copies(core_ref, keeps, gots, state_ref, sems, chunks)
    for c in range(chunks):
        wait(c)
        for head in [n * half + c * per + j for n in range(2) for j in range(per)]:
            cols = slice(head * HEAD, (head + 1) * HEAD)
            hi, lo = split(state_ref[head])
            q = q_ref[:, cols]
            value = growth_ref[:, head : head + 1] * (dot(q, hi) + dot(q, lo))
            picked_ref[:, cols] = intra_ref[:, cols] + value
    x = picked_ref[...]
    scale = lax.rsqrt(jnp.mean(x * x, axis=-1, keepdims=True) + 1e-06)
    hres = resid_ref[...] + x * scale * again_ref[...]
    picked_ref[...] = hres
    scale = lax.rsqrt(jnp.mean(hres * hres, axis=-1, keepdims=True) + 1e-06)
    outbox_ref[...] = (hres * scale * mgain_ref[...]).astype(BF16)


def selected_rows(core, growth, queries, resid, intra, keeps, gots, attn_gain, moe_gain):
    slots, width = queries.shape
    heads = width // HEAD
    steps = len(keeps)
    return pl.pallas_call(
        lambda *refs: rows_kernel(CHUNKS, steps, *refs),
        in_specs=[SMEM_SPEC] + [VMEM_SPEC] * 4 + [ANY_SPEC] * (2 * steps) + [VMEM_SPEC] * 2,
        out_specs=[VMEM_SPEC] * 2,
        out_shape=[pltpu.VMEM((slots, width), BF16), pltpu.VMEM((slots, width), F32)],
        scratch_shapes=[
            pltpu.VMEM((heads, HEAD, HEAD), F32),
            pltpu.SemaphoreType.DMA((2, CHUNKS)),
        ],
        compiler_params=pltpu.CompilerParams(vmem_limit_bytes=16 << 20),
        name="selected_rows",
    )(core, growth, queries, resid, intra, *keeps, *gots, attn_gain, moe_gain)


def finish_kernel(parts, chunks, steps, core_ref, rate_ref, q_hbm, *refs):
    intra_hbm, refs = refs[:parts], refs[parts:]
    keeps, gots, refs = refs[:steps], refs[steps : 2 * steps], refs[2 * steps :]
    (
        resid_hbm, again_ref, early_ref,
        attn_ref, q_ref, intra_ref, state_ref, resid_ref, scale_ref, sems, state_sems,
    ) = refs
    length, width = resid_ref.shape
    heads = width // HEAD
    groups = heads // GROUP
    span = GROUP * HEAD

    def copies(g):
        at = pl.ds(g * span, span)
        part, place = divmod(g * parts, groups)
        place = place // parts
        return [
            pltpu.make_async_copy(q_hbm.at[:, at], q_ref.at[g], sems.at[0, g]),
            pltpu.make_async_copy(
                intra_hbm[part].at[:, pl.ds(place * span, span)], intra_ref.at[g], sems.at[1, g]
            ),
        ]

    for g in range(groups):
        for copy in copies(g):
            copy.start()
    wait = prefix_copies(core_ref, keeps, gots, state_ref, state_sems, chunks)
    rest = pltpu.make_async_copy(resid_hbm, resid_ref, sems.at[2, 0])
    rest.start()
    growth = jnp.exp(cumul_rows(rate_ref))
    for head in range(heads):
        across = jnp.broadcast_to(growth[head : head + 1, :], (length, length))
        scale_ref[:, head * HEAD : (head + 1) * HEAD] = across.T
    for c in range(chunks):
        wait(c)
    for g in range(groups):
        for copy in copies(g):
            copy.wait()
        for j in range(GROUP):
            head = g * GROUP + j
            mine = slice(j * HEAD, (j + 1) * HEAD)
            cols = slice(head * HEAD, (head + 1) * HEAD)
            hi, lo = split(state_ref[head])
            q = q_ref[g, :, mine]
            value = dot(q, hi) + dot(q, lo)
            attn_ref[:, cols] = intra_ref[g, :, mine] + scale_ref[:, cols] * value
    rest.wait()
    rows = 16

    def norm(r, carry):
        at = pl.ds(pl.multiple_of(r * rows, rows), rows)
        x = attn_ref[at, :]
        scale = lax.rsqrt(jnp.mean(x * x, axis=-1, keepdims=True) + 1e-06)
        hres = resid_ref[at, :].astype(F32) + x * scale * again_ref[...]
        early_ref[at, :] = hres.astype(BF16)
        return carry

    lax.fori_loop(0, length // rows, norm, 0)


def finish(core, rate, queries, intra, keeps, gots, resid, attn_gain):
    length, width = queries.shape
    heads = width // HEAD
    groups = heads // GROUP
    parts, steps = len(intra), len(keeps)
    args = [rate, queries, *intra, *keeps, *gots, resid, attn_gain]
    return pl.pallas_call(
        lambda *refs: finish_kernel(parts, CHUNKS, steps, *refs),
        in_specs=[SMEM_SPEC, VMEM_SPEC]
        + [HBM_SPEC] * (1 + parts)
        + [ANY_SPEC] * (2 * steps)
        + [HBM_SPEC, VMEM_SPEC],
        out_specs=VMEM_SPEC,
        out_shape=pltpu.VMEM((length, width), BF16),
        scratch_shapes=[
            pltpu.VMEM((length, width), F32),
            pltpu.VMEM((groups, length, GROUP * HEAD), BF16),
            pltpu.VMEM((groups, length, GROUP * HEAD), F32),
            pltpu.VMEM((heads, HEAD, HEAD), F32),
            pltpu.VMEM((length, width), BF16),
            pltpu.VMEM((length, width), F32),
            pltpu.SemaphoreType.DMA((3, groups)),
            pltpu.SemaphoreType.DMA((2, CHUNKS)),
        ],
        compiler_params=pltpu.CompilerParams(vmem_limit_bytes=32 << 20),
        name="finish",
    )(core, *args)


def late_kernel(count, picked_ref, wcol_ref, token_ref, *refs):
    parts, out_ref = refs[:count], refs[count]
    width = picked_ref.shape[1]
    total = parts[0][...].astype(F32)
    for part in parts[1:]:
        total = total + part[...].astype(F32)
    out_ref[:, :width] = (picked_ref[...] + wcol_ref[:, :1] * total).astype(BF16)
    out_ref[:, width:] = token_ref[...].astype(BF16)


def late_rows(picked, wcol, token, parts):
    slots, width = picked.shape
    return pl.pallas_call(
        lambda *refs: late_kernel(len(parts), *refs),
        in_specs=[VMEM_SPEC] * (3 + len(parts)),
        out_specs=VMEM_SPEC,
        out_shape=pltpu.VMEM((slots, width + 128), BF16),
        compiler_params=pltpu.CompilerParams(vmem_limit_bytes=8 << 20),
        name="late_rows",
    )(in_vmem(picked), wcol, token, *[in_vmem(p) for p in parts])


def merge_kernel(early_ref, late_ref, out_hbm, out_ref, sems):
    length, width = early_ref.shape
    slots = late_ref.shape[0]
    parts = sems.shape[0]
    span = width // parts
    token = late_ref[:, width:].astype(F32)
    found = token == lax.broadcasted_iota(jnp.int32, (slots, length), 1).astype(F32)
    found = found.astype(BF16)
    down = ((0,), (0,))
    hit = dot(found, jnp.ones((slots, 128), BF16), down)[:, :1] > 0.5

    def store(i):
        at = pl.ds(i * span, span)
        return pltpu.make_async_copy(out_ref.at[:, at], out_hbm.at[:, at], sems.at[i])

    for i in range(parts):
        at = slice(i * span, (i + 1) * span)
        rows = dot(found, late_ref[:, at], down)
        out_ref[:, at] = jnp.where(hit, rows, early_ref[:, at].astype(F32)).astype(BF16)
        store(i).start()
    for i in range(parts):
        store(i).wait()


def merged(early, late):
    return pl.pallas_call(
        merge_kernel,
        in_specs=[VMEM_SPEC] * 2,
        out_specs=HBM_SPEC,
        out_shape=jax.ShapeDtypeStruct(early.shape, BF16),
        scratch_shapes=[pltpu.VMEM(early.shape, BF16), pltpu.SemaphoreType.DMA((4,))],
        compiler_params=pltpu.CompilerParams(vmem_limit_bytes=8 << 20),
        name="merged",
    )(in_vmem(early), in_vmem(late))


def fetch_kernel(up_hbm, down_hbm, up_ref, down_ref, sems):
    copies = [
        pltpu.make_async_copy(up_hbm, up_ref, sems.at[0]),
        pltpu.make_async_copy(down_hbm, down_ref, sems.at[1]),
    ]
    for copy in copies:
        copy.start()
    for copy in copies:
        copy.wait()


def fetch(up, down):
    return pl.pallas_call(
        fetch_kernel,
        in_specs=[HBM_SPEC] * 2,
        out_specs=[VMEM_SPEC] * 2,
        out_shape=[pltpu.VMEM(up.shape, BF16), pltpu.VMEM(down.shape, BF16)],
        scratch_shapes=[pltpu.SemaphoreType.DMA((2,))],
        compiler_params=pltpu.CompilerParams(vmem_limit_bytes=FETCH_MIB << 20),
        name="fetch",
    )(up, down)


def expert_kernel(count, *refs):
    row_refs = refs[:count]
    up_ref, down_ref, mine_ref, other_ref, rows_ref, hidden_ref = refs[count:]
    half = mine_ref.shape[0]
    each = row_refs[0].shape[0]
    for n, ref in enumerate(row_refs):
        rows_ref[n * each : (n + 1) * each, :] = ref[...]
    hidden = dot(rows_ref[...], up_ref[...])
    hidden_ref[...] = jax.nn.gelu(hidden, approximate=True).astype(BF16)
    parts = 4
    length = down_ref.shape[1] // parts
    for i in range(parts):
        at = slice(i * length, (i + 1) * length)
        part = dot(hidden_ref[...], down_ref[:, at]).astype(BF16)
        mine_ref[:, at] = part[:half]
        other_ref[:, at] = part[half:]


def expert_rows(rows, up, down):
    width, units = up.shape
    total = sum(r.shape[0] for r in rows)
    return pl.pallas_call(
        lambda *refs: expert_kernel(len(rows), *refs),
        in_specs=[VMEM_SPEC] * (len(rows) + 2),
        out_specs=[VMEM_SPEC] * 2,
        out_shape=[pltpu.VMEM((total // 2, width), BF16)] * 2,
        scratch_shapes=[pltpu.VMEM((total, width), BF16), pltpu.VMEM((total, units), BF16)],
        compiler_params=pltpu.CompilerParams(vmem_limit_bytes=12 << 20),
        name="expert_rows",
    )(*[in_vmem(r) for r in rows], up, down)


def passed_along(value, axis, steps):
    count = lax.axis_size(axis)
    pairs = [(source, (source + steps) % count) for source in range(count)]
    return lax.ppermute(value, axis, pairs)


def swapped(value):
    count = lax.axis_size("ctx")
    return lax.ppermute(value, "ctx", [(i, i ^ 1) for i in range(count)])


def chain_prefix(mine, partner, decay, decay_partner, chip, chips, first, scale):
    heads = mine.shape[0]
    per = heads // CHUNKS
    keeps, gives, before = [], [], None

    def chunk(index):
        place = jnp.clip(index, 0, CHUNKS - 1) * per
        cut = [
            lax.dynamic_slice_in_dim(a, place, per, 0)
            for a in (mine, partner, decay, decay_partner)
        ]
        state0, state1 = jnp.where(first, cut[0], cut[1]), jnp.where(first, cut[1], cut[0])
        decay0, decay1 = jnp.where(first, cut[2], cut[3]), jnp.where(first, cut[3], cut[2])
        return state0, state1, decay0[:, None, :], decay1[:, None, :]

    for step in range(CHUNKS + chips - 2):
        state0, state1, decay0, decay1 = chunk(step - chip)
        gone = (decay1 * state0 + state1) * scale
        if before is not None:
            gone = (decay0 * decay1) * before.astype(F32) + gone
        pairs = [
            (2 * z + core, 2 * z + 2 + core)
            for z in range(chips - 1)
            if 0 <= step - z < CHUNKS
            for core in range(2)
        ]
        gone = gone.astype(jnp.float16)
        if step >= 2:
            gone, keeps[-1], gives[-1] = lax.optimization_barrier((gone, keeps[-1], gives[-1]))
        before = lax.ppermute(gone, "ctx", pairs)
        state0, _, decay0, _ = chunk(step - jnp.maximum(chip - 1, 0))
        prefix = lax.optimization_barrier(before).astype(F32) * (1.0 / scale)
        after0 = decay0 * prefix + state0
        keeps.append(jnp.where(first, prefix, after0))
        gives.append(jnp.where(first, after0, prefix))
    return keeps, [swapped(give) for give in gives]


def local(
    resid,
    queries,
    keys,
    values,
    log_decay,
    attn_gain,
    moe_gain,
    experts,
    combine_weight,
    w_up,
    w_down,
):
    return layer(
        resid[0], queries[0], keys[0], values[0], log_decay[0], attn_gain, moe_gain,
        experts[0], combine_weight[0], w_up[0], w_down[0],
    )


def layer(resid, queries, keys, values, rate, attn_gain, moe_gain, experts, weight, up, down):
    length, width = queries.shape
    count = lax.axis_size("ctx")
    me = lax.axis_index("ctx")
    chips, chip, core = count // 2, me // 2, me % 2
    half = width // HEAD // 2
    first = core == 0
    core1 = core.astype(jnp.int32)[None]
    turned = rate.T

    other, decay = half_state(1 - core1, turned, keys, values)
    partner = swapped(other)
    decay_partner = swapped(decay)
    mine, _ = half_state(core1, turned, keys, values)
    decay = lax.dynamic_slice_in_dim(decay, core * half, half, 0)
    decay_partner = lax.dynamic_slice_in_dim(decay_partner, core * half, half, 0)
    scale = 1.0
    while 36.0 * count * length * scale > 65000.0:
        scale = scale / 2
    keeps, gots = chain_prefix(
        mine, partner, decay, decay_partner, chip, chips, first, scale
    )
    late_by = jnp.maximum(chip - 1, 0)
    intra = []
    for part in range(PARTS):
        intra.append(intra_attention(part, PARTS, turned, queries, keys, values))
    flying = count // SHARDS
    if flying > 1:
        keep, got = (
            lax.dynamic_slice_in_dim(jnp.concatenate(a), late_by * (half // CHUNKS), half, 0)
            for a in (keeps, gots)
        )
        prefix = jnp.where(first, jnp.concatenate([keep, got]), jnp.concatenate([got, keep]))
        return many_experts(
            flying, rate, queries, jnp.concatenate(intra, axis=1), prefix, resid,
            attn_gain, moe_gain, experts, weight, up, down,
        )
    where = jnp.stack([core, late_by]).astype(jnp.int32)
    wcol, token, growth, q_rows, resid_rows, intra_rows = select(
        experts.T, weight.T, turned, queries, resid, intra
    )
    outbox, picked = selected_rows(
        where, growth, q_rows, resid_rows, intra_rows, keeps, gots, attn_gain, moe_gain
    )
    own = [outbox] + [
        lax.ppermute(outbox, "ctx", [(i, (i + 2 * d) % count) for i in range(count)])
        for d in range(1, chips)
    ]
    early = finish(where, turned, queries, intra, keeps, gots, resid, attn_gain)
    early = passed_along(early, "section", 1)
    up, down = fetch(up, down)
    others = [swapped(r) for r in own]
    mine, other = expert_rows(own + others, up, down)
    pair = (mine.astype(F32) + swapped(other).astype(F32)).astype(BF16)
    pair = pair.reshape(chips, CAP_SRC, width)
    backs = [
        lax.ppermute(pair[d], "ctx", [(i, (i - 2 * d) % count) for i in range(count)])
        for d in range(1, chips)
    ]
    late = passed_along(late_rows(picked, wcol, token, [pair[0], *backs]), "section", 1)
    return merged(early, late)[None]


def rms_scale(values_in, gain):
    return (
        values_in
        * lax.rsqrt(jnp.mean(values_in * values_in, axis=-1, keepdims=True) + 1e-06)
        * gain
    )


def many_experts(
    flying, rate, queries, intra, prefix, resid, attn_gain, moe_gain, experts, weight, up, down
):
    length, width = queries.shape
    heads = width // HEAD
    count = lax.axis_size("ctx")
    inter = jnp.exp(jnp.cumsum(rate, axis=0))[:, :, None] * jnp.einsum(
        "thd,hde->the",
        queries.astype(F32).reshape(length, heads, HEAD),
        prefix,
        precision=lax.Precision.HIGHEST,
    )
    hres = resid.astype(F32) + rms_scale(intra + inter.reshape(length, width), attn_gain)
    normed = rms_scale(hres, moe_gain).astype(BF16)
    slots = flying * CAP_SRC
    chosen = experts.reshape(-1)
    onehot = (chosen[:, None] == jnp.arange(flying)[None, :]).astype(jnp.int32)
    slot = jnp.sum((jnp.cumsum(onehot, axis=0) - onehot) * onehot, axis=1)
    target = jnp.where(chosen < flying, chosen * CAP_SRC + slot, -1)
    hot = (target[None, :] == jnp.arange(slots)[:, None]).reshape(slots, length, 2)
    outbox = dot(hot.any(axis=2).astype(BF16), normed).astype(BF16)
    outbox = outbox.reshape(1, flying, CAP_SRC, width)
    mine = lax.dynamic_index_in_dim(
        lax.all_gather(outbox, "ctx", axis=0, tiled=True), lax.axis_index("ctx") // SHARDS, 1, False
    )
    hidden = jax.nn.gelu(dot(mine.reshape(count * CAP_SRC, width), up), approximate=True)
    part = dot(hidden.astype(BF16), down).astype(BF16).reshape(count, CAP_SRC, width)
    returned = lax.all_to_all(part, "ctx", split_axis=0, concat_axis=0, tiled=True)
    summed = returned.reshape(flying, SHARDS, CAP_SRC, width).astype(F32).sum(axis=1)
    mixed = lax.dot_general(
        jnp.where(hot, weight[None], 0.0).sum(axis=2),
        summed.reshape(slots, width),
        (((0,), (0,)), ((), ())),
        precision=lax.Precision.HIGHEST,
    )
    return passed_along((hres + mixed).astype(BF16)[None], "section", 1)


def solution(mesh):
    return jax.shard_map(
        local,
        mesh=mesh,
        in_specs=(
            P("section", "ctx", None),
            P("section", "ctx", None),
            P("section", "ctx", None),
            P("section", "ctx", None),
            P("section", "ctx", None),
            P("section", None),
            P("section", None),
            P("section", "ctx", None),
            P("section", "ctx", None),
            P("section", None, "ctx"),
            P("section", "ctx", None),
        ),
        out_specs=P("section", "ctx", None),
        check_vma=False,
    )
```

```python
import jax
import jax.numpy as jnp
from jax import lax
from jax.experimental import pallas as pl
from jax.experimental.pallas import tpu as pltpu
from jax.sharding import PartitionSpec as P

HEAD = 128
SHARDS = 8
CAP_SRC = 16
GROUP = 8
CHUNKS = 4
PARTS = 3
FETCH_MIB = 42

F32, BF16 = jnp.float32, jnp.bfloat16


def dot(a, b, dims=((1,), (0,))):
    return lax.dot_general(a, b, (dims, ((), ())), preferred_element_type=F32)


def split(a):
    hi = a.astype(BF16)
    return hi, (a - hi.astype(F32)).astype(BF16)


def cumul_rows(rate_ref):
    length = rate_ref.shape[1]
    upper = (
        lax.broadcasted_iota(jnp.int32, (length, length), 0)
        <= lax.broadcasted_iota(jnp.int32, (length, length), 1)
    ).astype(F32)
    return lax.dot_general(
        rate_ref[...], upper, (((1,), (0,)), ((), ())), precision=lax.Precision.HIGHEST,
        preferred_element_type=F32,
    )


def in_vmem(x):
    return pltpu.with_memory_space_constraint(x, pltpu.VMEM)


VMEM_SPEC = pl.BlockSpec(memory_space=pltpu.VMEM)
HBM_SPEC = pl.BlockSpec(memory_space=pltpu.HBM)
ANY_SPEC = pl.BlockSpec(memory_space=pl.ANY)
SMEM_SPEC = pl.BlockSpec(memory_space=pltpu.SMEM)


def state_kernel(
    half_ref, rate_hbm, k_hbm, v_hbm, state_hbm, decay_hbm,
    rate_ref, k_ref, v_ref, state_ref, decay_ref, cum_ref, sems,
):
    groups = k_ref.shape[0]
    length = rate_ref.shape[1]
    span = GROUP * HEAD
    rates = pltpu.make_async_copy(rate_hbm, rate_ref, sems.at[3, 0])
    rates.start()

    def fetch(kind, g):
        source, target = ((k_hbm, k_ref), (v_hbm, v_ref))[kind]
        column = pl.multiple_of((half_ref[0] * groups + g) * span, span)
        return pltpu.make_async_copy(
            source.at[:, pl.ds(column, span)], target.at[g], sems.at[kind, g]
        )

    def store(g):
        at = pl.ds(g * GROUP, GROUP)
        return pltpu.make_async_copy(state_ref.at[at], state_hbm.at[at], sems.at[2, g])

    for g in range(groups):
        for kind in range(2):
            fetch(kind, g).start()
    rates.wait()
    cum_ref[...] = cumul_rows(rate_ref)
    decay_ref[...] = jnp.broadcast_to(jnp.exp(cum_ref[:, length - 1 :]), decay_ref.shape)
    decays = pltpu.make_async_copy(decay_ref, decay_hbm, sems.at[3, 1])
    decays.start()
    for g in range(groups):
        row = pl.multiple_of((half_ref[0] * groups + g) * GROUP, GROUP)
        cum = cum_ref[pl.ds(row, GROUP), :]
        tail = jnp.exp(cum[:, length - 1 :] - cum)
        for kind in range(2):
            fetch(kind, g).wait()
        for j in range(GROUP):
            cols = slice(j * HEAD, (j + 1) * HEAD)
            turned = k_ref[g, :, cols].T.astype(F32) * tail[j : j + 1, :]
            hi, lo = split(turned)
            v = v_ref[g, :, cols]
            state_ref[g * GROUP + j] = dot(hi, v) + dot(lo, v)
        store(g).start()
    for g in range(groups):
        store(g).wait()
    decays.wait()


def half_state(half, rate, keys, values):
    length, width = keys.shape
    heads = width // HEAD
    groups = heads // 2 // GROUP
    return pl.pallas_call(
        state_kernel,
        in_specs=[SMEM_SPEC, HBM_SPEC, HBM_SPEC, HBM_SPEC],
        out_specs=[HBM_SPEC, HBM_SPEC],
        out_shape=[
            jax.ShapeDtypeStruct((heads // 2, HEAD, HEAD), F32),
            jax.ShapeDtypeStruct((heads, HEAD), F32),
        ],
        scratch_shapes=[
            pltpu.VMEM((heads, length), F32),
            pltpu.VMEM((groups, length, GROUP * HEAD), BF16),
            pltpu.VMEM((groups, length, GROUP * HEAD), BF16),
            pltpu.VMEM((heads // 2, HEAD, HEAD), F32),
            pltpu.VMEM((heads, HEAD), F32),
            pltpu.VMEM((heads, length), F32),
            pltpu.SemaphoreType.DMA((4, max(groups, 2))),
        ],
        name="half_state",
    )(half, rate, keys, values)


def intra_kernel(first, rate_ref, q_hbm, k_hbm, v_hbm, out_hbm, q_ref, k_ref, v_ref, out_ref, sems):
    groups = sems.shape[1]
    length = rate_ref.shape[1]
    span = GROUP * HEAD

    def fetch(kind, g):
        source, target = ((q_hbm, q_ref), (k_hbm, k_ref), (v_hbm, v_ref))[kind]
        return pltpu.make_async_copy(
            source.at[:, pl.ds((first + g) * span, span)], target.at[g], sems.at[kind, g]
        )

    def store(g):
        at = pl.ds(g * span, span)
        return pltpu.make_async_copy(out_ref.at[g], out_hbm.at[:, at], sems.at[3, g])

    for g in range(groups):
        for kind in range(3):
            fetch(kind, g).start()
    cumul = cumul_rows(rate_ref)
    lower = lax.broadcasted_iota(jnp.int32, (length, length), 0) >= lax.broadcasted_iota(
        jnp.int32, (length, length), 1
    )
    for g in range(groups):
        for kind in range(3):
            fetch(kind, g).wait()
        for j in range(GROUP):
            head = (first + g) * GROUP + j
            cols = slice(j * HEAD, (j + 1) * HEAD)
            across = jnp.broadcast_to(cumul[head : head + 1, :], (length, length))
            weights = jnp.exp(jnp.where(lower, across.T - across, -1e30))
            scores = dot(q_ref[g, :, cols], k_ref[g, :, cols], ((1,), (1,)))
            hi, lo = split(scores * weights)
            v = v_ref[g, :, cols]
            out_ref[g, :, cols] = dot(hi, v) + dot(lo, v)
        store(g).start()
    for g in range(groups):
        store(g).wait()


def intra_attention(part, parts, rate, queries, keys, values):
    length, width = keys.shape
    groups = width // HEAD // GROUP // parts
    piece = (groups, length, GROUP * HEAD)
    return pl.pallas_call(
        lambda *refs: intra_kernel(part * groups, *refs),
        in_specs=[VMEM_SPEC] + [HBM_SPEC] * 3,
        out_specs=HBM_SPEC,
        out_shape=jax.ShapeDtypeStruct((length, width // parts), F32),
        scratch_shapes=[pltpu.VMEM(piece, BF16)] * 3
        + [pltpu.VMEM(piece, F32), pltpu.SemaphoreType.DMA((4, groups))],
        name="intra_attention",
    )(rate, queries, keys, values)


def select_kernel(
    parts, experts_ref, weight_ref, rate_ref, q_ref, resid_ref, *refs
):
    intra_refs = refs[:parts]
    wcol_ref, token_ref, growth_ref, q_out, resid_out, intra_out, at_ref, at_smem, sem = refs[parts:]
    slots = wcol_ref.shape[0]
    length = experts_ref.shape[1]
    before = (
        lax.broadcasted_iota(jnp.int32, (length, length), 0)
        < lax.broadcasted_iota(jnp.int32, (length, length), 1)
    ).astype(BF16)
    named = experts_ref[...] == 0
    taken = jnp.max(named.astype(F32), axis=0, keepdims=True)
    slot = dot(jnp.broadcast_to(taken, (8, length)).astype(BF16), before)[0:1, :]
    slot = jnp.where(taken > 0, slot, -1.0)
    hot = lax.broadcasted_iota(jnp.int32, (slots, length), 0).astype(F32) == slot
    weight = jnp.sum(jnp.where(named, weight_ref[...], 0.0), axis=0, keepdims=True)
    weight = jnp.sum(jnp.where(hot, weight, 0.0), axis=1, keepdims=True)
    wcol_ref[...] = jnp.broadcast_to(weight, wcol_ref.shape)
    at = lax.broadcasted_iota(jnp.int32, (slots, length), 1).astype(F32) + 1.0
    token = jnp.sum(jnp.where(hot, at, 0.0), axis=1, keepdims=True) - 1.0
    token_ref[...] = jnp.broadcast_to(token, token_ref.shape)
    at_ref[...] = jnp.broadcast_to(jnp.maximum(token, 0.0), at_ref.shape).astype(jnp.int32)
    known = pltpu.make_async_copy(at_ref, at_smem, sem)
    known.start()
    growth_ref[...] = lax.dot_general(
        hot.astype(F32), jnp.exp(cumul_rows(rate_ref)), (((1,), (1,)), ((), ())),
        precision=lax.Precision.HIGHEST, preferred_element_type=F32,
    )
    hot = hot.astype(BF16)
    q_out[...] = dot(hot, q_ref[...]).astype(BF16)
    resid_out[...] = dot(hot, resid_ref[...])
    known.wait()
    for s in range(slots):
        row = pl.ds(at_smem[s, 0], 1)
        for part, ref in enumerate(intra_refs):
            cols = slice(part * ref.shape[1], (part + 1) * ref.shape[1])
            intra_out[s : s + 1, cols] = ref[row, :]


def select(experts, weight, rate, queries, resid, intra):
    _, width = queries.shape
    heads = width // HEAD
    parts = len(intra)
    return pl.pallas_call(
        lambda *refs: select_kernel(parts, *refs),
        in_specs=[VMEM_SPEC] * (5 + parts),
        out_specs=[VMEM_SPEC] * 6,
        out_shape=[
            jax.ShapeDtypeStruct((CAP_SRC, 128), F32),
            jax.ShapeDtypeStruct((CAP_SRC, 128), F32),
            jax.ShapeDtypeStruct((CAP_SRC, heads), F32),
            jax.ShapeDtypeStruct((CAP_SRC, width), BF16),
            jax.ShapeDtypeStruct((CAP_SRC, width), F32),
            jax.ShapeDtypeStruct((CAP_SRC, width), F32),
        ],
        scratch_shapes=[
            pltpu.VMEM((CAP_SRC, 128), jnp.int32),
            pltpu.SMEM((CAP_SRC, 128), jnp.int32),
            pltpu.SemaphoreType.DMA,
        ],
        name="select",
    )(experts, weight, rate, queries, resid, *intra)


def prefix_copies(core_ref, given, keeps, gots, state_ref, start_ref, sems, chunks):
    decay_ref, partner, partner_mine = given
    steps = len(keeps)
    half = state_ref.shape[0] // 2
    per = half // chunks

    def own(n, c):
        place = pl.multiple_of(lax.rem(core_ref[0] + n, 2) * half + c * per, per)
        source = (partner, partner_mine)[n].at[pl.ds(c * per, per)]
        return pltpu.make_async_copy(source, start_ref.at[pl.ds(place, per)], sems.at[2 + n, c])

    def states(n, c, late):
        place = pl.multiple_of(lax.rem(core_ref[0] + n, 2) * half + c * per, per)
        source = (keeps, gots)[n][c + late]
        return pltpu.make_async_copy(source, state_ref.at[pl.ds(place, per)], sems.at[n, c])

    for c in range(chunks):
        for n in range(2):
            own(n, c).start()
    for late in range(steps - chunks + 1):

        @pl.when(core_ref[1] == late)
        def _():
            for c in range(chunks):
                for n in range(2):
                    states(n, c, late).start()

    def wait(c):
        for n in range(2):
            own(n, c).wait()
            states(n, c, 0).wait()

    second = core_ref[0].astype(F32)
    decays = jnp.where(core_ref[0] == 0, 1.0, decay_ref[...])

    def prefix(head):
        return decays[head : head + 1, :] * state_ref[head] + second * start_ref[head]

    return wait, prefix


def rows_kernel(chunks, steps, core_ref, growth_ref, q_ref, resid_ref, intra_ref, *refs):
    given, refs = refs[:3], refs[3:]
    keeps, gots, refs = refs[:steps], refs[steps : 2 * steps], refs[2 * steps :]
    again_ref, mgain_ref, outbox_ref, picked_ref, state_ref, start_ref, sems = refs
    _, width = picked_ref.shape
    heads = width // HEAD
    half = heads // 2
    per = half // chunks
    wait, prefix = prefix_copies(core_ref, given, keeps, gots, state_ref, start_ref, sems, chunks)
    for c in range(chunks):
        wait(c)
        for head in [n * half + c * per + j for n in range(2) for j in range(per)]:
            cols = slice(head * HEAD, (head + 1) * HEAD)
            hi, lo = split(prefix(head))
            q = q_ref[:, cols]
            value = growth_ref[:, head : head + 1] * (dot(q, hi) + dot(q, lo))
            picked_ref[:, cols] = intra_ref[:, cols] + value
    x = picked_ref[...]
    scale = lax.rsqrt(jnp.mean(x * x, axis=-1, keepdims=True) + 1e-06)
    hres = resid_ref[...] + x * scale * again_ref[...]
    picked_ref[...] = hres
    scale = lax.rsqrt(jnp.mean(hres * hres, axis=-1, keepdims=True) + 1e-06)
    outbox_ref[...] = (hres * scale * mgain_ref[...]).astype(BF16)


def selected_rows(
    core, growth, queries, resid, intra, given, keeps, gots, attn_gain, moe_gain
):
    slots, width = queries.shape
    heads = width // HEAD
    steps = len(keeps)
    return pl.pallas_call(
        lambda *refs: rows_kernel(CHUNKS, steps, *refs),
        in_specs=[SMEM_SPEC] + [VMEM_SPEC] * 5 + [ANY_SPEC] * (2 + 2 * steps) + [VMEM_SPEC] * 2,
        out_specs=[VMEM_SPEC] * 2,
        out_shape=[pltpu.VMEM((slots, width), BF16), pltpu.VMEM((slots, width), F32)],
        scratch_shapes=[
            pltpu.VMEM((heads, HEAD, HEAD), F32),
            pltpu.VMEM((heads, HEAD, HEAD), F32),
            pltpu.SemaphoreType.DMA((4, CHUNKS)),
        ],
        compiler_params=pltpu.CompilerParams(vmem_limit_bytes=16 << 20),
        name="selected_rows",
    )(core, growth, queries, resid, intra, *given, *keeps, *gots, attn_gain, moe_gain)


def finish_kernel(parts, chunks, steps, core_ref, rate_ref, q_hbm, *refs):
    intra_hbm, refs = refs[:parts], refs[parts:]
    given, refs = refs[:3], refs[3:]
    keeps, gots, refs = refs[:steps], refs[steps : 2 * steps], refs[2 * steps :]
    (
        resid_hbm, again_ref, early_ref,
        attn_ref, q_ref, intra_ref, state_ref, start_ref, resid_ref, sems, state_sems,
    ) = refs
    length, width = resid_ref.shape
    heads = width // HEAD
    groups = heads // GROUP
    span = GROUP * HEAD

    def copies(g):
        at = pl.ds(g * span, span)
        part, place = divmod(g * parts, groups)
        place = place // parts
        return [
            pltpu.make_async_copy(q_hbm.at[:, at], q_ref.at[g], sems.at[0, g]),
            pltpu.make_async_copy(
                intra_hbm[part].at[:, pl.ds(place * span, span)], intra_ref.at[g], sems.at[1, g]
            ),
        ]

    wait, prefix = prefix_copies(
        core_ref, given, keeps, gots, state_ref, start_ref, state_sems, chunks
    )
    for g in range(groups):
        for copy in copies(g):
            copy.start()
    rest = pltpu.make_async_copy(resid_hbm, resid_ref, sems.at[2, 0])
    rest.start()
    lower = (
        lax.broadcasted_iota(jnp.int32, (length, length), 0)
        >= lax.broadcasted_iota(jnp.int32, (length, length), 1)
    ).astype(F32)
    growth = jnp.exp(
        lax.dot_general(
            lower, rate_ref[...], (((1,), (1,)), ((), ())), precision=lax.Precision.HIGHEST,
            preferred_element_type=F32,
        )
    )
    for c in range(chunks):
        wait(c)
    squares = jnp.zeros((length, HEAD), F32)
    for g in range(groups):
        for copy in copies(g):
            copy.wait()
        for j in range(GROUP):
            head = g * GROUP + j
            mine = slice(j * HEAD, (j + 1) * HEAD)
            cols = slice(head * HEAD, (head + 1) * HEAD)
            hi, lo = split(prefix(head))
            q = q_ref[g, :, mine]
            value = growth[:, head : head + 1] * (dot(q, hi) + dot(q, lo))
            value = intra_ref[g, :, mine] + value
            attn_ref[:, cols] = value
            squares = squares + value * value
    scale_all = lax.rsqrt(jnp.sum(squares, axis=1, keepdims=True) * (1.0 / width) + 1e-06)
    rest.wait()
    rows = 16
    for r in range(length // rows):
        at = slice(r * rows, (r + 1) * rows)
        hres = resid_ref[at, :].astype(F32) + attn_ref[at, :] * scale_all[at] * again_ref[...]
        early_ref[at, :] = hres.astype(BF16)


def finish(core, rate, queries, intra, given, keeps, gots, resid, attn_gain):
    length, width = queries.shape
    heads = width // HEAD
    groups = heads // GROUP
    parts, steps = len(intra), len(keeps)
    args = [rate, queries, *intra, *given, *keeps, *gots, resid, attn_gain]
    return pl.pallas_call(
        lambda *refs: finish_kernel(parts, CHUNKS, steps, *refs),
        in_specs=[SMEM_SPEC, VMEM_SPEC]
        + [HBM_SPEC] * (1 + parts)
        + [VMEM_SPEC]
        + [ANY_SPEC] * (2 + 2 * steps)
        + [HBM_SPEC, VMEM_SPEC],
        out_specs=VMEM_SPEC,
        out_shape=pltpu.VMEM((length, width), BF16),
        scratch_shapes=[
            pltpu.VMEM((length, width), F32),
            pltpu.VMEM((groups, length, GROUP * HEAD), BF16),
            pltpu.VMEM((groups, length, GROUP * HEAD), F32),
            pltpu.VMEM((heads, HEAD, HEAD), F32),
            pltpu.VMEM((heads, HEAD, HEAD), F32),
            pltpu.VMEM((length, width), BF16),
            pltpu.SemaphoreType.DMA((3, groups)),
            pltpu.SemaphoreType.DMA((4, CHUNKS)),
        ],
        compiler_params=pltpu.CompilerParams(vmem_limit_bytes=32 << 20),
        name="finish",
    )(core, *args)


def late_kernel(count, picked_ref, wcol_ref, token_ref, *refs):
    parts, out_ref = refs[:count], refs[count]
    width = picked_ref.shape[1]
    total = parts[0][...].astype(F32)
    for part in parts[1:]:
        total = total + part[...].astype(F32)
    out_ref[:, :width] = (picked_ref[...] + wcol_ref[:, :1] * total).astype(BF16)
    out_ref[:, width:] = token_ref[...].astype(BF16)


def late_rows(picked, wcol, token, parts):
    slots, width = picked.shape
    return pl.pallas_call(
        lambda *refs: late_kernel(len(parts), *refs),
        in_specs=[VMEM_SPEC] * (3 + len(parts)),
        out_specs=VMEM_SPEC,
        out_shape=pltpu.VMEM((slots, width + 128), BF16),
        compiler_params=pltpu.CompilerParams(vmem_limit_bytes=8 << 20),
        name="late_rows",
    )(in_vmem(picked), wcol, token, *[in_vmem(p) for p in parts])


def merge_kernel(early_ref, late_ref, out_hbm, out_ref, sems):
    length, width = early_ref.shape
    slots = late_ref.shape[0]
    parts = sems.shape[0]
    span = width // parts
    token = late_ref[:, width:].astype(F32)
    found = token == lax.broadcasted_iota(jnp.int32, (slots, length), 1).astype(F32)
    found = found.astype(BF16)
    down = ((0,), (0,))
    hit = dot(found, jnp.ones((slots, 128), BF16), down)[:, :1] > 0.5

    def store(i):
        at = pl.ds(i * span, span)
        return pltpu.make_async_copy(out_ref.at[:, at], out_hbm.at[:, at], sems.at[i])

    for i in range(parts):
        at = slice(i * span, (i + 1) * span)
        rows = dot(found, late_ref[:, at], down)
        out_ref[:, at] = jnp.where(hit, rows, early_ref[:, at].astype(F32)).astype(BF16)
        store(i).start()
    for i in range(parts):
        store(i).wait()


def merged(early, late):
    return pl.pallas_call(
        merge_kernel,
        in_specs=[VMEM_SPEC] * 2,
        out_specs=HBM_SPEC,
        out_shape=jax.ShapeDtypeStruct(early.shape, BF16),
        scratch_shapes=[pltpu.VMEM(early.shape, BF16), pltpu.SemaphoreType.DMA((4,))],
        compiler_params=pltpu.CompilerParams(vmem_limit_bytes=8 << 20),
        name="merged",
    )(in_vmem(early), in_vmem(late))


def fetch_kernel(up_hbm, down_hbm, up_ref, down_ref, sems):
    copies = [
        pltpu.make_async_copy(up_hbm, up_ref, sems.at[0]),
        pltpu.make_async_copy(down_hbm, down_ref, sems.at[1]),
    ]
    for copy in copies:
        copy.start()
    for copy in copies:
        copy.wait()


def fetch(up, down):
    return pl.pallas_call(
        fetch_kernel,
        in_specs=[HBM_SPEC] * 2,
        out_specs=[VMEM_SPEC] * 2,
        out_shape=[pltpu.VMEM(up.shape, BF16), pltpu.VMEM(down.shape, BF16)],
        scratch_shapes=[pltpu.SemaphoreType.DMA((2,))],
        compiler_params=pltpu.CompilerParams(vmem_limit_bytes=FETCH_MIB << 20),
        name="fetch",
    )(up, down)


def expert_kernel(count, *refs):
    row_refs = refs[:count]
    up_ref, down_ref, mine_ref, other_ref, rows_ref, hidden_ref = refs[count:]
    half = mine_ref.shape[0]
    each = row_refs[0].shape[0]
    for n, ref in enumerate(row_refs):
        rows_ref[n * each : (n + 1) * each, :] = ref[...]
    hidden = dot(rows_ref[...], up_ref[...])
    hidden_ref[...] = jax.nn.gelu(hidden, approximate=True).astype(BF16)
    parts = 4
    length = down_ref.shape[1] // parts
    for i in range(parts):
        at = slice(i * length, (i + 1) * length)
        part = dot(hidden_ref[...], down_ref[:, at]).astype(BF16)
        mine_ref[:, at] = part[:half]
        other_ref[:, at] = part[half:]


def expert_rows(rows, up, down):
    width, units = up.shape
    total = sum(r.shape[0] for r in rows)
    return pl.pallas_call(
        lambda *refs: expert_kernel(len(rows), *refs),
        in_specs=[VMEM_SPEC] * (len(rows) + 2),
        out_specs=[VMEM_SPEC] * 2,
        out_shape=[pltpu.VMEM((total // 2, width), BF16)] * 2,
        scratch_shapes=[pltpu.VMEM((total, width), BF16), pltpu.VMEM((total, units), BF16)],
        compiler_params=pltpu.CompilerParams(vmem_limit_bytes=12 << 20),
        name="expert_rows",
    )(*[in_vmem(r) for r in rows], up, down)


def passed_along(value, axis, steps):
    count = lax.axis_size(axis)
    pairs = [(source, (source + steps) % count) for source in range(count)]
    return lax.ppermute(value, axis, pairs)


def swapped(value):
    count = lax.axis_size("ctx")
    return lax.ppermute(value, "ctx", [(i, i ^ 1) for i in range(count)])


def chain_prefix(mine, partner, decay, decay_partner, chip, chips, first, scale):
    heads = mine.shape[0]
    per = heads // CHUNKS
    keeps, gots, before = [], [], None
    for step in range(CHUNKS + chips - 2):
        place = jnp.clip(step - chip, 0, CHUNKS - 1) * per
        cut = [
            lax.dynamic_slice_in_dim(a, place, per, 0)
            for a in (mine, partner, decay, decay_partner)
        ]
        state0, state1 = jnp.where(first, cut[0], cut[1]), jnp.where(first, cut[1], cut[0])
        decay0, decay1 = jnp.where(first, cut[2], cut[3]), jnp.where(first, cut[3], cut[2])
        gone = (decay1[:, None, :] * state0 + state1) * scale
        if before is not None:
            gone = (decay0 * decay1)[:, None, :] * before.astype(F32) + gone
        pairs = [
            (2 * z + core, 2 * z + 2 + core)
            for z in range(chips - 1)
            if 0 <= step - z < CHUNKS
            for core in range(2)
        ]
        before = lax.ppermute(gone.astype(jnp.float16), "ctx", pairs)
        keeps.append(before.astype(F32) * (1.0 / scale))
        gots.append(swapped(before).astype(F32) * (1.0 / scale))
    return keeps, gots


def local(
    resid,
    queries,
    keys,
    values,
    log_decay,
    attn_gain,
    moe_gain,
    experts,
    combine_weight,
    w_up,
    w_down,
):
    return layer(
        resid[0], queries[0], keys[0], values[0], log_decay[0], attn_gain, moe_gain,
        experts[0], combine_weight[0], w_up[0], w_down[0],
    )


def layer(resid, queries, keys, values, rate, attn_gain, moe_gain, experts, weight, up, down):
    length, width = queries.shape
    count = lax.axis_size("ctx")
    me = lax.axis_index("ctx")
    chips, chip, core = count // 2, me // 2, me % 2
    half = width // HEAD // 2
    first = core == 0
    core1 = core.astype(jnp.int32)[None]
    turned = rate.T

    other, decay = half_state(1 - core1, turned, keys, values)
    partner = swapped(other)
    decay_partner = swapped(decay)
    mine, _ = half_state(core1, turned, keys, values)
    partner_mine = swapped(mine)
    before_me = (decay_partner, partner, partner_mine)
    decay = lax.dynamic_slice_in_dim(decay, core * half, half, 0)
    decay_partner = lax.dynamic_slice_in_dim(decay_partner, core * half, half, 0)
    scale = 1.0
    while 36.0 * count * length * scale > 65000.0:
        scale = scale / 2
    keeps, gots = chain_prefix(
        mine, partner, decay, decay_partner, chip, chips, first, scale
    )
    late_by = jnp.maximum(chip - 1, 0)
    intra = []
    for part in range(PARTS):
        intra.append(intra_attention(part, PARTS, turned, queries, keys, values))
    flying = count // SHARDS
    if flying > 1:
        keep, got = (
            lax.dynamic_slice_in_dim(jnp.concatenate(a), late_by * (half // CHUNKS), half, 0)
            for a in (keeps, gots)
        )
        prefix = jnp.where(first, jnp.concatenate([keep, got]), jnp.concatenate([got, keep]))
        done = prefix * before_me[0][:, None, :] + jnp.concatenate([partner_mine, partner])
        prefix = jnp.where(first, prefix, done)
        return many_experts(
            flying, rate, queries, jnp.concatenate(intra, axis=1), prefix, resid,
            attn_gain, moe_gain, experts, weight, up, down,
        )
    where = jnp.stack([core, late_by]).astype(jnp.int32)
    wcol, token, growth, q_rows, resid_rows, intra_rows = select(
        experts.T, weight.T, turned, queries, resid, intra
    )
    outbox, picked = selected_rows(
        where, growth, q_rows, resid_rows, intra_rows, before_me, keeps, gots, attn_gain, moe_gain
    )
    own = [outbox] + [
        lax.ppermute(outbox, "ctx", [(i, (i + 2 * d) % count) for i in range(count)])
        for d in range(1, chips)
    ]
    early = finish(where, turned, queries, intra, before_me, keeps, gots, resid, attn_gain)
    early = passed_along(early, "section", 1)
    up, down = fetch(up, down)
    others = [swapped(r) for r in own]
    mine, other = expert_rows(own + others, up, down)
    pair = (mine.astype(F32) + swapped(other).astype(F32)).astype(BF16)
    pair = pair.reshape(chips, CAP_SRC, width)
    backs = [
        lax.ppermute(pair[d], "ctx", [(i, (i - 2 * d) % count) for i in range(count)])
        for d in range(1, chips)
    ]
    late = passed_along(late_rows(picked, wcol, token, [pair[0], *backs]), "section", 1)
    return merged(early, late)[None]


def rms_scale(values_in, gain):
    return (
        values_in
        * lax.rsqrt(jnp.mean(values_in * values_in, axis=-1, keepdims=True) + 1e-06)
        * gain
    )


def many_experts(
    flying, rate, queries, intra, prefix, resid, attn_gain, moe_gain, experts, weight, up, down
):
    length, width = queries.shape
    heads = width // HEAD
    count = lax.axis_size("ctx")
    inter = jnp.exp(jnp.cumsum(rate, axis=0))[:, :, None] * jnp.einsum(
        "thd,hde->the",
        queries.astype(F32).reshape(length, heads, HEAD),
        prefix,
        precision=lax.Precision.HIGHEST,
    )
    hres = resid.astype(F32) + rms_scale(intra + inter.reshape(length, width), attn_gain)
    normed = rms_scale(hres, moe_gain).astype(BF16)
    slots = flying * CAP_SRC
    chosen = experts.reshape(-1)
    onehot = (chosen[:, None] == jnp.arange(flying)[None, :]).astype(jnp.int32)
    slot = jnp.sum((jnp.cumsum(onehot, axis=0) - onehot) * onehot, axis=1)
    target = jnp.where(chosen < flying, chosen * CAP_SRC + slot, -1)
    hot = (target[None, :] == jnp.arange(slots)[:, None]).reshape(slots, length, 2)
    outbox = dot(hot.any(axis=2).astype(BF16), normed).astype(BF16)
    outbox = outbox.reshape(1, flying, CAP_SRC, width)
    mine = lax.dynamic_index_in_dim(
        lax.all_gather(outbox, "ctx", axis=0, tiled=True), lax.axis_index("ctx") // SHARDS, 1, False
    )
    hidden = jax.nn.gelu(dot(mine.reshape(count * CAP_SRC, width), up), approximate=True)
    part = dot(hidden.astype(BF16), down).astype(BF16).reshape(count, CAP_SRC, width)
    returned = lax.all_to_all(part, "ctx", split_axis=0, concat_axis=0, tiled=True)
    summed = returned.reshape(flying, SHARDS, CAP_SRC, width).astype(F32).sum(axis=1)
    mixed = lax.dot_general(
        jnp.where(hot, weight[None], 0.0).sum(axis=2),
        summed.reshape(slots, width),
        (((0,), (0,)), ((), ())),
        precision=lax.Precision.HIGHEST,
    )
    return passed_along((hres + mixed).astype(BF16)[None], "section", 1)


def solution(mesh):
    return jax.shard_map(
        local,
        mesh=mesh,
        in_specs=(
            P("section", "ctx", None),
            P("section", "ctx", None),
            P("section", "ctx", None),
            P("section", "ctx", None),
            P("section", "ctx", None),
            P("section", None),
            P("section", None),
            P("section", "ctx", None),
            P("section", "ctx", None),
            P("section", None, "ctx"),
            P("section", "ctx", None),
        ),
        out_specs=P("section", "ctx", None),
        check_vma=False,
    )
```

```python
import jax
import jax.numpy as jnp
from jax import lax
from jax.experimental import pallas as pl
from jax.experimental.pallas import tpu as pltpu
from jax.sharding import PartitionSpec as P

HEAD = 128
SHARDS = 8
CAP_SRC = 16
GROUP = 8
CHUNKS = 4
PARTS = 3
FETCH_MIB = 42

F32, BF16 = jnp.float32, jnp.bfloat16


def dot(a, b, dims=((1,), (0,))):
    return lax.dot_general(a, b, (dims, ((), ())), preferred_element_type=F32)


def split(a):
    hi = a.astype(BF16)
    return hi, (a - hi.astype(F32)).astype(BF16)


def cumul_rows(rate_ref):
    length = rate_ref.shape[1]
    upper = (
        lax.broadcasted_iota(jnp.int32, (length, length), 0)
        <= lax.broadcasted_iota(jnp.int32, (length, length), 1)
    ).astype(F32)
    return lax.dot_general(
        rate_ref[...], upper, (((1,), (0,)), ((), ())), precision=lax.Precision.HIGHEST,
        preferred_element_type=F32,
    )


def in_vmem(x):
    return pltpu.with_memory_space_constraint(x, pltpu.VMEM)


VMEM_SPEC = pl.BlockSpec(memory_space=pltpu.VMEM)
HBM_SPEC = pl.BlockSpec(memory_space=pltpu.HBM)
ANY_SPEC = pl.BlockSpec(memory_space=pl.ANY)
SMEM_SPEC = pl.BlockSpec(memory_space=pltpu.SMEM)


def state_kernel(
    half_ref, rate_hbm, k_hbm, v_hbm, state_hbm, decay_hbm,
    rate_ref, k_ref, v_ref, state_ref, decay_ref, cum_ref, sems,
):
    groups = k_ref.shape[0]
    length = rate_ref.shape[1]
    span = GROUP * HEAD
    rates = pltpu.make_async_copy(rate_hbm, rate_ref, sems.at[3, 0])
    rates.start()

    def fetch(kind, g):
        source, target = ((k_hbm, k_ref), (v_hbm, v_ref))[kind]
        column = pl.multiple_of((half_ref[0] * groups + g) * span, span)
        return pltpu.make_async_copy(
            source.at[:, pl.ds(column, span)], target.at[g], sems.at[kind, g]
        )

    def store(g):
        at = pl.ds(g * GROUP, GROUP)
        return pltpu.make_async_copy(state_ref.at[at], state_hbm.at[at], sems.at[2, g])

    for g in range(groups):
        for kind in range(2):
            fetch(kind, g).start()
    rates.wait()
    cum_ref[...] = cumul_rows(rate_ref)
    rows = pl.ds(pl.multiple_of(half_ref[0] * groups * GROUP, GROUP), groups * GROUP)
    decay_ref[...] = jnp.broadcast_to(jnp.exp(cum_ref[rows, length - 1 :]), decay_ref.shape)
    decays = pltpu.make_async_copy(decay_ref, decay_hbm, sems.at[3, 1])
    decays.start()
    for g in range(groups):
        row = pl.multiple_of((half_ref[0] * groups + g) * GROUP, GROUP)
        cum = cum_ref[pl.ds(row, GROUP), :]
        tail = jnp.exp(cum[:, length - 1 :] - cum)
        for kind in range(2):
            fetch(kind, g).wait()
        for j in range(GROUP):
            cols = slice(j * HEAD, (j + 1) * HEAD)
            turned = k_ref[g, :, cols].T.astype(F32) * tail[j : j + 1, :]
            hi, lo = split(turned)
            v = v_ref[g, :, cols]
            state_ref[g * GROUP + j] = dot(hi, v) + dot(lo, v)
        store(g).start()
    for g in range(groups):
        store(g).wait()
    decays.wait()


def half_state(half, rate, keys, values):
    length, width = keys.shape
    heads = width // HEAD
    groups = heads // 2 // GROUP
    return pl.pallas_call(
        state_kernel,
        in_specs=[SMEM_SPEC, HBM_SPEC, HBM_SPEC, HBM_SPEC],
        out_specs=[HBM_SPEC, HBM_SPEC],
        out_shape=[
            jax.ShapeDtypeStruct((heads // 2, HEAD, HEAD), F32),
            jax.ShapeDtypeStruct((heads // 2, HEAD), F32),
        ],
        scratch_shapes=[
            pltpu.VMEM((heads, length), F32),
            pltpu.VMEM((groups, length, GROUP * HEAD), BF16),
            pltpu.VMEM((groups, length, GROUP * HEAD), BF16),
            pltpu.VMEM((heads // 2, HEAD, HEAD), F32),
            pltpu.VMEM((heads // 2, HEAD), F32),
            pltpu.VMEM((heads, length), F32),
            pltpu.SemaphoreType.DMA((4, max(groups, 2))),
        ],
        name="half_state",
    )(half, rate, keys, values)


def intra_kernel(first, rate_ref, q_hbm, k_hbm, v_hbm, *refs):
    out_hbm, q_ref, k_ref, v_ref, out_ref, sems = refs[-6:]
    groups = sems.shape[1]
    length = rate_ref.shape[1]
    span = GROUP * HEAD

    def fetch(kind, g):
        source, target = ((q_hbm, q_ref), (k_hbm, k_ref), (v_hbm, v_ref))[kind]
        return pltpu.make_async_copy(
            source.at[:, pl.ds((first + g) * span, span)], target.at[g], sems.at[kind, g]
        )

    def store(g):
        at = pl.ds((first + g) * span, span)
        return pltpu.make_async_copy(out_ref.at[g], out_hbm.at[:, at], sems.at[3, g])

    for g in range(groups):
        for kind in range(3):
            fetch(kind, g).start()
    cumul = cumul_rows(rate_ref)
    lower = lax.broadcasted_iota(jnp.int32, (length, length), 0) >= lax.broadcasted_iota(
        jnp.int32, (length, length), 1
    )
    for g in range(groups):
        for kind in range(3):
            fetch(kind, g).wait()
        for j in range(GROUP):
            head = (first + g) * GROUP + j
            cols = slice(j * HEAD, (j + 1) * HEAD)
            across = jnp.broadcast_to(cumul[head : head + 1, :], (length, length))
            weights = jnp.exp(jnp.where(lower, across.T - across, -1e30))
            scores = dot(q_ref[g, :, cols], k_ref[g, :, cols], ((1,), (1,)))
            hi, lo = split(scores * weights)
            v = v_ref[g, :, cols]
            out_ref[g, :, cols] = dot(hi, v) + dot(lo, v)
        store(g).start()
    for g in range(groups):
        store(g).wait()


def intra_attention(part, parts, rate, queries, keys, values, out):
    length, width = keys.shape
    groups = width // HEAD // GROUP // parts
    piece = (groups, length, GROUP * HEAD)
    return pl.pallas_call(
        lambda *refs: intra_kernel(part * groups, *refs),
        in_specs=[VMEM_SPEC] + [HBM_SPEC] * (3 + len(out)),
        out_specs=HBM_SPEC,
        out_shape=jax.ShapeDtypeStruct((length, width), F32),
        scratch_shapes=[pltpu.VMEM(piece, BF16)] * 3
        + [pltpu.VMEM(piece, F32), pltpu.SemaphoreType.DMA((4, groups))],
        input_output_aliases={4: 0} if out else {},
        name="intra_attention",
    )(rate, queries, keys, values, *out)


def select_kernel(
    experts_ref, weight_ref, rate_ref, q_ref, resid_ref, intra_ref,
    wcol_ref, token_ref, growth_ref, q_out, resid_out, intra_out, at_ref, at_smem, sem,
):
    slots = wcol_ref.shape[0]
    length = experts_ref.shape[1]
    before = (
        lax.broadcasted_iota(jnp.int32, (length, length), 0)
        < lax.broadcasted_iota(jnp.int32, (length, length), 1)
    ).astype(BF16)
    named = experts_ref[...] == 0
    taken = jnp.max(named.astype(F32), axis=0, keepdims=True)
    slot = dot(jnp.broadcast_to(taken, (8, length)).astype(BF16), before)[0:1, :]
    slot = jnp.where(taken > 0, slot, -1.0)
    hot = lax.broadcasted_iota(jnp.int32, (slots, length), 0).astype(F32) == slot
    weight = jnp.sum(jnp.where(named, weight_ref[...], 0.0), axis=0, keepdims=True)
    weight = jnp.sum(jnp.where(hot, weight, 0.0), axis=1, keepdims=True)
    wcol_ref[...] = jnp.broadcast_to(weight, wcol_ref.shape)
    at = lax.broadcasted_iota(jnp.int32, (slots, length), 1).astype(F32) + 1.0
    token = jnp.sum(jnp.where(hot, at, 0.0), axis=1, keepdims=True) - 1.0
    token_ref[...] = jnp.broadcast_to(token, token_ref.shape)
    at_ref[...] = jnp.broadcast_to(jnp.maximum(token, 0.0), at_ref.shape).astype(jnp.int32)
    known = pltpu.make_async_copy(at_ref, at_smem, sem)
    known.start()
    growth = lax.dot_general(
        hot.astype(F32), jnp.exp(cumul_rows(rate_ref)), (((1,), (1,)), ((), ())),
        precision=lax.Precision.HIGHEST, preferred_element_type=F32,
    )
    for head in range(growth.shape[1]):
        growth_ref[:, head * HEAD : (head + 1) * HEAD] = jnp.broadcast_to(
            growth[:, head : head + 1], (slots, HEAD)
        )
    hot = hot.astype(BF16)
    q_out[...] = dot(hot, q_ref[...]).astype(BF16)
    resid_out[...] = dot(hot, resid_ref[...])
    known.wait()
    for s in range(slots):
        intra_out[s : s + 1, :] = intra_ref[pl.ds(at_smem[s, 0], 1), :]


def select(experts, weight, rate, queries, resid, intra):
    _, width = queries.shape
    return pl.pallas_call(
        select_kernel,
        in_specs=[VMEM_SPEC] * 6,
        out_specs=[VMEM_SPEC] * 6,
        out_shape=[
            jax.ShapeDtypeStruct((CAP_SRC, 128), F32),
            jax.ShapeDtypeStruct((CAP_SRC, 128), F32),
            jax.ShapeDtypeStruct((CAP_SRC, width), F32),
            jax.ShapeDtypeStruct((CAP_SRC, width), BF16),
            jax.ShapeDtypeStruct((CAP_SRC, width), F32),
            jax.ShapeDtypeStruct((CAP_SRC, width), F32),
        ],
        scratch_shapes=[
            pltpu.VMEM((CAP_SRC, 128), jnp.int32),
            pltpu.SMEM((CAP_SRC, 128), jnp.int32),
            pltpu.SemaphoreType.DMA,
        ],
        name="select",
    )(experts, weight, rate, queries, resid, intra)


def each_state(core_ref, keeps, gots, chunks, use):
    steps, per = len(keeps), keeps[0].shape[0]
    half = chunks * per
    for late in range(steps - chunks + 1):

        @pl.when(core_ref[1] == late)
        def _():
            for n in range(2):
                start = lax.rem(core_ref[0] + n, 2) * half
                for c in range(chunks):
                    for j in range(per):
                        column = pl.multiple_of((start + c * per + j) * HEAD, HEAD)
                        use(pl.ds(column, HEAD), (keeps, gots)[n][c + late][j])


def rows_kernel(chunks, steps, core_ref, growth_ref, q_ref, resid_ref, intra_ref, *refs):
    keeps, gots, refs = refs[:steps], refs[steps : 2 * steps], refs[2 * steps :]
    again_ref, mgain_ref, outbox_ref, picked_ref = refs

    def use(cols, state):
        hi, lo = split(state)
        q = q_ref[:, cols]
        picked_ref[:, cols] = intra_ref[:, cols] + growth_ref[:, cols] * (dot(q, hi) + dot(q, lo))

    each_state(core_ref, keeps, gots, chunks, use)
    x = picked_ref[...]
    scale = lax.rsqrt(jnp.mean(x * x, axis=-1, keepdims=True) + 1e-06)
    hres = resid_ref[...] + x * scale * again_ref[...]
    picked_ref[...] = hres
    scale = lax.rsqrt(jnp.mean(hres * hres, axis=-1, keepdims=True) + 1e-06)
    outbox_ref[...] = (hres * scale * mgain_ref[...]).astype(BF16)


def selected_rows(core, growth, queries, resid, intra, keeps, gots, attn_gain, moe_gain):
    slots, width = queries.shape
    steps = len(keeps)
    args = [growth, queries, resid, intra, *keeps, *gots, attn_gain, moe_gain]
    return pl.pallas_call(
        lambda *refs: rows_kernel(CHUNKS, steps, *refs),
        in_specs=[SMEM_SPEC] + [VMEM_SPEC] * len(args),
        out_specs=[VMEM_SPEC] * 2,
        out_shape=[pltpu.VMEM((slots, width), BF16), pltpu.VMEM((slots, width), F32)],
        compiler_params=pltpu.CompilerParams(vmem_limit_bytes=8 << 20),
        name="selected_rows",
    )(core, *[in_vmem(a) for a in args])


def finish_kernel(chunks, steps, core_ref, rate_ref, q_ref, intra_ref, *refs):
    keeps, gots, refs = refs[:steps], refs[steps : 2 * steps], refs[2 * steps :]
    resid_ref, again_ref, early_ref, attn_ref, scale_ref = refs
    length, width = resid_ref.shape
    growth = jnp.exp(cumul_rows(rate_ref))
    for head in range(width // HEAD):
        across = jnp.broadcast_to(growth[head : head + 1, :], (length, length))
        scale_ref[:, head * HEAD : (head + 1) * HEAD] = across.T

    def use(cols, state):
        hi, lo = split(state)
        q = q_ref[:, cols]
        attn_ref[:, cols] = intra_ref[:, cols] + scale_ref[:, cols] * (dot(q, hi) + dot(q, lo))

    each_state(core_ref, keeps, gots, chunks, use)
    rows = 16

    def norm(r, carry):
        at = pl.ds(pl.multiple_of(r * rows, rows), rows)
        x = attn_ref[at, :]
        scale = lax.rsqrt(jnp.mean(x * x, axis=-1, keepdims=True) + 1e-06)
        hres = resid_ref[at, :].astype(F32) + x * scale * again_ref[...]
        early_ref[at, :] = hres.astype(BF16)
        return carry

    lax.fori_loop(0, length // rows, norm, 0)


def finish(core, rate, queries, intra, keeps, gots, resid, attn_gain):
    length, width = queries.shape
    steps = len(keeps)
    args = [rate, queries, intra, *keeps, *gots, resid, attn_gain]
    return pl.pallas_call(
        lambda *refs: finish_kernel(CHUNKS, steps, *refs),
        in_specs=[SMEM_SPEC] + [VMEM_SPEC] * len(args),
        out_specs=VMEM_SPEC,
        out_shape=pltpu.VMEM((length, width), BF16),
        scratch_shapes=[pltpu.VMEM((length, width), F32), pltpu.VMEM((length, width), F32)],
        compiler_params=pltpu.CompilerParams(vmem_limit_bytes=14 << 20),
        name="finish",
    )(core, *[in_vmem(a) for a in args])


def late_kernel(count, picked_ref, wcol_ref, token_ref, *refs):
    parts, out_ref = refs[:count], refs[count]
    width = picked_ref.shape[1]
    total = parts[0][...].astype(F32)
    for part in parts[1:]:
        total = total + part[...].astype(F32)
    out_ref[:, :width] = (picked_ref[...] + wcol_ref[:, :1] * total).astype(BF16)
    out_ref[:, width:] = token_ref[...].astype(BF16)


def late_rows(picked, wcol, token, parts):
    slots, width = picked.shape
    return pl.pallas_call(
        lambda *refs: late_kernel(len(parts), *refs),
        in_specs=[VMEM_SPEC] * (3 + len(parts)),
        out_specs=VMEM_SPEC,
        out_shape=pltpu.VMEM((slots, width + 128), BF16),
        compiler_params=pltpu.CompilerParams(vmem_limit_bytes=8 << 20),
        name="late_rows",
    )(in_vmem(picked), wcol, token, *[in_vmem(p) for p in parts])


def merge_kernel(early_ref, late_ref, out_hbm, out_ref, sems):
    length, width = early_ref.shape
    slots = late_ref.shape[0]
    parts = sems.shape[0]
    span = width // parts
    token = late_ref[:, width:].astype(F32)
    found = token == lax.broadcasted_iota(jnp.int32, (slots, length), 1).astype(F32)
    found = found.astype(BF16)
    down = ((0,), (0,))
    hit = dot(found, jnp.ones((slots, 128), BF16), down)[:, :1] > 0.5

    def store(i):
        at = pl.ds(i * span, span)
        return pltpu.make_async_copy(out_ref.at[:, at], out_hbm.at[:, at], sems.at[i])

    for i in range(parts):
        at = slice(i * span, (i + 1) * span)
        rows = dot(found, late_ref[:, at], down)
        out_ref[:, at] = jnp.where(hit, rows, early_ref[:, at].astype(F32)).astype(BF16)
        store(i).start()
    for i in range(parts):
        store(i).wait()


def merged(early, late):
    return pl.pallas_call(
        merge_kernel,
        in_specs=[VMEM_SPEC] * 2,
        out_specs=HBM_SPEC,
        out_shape=jax.ShapeDtypeStruct(early.shape, BF16),
        scratch_shapes=[pltpu.VMEM(early.shape, BF16), pltpu.SemaphoreType.DMA((4,))],
        compiler_params=pltpu.CompilerParams(vmem_limit_bytes=8 << 20),
        name="merged",
    )(in_vmem(early), in_vmem(late))


def fetch_kernel(up_hbm, down_hbm, up_ref, down_ref, sems):
    copies = [
        pltpu.make_async_copy(up_hbm, up_ref, sems.at[0]),
        pltpu.make_async_copy(down_hbm, down_ref, sems.at[1]),
    ]
    for copy in copies:
        copy.start()
    for copy in copies:
        copy.wait()


def fetch(up, down):
    return pl.pallas_call(
        fetch_kernel,
        in_specs=[HBM_SPEC] * 2,
        out_specs=[VMEM_SPEC] * 2,
        out_shape=[pltpu.VMEM(up.shape, BF16), pltpu.VMEM(down.shape, BF16)],
        scratch_shapes=[pltpu.SemaphoreType.DMA((2,))],
        compiler_params=pltpu.CompilerParams(vmem_limit_bytes=FETCH_MIB << 20),
        name="fetch",
    )(up, down)


def expert_kernel(count, *refs):
    row_refs = refs[:count]
    up_ref, down_ref, mine_ref, other_ref, rows_ref, hidden_ref = refs[count:]
    half = mine_ref.shape[0]
    each = row_refs[0].shape[0]
    for n, ref in enumerate(row_refs):
        rows_ref[n * each : (n + 1) * each, :] = ref[...]
    hidden = dot(rows_ref[...], up_ref[...])
    hidden_ref[...] = jax.nn.gelu(hidden, approximate=True).astype(BF16)
    parts = 4
    length = down_ref.shape[1] // parts
    for i in range(parts):
        at = slice(i * length, (i + 1) * length)
        part = dot(hidden_ref[...], down_ref[:, at]).astype(BF16)
        mine_ref[:, at] = part[:half]
        other_ref[:, at] = part[half:]


def expert_rows(rows, up, down):
    width, units = up.shape
    total = sum(r.shape[0] for r in rows)
    return pl.pallas_call(
        lambda *refs: expert_kernel(len(rows), *refs),
        in_specs=[VMEM_SPEC] * (len(rows) + 2),
        out_specs=[VMEM_SPEC] * 2,
        out_shape=[pltpu.VMEM((total // 2, width), BF16)] * 2,
        scratch_shapes=[pltpu.VMEM((total, width), BF16), pltpu.VMEM((total, units), BF16)],
        compiler_params=pltpu.CompilerParams(vmem_limit_bytes=12 << 20),
        name="expert_rows",
    )(*[in_vmem(r) for r in rows], up, down)


def passed_along(value, axis, steps):
    count = lax.axis_size(axis)
    pairs = [(source, (source + steps) % count) for source in range(count)]
    return lax.ppermute(value, axis, pairs)


def swapped(value):
    count = lax.axis_size("ctx")
    return lax.ppermute(value, "ctx", [(i, i ^ 1) for i in range(count)])


def chain_prefix(mine, partner, decay, decay_partner, chip, chips, first, scale):
    heads = mine.shape[0]
    per = heads // CHUNKS
    keeps, gives, before = [], [], None

    def chunk(index):
        place = jnp.clip(index, 0, CHUNKS - 1) * per
        cut = [
            lax.dynamic_slice_in_dim(a, place, per, 0)
            for a in (mine, partner, decay, decay_partner)
        ]
        state0, state1 = jnp.where(first, cut[0], cut[1]), jnp.where(first, cut[1], cut[0])
        decay0, decay1 = jnp.where(first, cut[2], cut[3]), jnp.where(first, cut[3], cut[2])
        return state0, state1, decay0[:, None, :], decay1[:, None, :]

    for step in range(CHUNKS + chips - 2):
        state0, state1, decay0, decay1 = chunk(step - chip)
        gone = (decay1 * state0 + state1) * scale
        if before is not None:
            gone = (decay0 * decay1) * before.astype(F32) + gone
        pairs = [
            (2 * z + core, 2 * z + 2 + core)
            for z in range(chips - 1)
            if 0 <= step - z < CHUNKS
            for core in range(2)
        ]
        gone = gone.astype(jnp.float16)
        if step >= 2:
            gone, keeps[-1], gives[-1] = lax.optimization_barrier((gone, keeps[-1], gives[-1]))
        before = lax.ppermute(gone, "ctx", pairs)
        state0, _, decay0, _ = chunk(step - jnp.maximum(chip - 1, 0))
        prefix = lax.optimization_barrier(before).astype(F32) * (1.0 / scale)
        after0 = decay0 * prefix + state0
        keeps.append(jnp.where(first, prefix, after0))
        gives.append(jnp.where(first, after0, prefix))
    return keeps, [swapped(give) for give in gives]


def local(
    resid,
    queries,
    keys,
    values,
    log_decay,
    attn_gain,
    moe_gain,
    experts,
    combine_weight,
    w_up,
    w_down,
):
    return layer(
        resid[0], queries[0], keys[0], values[0], log_decay[0], attn_gain, moe_gain,
        experts[0], combine_weight[0], w_up[0], w_down[0],
    )


def layer(resid, queries, keys, values, rate, attn_gain, moe_gain, experts, weight, up, down):
    length, width = queries.shape
    count = lax.axis_size("ctx")
    me = lax.axis_index("ctx")
    chips, chip, core = count // 2, me // 2, me % 2
    half = width // HEAD // 2
    first = core == 0
    core1 = core.astype(jnp.int32)[None]
    turned = rate.T

    other, decay_other = half_state(1 - core1, turned, keys, values)
    partner, decay_partner = swapped(other), swapped(decay_other)
    mine, decay = half_state(core1, turned, keys, values)
    scale = 1.0
    while 36.0 * count * length * scale > 65000.0:
        scale = scale / 2
    keeps, gots = chain_prefix(
        mine, partner, decay, decay_partner, chip, chips, first, scale
    )
    late_by = jnp.maximum(chip - 1, 0)
    intra = []
    for part in range(PARTS):
        intra = [intra_attention(part, PARTS, turned, queries, keys, values, intra)]
    intra = intra[0]
    flying = count // SHARDS
    if flying > 1:
        keep, got = (
            lax.dynamic_slice_in_dim(jnp.concatenate(a), late_by * (half // CHUNKS), half, 0)
            for a in (keeps, gots)
        )
        prefix = jnp.where(first, jnp.concatenate([keep, got]), jnp.concatenate([got, keep]))
        return many_experts(
            flying, rate, queries, intra, prefix, resid,
            attn_gain, moe_gain, experts, weight, up, down,
        )
    where = jnp.stack([core, late_by]).astype(jnp.int32)
    wcol, token, growth, q_rows, resid_rows, intra_rows = select(
        experts.T, weight.T, turned, queries, resid, intra
    )
    outbox, picked = selected_rows(
        where, growth, q_rows, resid_rows, intra_rows, keeps, gots, attn_gain, moe_gain
    )
    own = [outbox] + [
        lax.ppermute(outbox, "ctx", [(i, (i + 2 * d) % count) for i in range(count)])
        for d in range(1, chips)
    ]
    early = finish(where, turned, queries, intra, keeps, gots, resid, attn_gain)
    early = passed_along(early, "section", 1)
    up, down = fetch(up, down)
    others = [swapped(r) for r in own]
    mine, other = expert_rows(own + others, up, down)
    pair = (mine.astype(F32) + swapped(other).astype(F32)).astype(BF16)
    pair = pair.reshape(chips, CAP_SRC, width)
    backs = [
        lax.ppermute(pair[d], "ctx", [(i, (i - 2 * d) % count) for i in range(count)])
        for d in range(1, chips)
    ]
    late = passed_along(late_rows(picked, wcol, token, [pair[0], *backs]), "section", 1)
    return merged(early, late)[None]


def rms_scale(values_in, gain):
    return (
        values_in
        * lax.rsqrt(jnp.mean(values_in * values_in, axis=-1, keepdims=True) + 1e-06)
        * gain
    )


def many_experts(
    flying, rate, queries, intra, prefix, resid, attn_gain, moe_gain, experts, weight, up, down
):
    length, width = queries.shape
    heads = width // HEAD
    count = lax.axis_size("ctx")
    inter = jnp.exp(jnp.cumsum(rate, axis=0))[:, :, None] * jnp.einsum(
        "thd,hde->the",
        queries.astype(F32).reshape(length, heads, HEAD),
        prefix,
        precision=lax.Precision.HIGHEST,
    )
    hres = resid.astype(F32) + rms_scale(intra + inter.reshape(length, width), attn_gain)
    normed = rms_scale(hres, moe_gain).astype(BF16)
    slots = flying * CAP_SRC
    chosen = experts.reshape(-1)
    onehot = (chosen[:, None] == jnp.arange(flying)[None, :]).astype(jnp.int32)
    slot = jnp.sum((jnp.cumsum(onehot, axis=0) - onehot) * onehot, axis=1)
    target = jnp.where(chosen < flying, chosen * CAP_SRC + slot, -1)
    hot = (target[None, :] == jnp.arange(slots)[:, None]).reshape(slots, length, 2)
    outbox = dot(hot.any(axis=2).astype(BF16), normed).astype(BF16)
    outbox = outbox.reshape(1, flying, CAP_SRC, width)
    mine = lax.dynamic_index_in_dim(
        lax.all_gather(outbox, "ctx", axis=0, tiled=True), lax.axis_index("ctx") // SHARDS, 1, False
    )
    hidden = jax.nn.gelu(dot(mine.reshape(count * CAP_SRC, width), up), approximate=True)
    part = dot(hidden.astype(BF16), down).astype(BF16).reshape(count, CAP_SRC, width)
    returned = lax.all_to_all(part, "ctx", split_axis=0, concat_axis=0, tiled=True)
    summed = returned.reshape(flying, SHARDS, CAP_SRC, width).astype(F32).sum(axis=1)
    mixed = lax.dot_general(
        jnp.where(hot, weight[None], 0.0).sum(axis=2),
        summed.reshape(slots, width),
        (((0,), (0,)), ((), ())),
        precision=lax.Precision.HIGHEST,
    )
    return passed_along((hres + mixed).astype(BF16)[None], "section", 1)


def solution(mesh):
    return jax.shard_map(
        local,
        mesh=mesh,
        in_specs=(
            P("section", "ctx", None),
            P("section", "ctx", None),
            P("section", "ctx", None),
            P("section", "ctx", None),
            P("section", "ctx", None),
            P("section", None),
            P("section", None),
            P("section", "ctx", None),
            P("section", "ctx", None),
            P("section", None, "ctx"),
            P("section", "ctx", None),
        ),
        out_specs=P("section", "ctx", None),
        check_vma=False,
    )
```

```python
import jax
import jax.numpy as jnp
from jax import lax
from jax.experimental import pallas as pl
from jax.experimental.pallas import tpu as pltpu
from jax.sharding import PartitionSpec as P

HEAD = 128
SHARDS = 8
CAP_SRC = 16
GROUP = 8
CHUNKS = 3
PARTS = 1
FETCH_MIB = 42

F32, BF16 = jnp.float32, jnp.bfloat16


def dot(a, b, dims=((1,), (0,))):
    return lax.dot_general(a, b, (dims, ((), ())), preferred_element_type=F32)


def split(a):
    hi = a.astype(BF16)
    return hi, (a - hi.astype(F32)).astype(BF16)


def cumul_rows(rate_ref):
    length = rate_ref.shape[1]
    upper = (
        lax.broadcasted_iota(jnp.int32, (length, length), 0)
        <= lax.broadcasted_iota(jnp.int32, (length, length), 1)
    ).astype(F32)
    return lax.dot_general(
        rate_ref[...], upper, (((1,), (0,)), ((), ())), precision=lax.Precision.HIGHEST,
        preferred_element_type=F32,
    )


def in_vmem(x):
    return pltpu.with_memory_space_constraint(x, pltpu.VMEM)


VMEM_SPEC = pl.BlockSpec(memory_space=pltpu.VMEM)
HBM_SPEC = pl.BlockSpec(memory_space=pltpu.HBM)
ANY_SPEC = pl.BlockSpec(memory_space=pl.ANY)
SMEM_SPEC = pl.BlockSpec(memory_space=pltpu.SMEM)


def state_kernel(
    half_ref, rate_hbm, k_hbm, v_hbm, state_hbm, decay_hbm,
    rate_ref, k_ref, v_ref, state_ref, decay_ref, cum_ref, sems,
):
    groups = k_ref.shape[0]
    length = rate_ref.shape[1]
    span = GROUP * HEAD
    rates = pltpu.make_async_copy(rate_hbm, rate_ref, sems.at[3, 0])
    rates.start()

    def fetch(kind, g):
        source, target = ((k_hbm, k_ref), (v_hbm, v_ref))[kind]
        column = pl.multiple_of((half_ref[0] * groups + g) * span, span)
        return pltpu.make_async_copy(
            source.at[:, pl.ds(column, span)], target.at[g], sems.at[kind, g]
        )

    def store(g):
        at = pl.ds(g * GROUP, GROUP)
        return pltpu.make_async_copy(state_ref.at[at], state_hbm.at[at], sems.at[2, g])

    for g in range(groups):
        for kind in range(2):
            fetch(kind, g).start()
    rates.wait()
    cum_ref[...] = cumul_rows(rate_ref)
    decay_ref[...] = jnp.broadcast_to(jnp.exp(cum_ref[:, length - 1 :]), decay_ref.shape)
    decays = pltpu.make_async_copy(decay_ref, decay_hbm, sems.at[3, 1])
    decays.start()
    for g in range(groups):
        row = pl.multiple_of((half_ref[0] * groups + g) * GROUP, GROUP)
        cum = cum_ref[pl.ds(row, GROUP), :]
        tail = jnp.exp(cum[:, length - 1 :] - cum)
        for kind in range(2):
            fetch(kind, g).wait()
        for j in range(GROUP):
            cols = slice(j * HEAD, (j + 1) * HEAD)
            turned = k_ref[g, :, cols].T.astype(F32) * tail[j : j + 1, :]
            hi, lo = split(turned)
            v = v_ref[g, :, cols]
            state_ref[g * GROUP + j] = dot(hi, v) + dot(lo, v)
        store(g).start()
    for g in range(groups):
        store(g).wait()
    decays.wait()


def half_state(half, rate, keys, values):
    length, width = keys.shape
    heads = width // HEAD
    groups = heads // 2 // GROUP
    return pl.pallas_call(
        state_kernel,
        in_specs=[SMEM_SPEC, HBM_SPEC, HBM_SPEC, HBM_SPEC],
        out_specs=[HBM_SPEC, HBM_SPEC],
        out_shape=[
            jax.ShapeDtypeStruct((heads // 2, HEAD, HEAD), F32),
            jax.ShapeDtypeStruct((heads, HEAD), F32),
        ],
        scratch_shapes=[
            pltpu.VMEM((heads, length), F32),
            pltpu.VMEM((groups, length, GROUP * HEAD), BF16),
            pltpu.VMEM((groups, length, GROUP * HEAD), BF16),
            pltpu.VMEM((heads // 2, HEAD, HEAD), F32),
            pltpu.VMEM((heads, HEAD), F32),
            pltpu.VMEM((heads, length), F32),
            pltpu.SemaphoreType.DMA((4, max(groups, 2))),
        ],
        name="half_state",
    )(half, rate, keys, values)


def intra_kernel(first, rate_ref, q_hbm, k_hbm, v_hbm, *refs):
    out_hbm, q_ref, k_ref, v_ref, out_ref, sems = refs[-6:]
    groups = sems.shape[1]
    length = rate_ref.shape[1]
    span = GROUP * HEAD

    def fetch(kind, g):
        source, target = ((q_hbm, q_ref), (k_hbm, k_ref), (v_hbm, v_ref))[kind]
        return pltpu.make_async_copy(
            source.at[:, pl.ds((first + g) * span, span)], target.at[g], sems.at[kind, g]
        )

    def store(g):
        at = pl.ds((first + g) * span, span)
        return pltpu.make_async_copy(out_ref.at[g], out_hbm.at[:, at], sems.at[3, g])

    for g in range(groups):
        for kind in range(3):
            fetch(kind, g).start()
    cumul = cumul_rows(rate_ref)
    lower = lax.broadcasted_iota(jnp.int32, (length, length), 0) >= lax.broadcasted_iota(
        jnp.int32, (length, length), 1
    )
    for g in range(groups):
        for kind in range(3):
            fetch(kind, g).wait()
        for j in range(GROUP):
            head = (first + g) * GROUP + j
            cols = slice(j * HEAD, (j + 1) * HEAD)
            across = jnp.broadcast_to(cumul[head : head + 1, :], (length, length))
            weights = jnp.exp(jnp.where(lower, across.T - across, -1e30))
            scores = dot(q_ref[g, :, cols], k_ref[g, :, cols], ((1,), (1,)))
            hi, lo = split(scores * weights)
            v = v_ref[g, :, cols]
            out_ref[g, :, cols] = dot(hi, v) + dot(lo, v)
        store(g).start()
    for g in range(groups):
        store(g).wait()


def intra_attention(part, parts, rate, queries, keys, values, out):
    length, width = keys.shape
    groups = width // HEAD // GROUP // parts
    piece = (groups, length, GROUP * HEAD)
    return pl.pallas_call(
        lambda *refs: intra_kernel(part * groups, *refs),
        in_specs=[VMEM_SPEC] + [HBM_SPEC] * (3 + len(out)),
        out_specs=HBM_SPEC,
        out_shape=jax.ShapeDtypeStruct((length, width), F32),
        scratch_shapes=[pltpu.VMEM(piece, BF16)] * 3
        + [pltpu.VMEM(piece, F32), pltpu.SemaphoreType.DMA((4, groups))],
        input_output_aliases={4: 0} if out else {},
        name="intra_attention",
    )(rate, queries, keys, values, *out)


def select_kernel(
    experts_ref, weight_ref, rate_ref, q_ref, resid_ref, intra_ref,
    wcol_ref, token_ref, growth_ref, q_out, resid_out, intra_out, at_ref, at_smem, sem,
):
    slots = wcol_ref.shape[0]
    length = experts_ref.shape[1]
    before = (
        lax.broadcasted_iota(jnp.int32, (length, length), 0)
        < lax.broadcasted_iota(jnp.int32, (length, length), 1)
    ).astype(BF16)
    named = experts_ref[...] == 0
    taken = jnp.max(named.astype(F32), axis=0, keepdims=True)
    slot = dot(jnp.broadcast_to(taken, (8, length)).astype(BF16), before)[0:1, :]
    slot = jnp.where(taken > 0, slot, -1.0)
    hot = lax.broadcasted_iota(jnp.int32, (slots, length), 0).astype(F32) == slot
    weight = jnp.sum(jnp.where(named, weight_ref[...], 0.0), axis=0, keepdims=True)
    weight = jnp.sum(jnp.where(hot, weight, 0.0), axis=1, keepdims=True)
    wcol_ref[...] = jnp.broadcast_to(weight, wcol_ref.shape)
    at = lax.broadcasted_iota(jnp.int32, (slots, length), 1).astype(F32) + 1.0
    token = jnp.sum(jnp.where(hot, at, 0.0), axis=1, keepdims=True) - 1.0
    token_ref[...] = jnp.broadcast_to(token, token_ref.shape)
    at_ref[...] = jnp.broadcast_to(jnp.maximum(token, 0.0), at_ref.shape).astype(jnp.int32)
    known = pltpu.make_async_copy(at_ref, at_smem, sem)
    known.start()
    growth = lax.dot_general(
        hot.astype(F32), jnp.exp(cumul_rows(rate_ref)), (((1,), (1,)), ((), ())),
        precision=lax.Precision.HIGHEST, preferred_element_type=F32,
    )
    for head in range(growth.shape[1]):
        growth_ref[:, head * HEAD : (head + 1) * HEAD] = jnp.broadcast_to(
            growth[:, head : head + 1], (slots, HEAD)
        )
    hot = hot.astype(BF16)
    q_out[...] = dot(hot, q_ref[...]).astype(BF16)
    resid_out[...] = dot(hot, resid_ref[...])
    known.wait()
    for s in range(slots):
        intra_out[s : s + 1, :] = intra_ref[pl.ds(at_smem[s, 0], 1), :]


def select(experts, weight, rate, queries, resid, intra):
    _, width = queries.shape
    return pl.pallas_call(
        select_kernel,
        in_specs=[VMEM_SPEC] * 6,
        out_specs=[VMEM_SPEC] * 6,
        out_shape=[
            jax.ShapeDtypeStruct((CAP_SRC, 128), F32),
            jax.ShapeDtypeStruct((CAP_SRC, 128), F32),
            jax.ShapeDtypeStruct((CAP_SRC, width), F32),
            jax.ShapeDtypeStruct((CAP_SRC, width), BF16),
            jax.ShapeDtypeStruct((CAP_SRC, width), F32),
            jax.ShapeDtypeStruct((CAP_SRC, width), F32),
        ],
        scratch_shapes=[
            pltpu.VMEM((CAP_SRC, 128), jnp.int32),
            pltpu.SMEM((CAP_SRC, 128), jnp.int32),
            pltpu.SemaphoreType.DMA,
        ],
        name="select",
    )(experts, weight, rate, queries, resid, intra)


def each_state(core_ref, keeps, gots, chunks, use):
    steps, per = len(keeps), keeps[0].shape[0]
    half = chunks * per
    for late in range(steps - chunks + 1):

        @pl.when(core_ref[1] == late)
        def _():
            for n in range(2):
                start = lax.rem(core_ref[0] + n, 2) * half
                for c in range(chunks):
                    for j in range(per):
                        column = pl.multiple_of((start + c * per + j) * HEAD, HEAD)
                        use(pl.ds(column, HEAD), (keeps, gots)[n][c + late][j])


def rows_kernel(chunks, steps, core_ref, growth_ref, q_ref, resid_ref, intra_ref, *refs):
    keeps, gots, refs = refs[:steps], refs[steps : 2 * steps], refs[2 * steps :]
    again_ref, mgain_ref, outbox_ref, picked_ref = refs

    def use(cols, state):
        hi, lo = split(state)
        q = q_ref[:, cols]
        picked_ref[:, cols] = intra_ref[:, cols] + growth_ref[:, cols] * (dot(q, hi) + dot(q, lo))

    each_state(core_ref, keeps, gots, chunks, use)
    x = picked_ref[...]
    scale = lax.rsqrt(jnp.mean(x * x, axis=-1, keepdims=True) + 1e-06)
    hres = resid_ref[...] + x * scale * again_ref[...]
    picked_ref[...] = hres
    scale = lax.rsqrt(jnp.mean(hres * hres, axis=-1, keepdims=True) + 1e-06)
    outbox_ref[...] = (hres * scale * mgain_ref[...]).astype(BF16)


def selected_rows(core, growth, queries, resid, intra, keeps, gots, attn_gain, moe_gain):
    slots, width = queries.shape
    steps = len(keeps)
    args = [growth, queries, resid, intra, *keeps, *gots, attn_gain, moe_gain]
    return pl.pallas_call(
        lambda *refs: rows_kernel(CHUNKS, steps, *refs),
        in_specs=[SMEM_SPEC] + [VMEM_SPEC] * len(args),
        out_specs=[VMEM_SPEC] * 2,
        out_shape=[pltpu.VMEM((slots, width), BF16), pltpu.VMEM((slots, width), F32)],
        compiler_params=pltpu.CompilerParams(vmem_limit_bytes=8 << 20),
        name="selected_rows",
    )(core, *[in_vmem(a) for a in args])


def finish_kernel(chunks, steps, core_ref, rate_ref, q_ref, intra_ref, *refs):
    keeps, gots, refs = refs[:steps], refs[steps : 2 * steps], refs[2 * steps :]
    resid_ref, again_ref, early_ref, attn_ref, scale_ref = refs
    length, width = resid_ref.shape
    growth = jnp.exp(cumul_rows(rate_ref))
    for head in range(width // HEAD):
        across = jnp.broadcast_to(growth[head : head + 1, :], (length, length))
        scale_ref[:, head * HEAD : (head + 1) * HEAD] = across.T

    def use(cols, state):
        hi, lo = split(state)
        q = q_ref[:, cols]
        attn_ref[:, cols] = intra_ref[:, cols] + scale_ref[:, cols] * (dot(q, hi) + dot(q, lo))

    each_state(core_ref, keeps, gots, chunks, use)
    rows = 16

    def norm(r, carry):
        at = pl.ds(pl.multiple_of(r * rows, rows), rows)
        x = attn_ref[at, :]
        scale = lax.rsqrt(jnp.mean(x * x, axis=-1, keepdims=True) + 1e-06)
        hres = resid_ref[at, :].astype(F32) + x * scale * again_ref[...]
        early_ref[at, :] = hres.astype(BF16)
        return carry

    lax.fori_loop(0, length // rows, norm, 0)


def finish(core, rate, queries, intra, keeps, gots, resid, attn_gain):
    length, width = queries.shape
    steps = len(keeps)
    args = [rate, queries, intra, *keeps, *gots, resid, attn_gain]
    return pl.pallas_call(
        lambda *refs: finish_kernel(CHUNKS, steps, *refs),
        in_specs=[SMEM_SPEC] + [VMEM_SPEC] * len(args),
        out_specs=VMEM_SPEC,
        out_shape=pltpu.VMEM((length, width), BF16),
        scratch_shapes=[pltpu.VMEM((length, width), F32), pltpu.VMEM((length, width), F32)],
        compiler_params=pltpu.CompilerParams(vmem_limit_bytes=14 << 20),
        name="finish",
    )(core, *[in_vmem(a) for a in args])


def late_kernel(count, picked_ref, wcol_ref, token_ref, *refs):
    parts, out_ref = refs[:count], refs[count]
    width = picked_ref.shape[1]
    total = parts[0][...].astype(F32)
    for part in parts[1:]:
        total = total + part[...].astype(F32)
    out_ref[:, :width] = (picked_ref[...] + wcol_ref[:, :1] * total).astype(BF16)
    out_ref[:, width:] = token_ref[...].astype(BF16)


def late_rows(picked, wcol, token, parts):
    slots, width = picked.shape
    return pl.pallas_call(
        lambda *refs: late_kernel(len(parts), *refs),
        in_specs=[VMEM_SPEC] * (3 + len(parts)),
        out_specs=VMEM_SPEC,
        out_shape=pltpu.VMEM((slots, width + 128), BF16),
        compiler_params=pltpu.CompilerParams(vmem_limit_bytes=8 << 20),
        name="late_rows",
    )(in_vmem(picked), wcol, token, *[in_vmem(p) for p in parts])


def merge_kernel(early_ref, late_ref, out_hbm, out_ref, sems):
    length, width = early_ref.shape
    slots = late_ref.shape[0]
    parts = sems.shape[0]
    span = width // parts
    token = late_ref[:, width:].astype(F32)
    found = token == lax.broadcasted_iota(jnp.int32, (slots, length), 1).astype(F32)
    found = found.astype(BF16)
    down = ((0,), (0,))
    hit = dot(found, jnp.ones((slots, 128), BF16), down)[:, :1] > 0.5

    def store(i):
        at = pl.ds(i * span, span)
        return pltpu.make_async_copy(out_ref.at[:, at], out_hbm.at[:, at], sems.at[i])

    for i in range(parts):
        at = slice(i * span, (i + 1) * span)
        rows = dot(found, late_ref[:, at], down)
        out_ref[:, at] = jnp.where(hit, rows, early_ref[:, at].astype(F32)).astype(BF16)
        store(i).start()
    for i in range(parts):
        store(i).wait()


def merged(early, late):
    return pl.pallas_call(
        merge_kernel,
        in_specs=[VMEM_SPEC] * 2,
        out_specs=HBM_SPEC,
        out_shape=jax.ShapeDtypeStruct(early.shape, BF16),
        scratch_shapes=[pltpu.VMEM(early.shape, BF16), pltpu.SemaphoreType.DMA((4,))],
        compiler_params=pltpu.CompilerParams(vmem_limit_bytes=8 << 20),
        name="merged",
    )(in_vmem(early), in_vmem(late))


def fetch_kernel(up_hbm, down_hbm, up_ref, down_ref, sems):
    copies = [
        pltpu.make_async_copy(up_hbm, up_ref, sems.at[0]),
        pltpu.make_async_copy(down_hbm, down_ref, sems.at[1]),
    ]
    for copy in copies:
        copy.start()
    for copy in copies:
        copy.wait()


def fetch(up, down):
    return pl.pallas_call(
        fetch_kernel,
        in_specs=[HBM_SPEC] * 2,
        out_specs=[VMEM_SPEC] * 2,
        out_shape=[pltpu.VMEM(up.shape, BF16), pltpu.VMEM(down.shape, BF16)],
        scratch_shapes=[pltpu.SemaphoreType.DMA((2,))],
        compiler_params=pltpu.CompilerParams(vmem_limit_bytes=FETCH_MIB << 20),
        name="fetch",
    )(up, down)


def expert_kernel(count, *refs):
    row_refs = refs[:count]
    up_ref, down_ref, mine_ref, other_ref, rows_ref, hidden_ref = refs[count:]
    half = mine_ref.shape[0]
    each = row_refs[0].shape[0]
    for n, ref in enumerate(row_refs):
        rows_ref[n * each : (n + 1) * each, :] = ref[...]
    hidden = dot(rows_ref[...], up_ref[...])
    hidden_ref[...] = jax.nn.gelu(hidden, approximate=True).astype(BF16)
    parts = 4
    length = down_ref.shape[1] // parts
    for i in range(parts):
        at = slice(i * length, (i + 1) * length)
        part = dot(hidden_ref[...], down_ref[:, at]).astype(BF16)
        mine_ref[:, at] = part[:half]
        other_ref[:, at] = part[half:]


def expert_rows(rows, up, down):
    width, units = up.shape
    total = sum(r.shape[0] for r in rows)
    return pl.pallas_call(
        lambda *refs: expert_kernel(len(rows), *refs),
        in_specs=[VMEM_SPEC] * (len(rows) + 2),
        out_specs=[VMEM_SPEC] * 2,
        out_shape=[pltpu.VMEM((total // 2, width), BF16)] * 2,
        scratch_shapes=[pltpu.VMEM((total, width), BF16), pltpu.VMEM((total, units), BF16)],
        compiler_params=pltpu.CompilerParams(vmem_limit_bytes=12 << 20),
        name="expert_rows",
    )(*[in_vmem(r) for r in rows], up, down)


def passed_along(value, axis, steps):
    count = lax.axis_size(axis)
    pairs = [(source, (source + steps) % count) for source in range(count)]
    return lax.ppermute(value, axis, pairs)


def swapped(value):
    count = lax.axis_size("ctx")
    return lax.ppermute(value, "ctx", [(i, i ^ 1) for i in range(count)])


def chain_prefix(mine, partner, decay, decay_partner, chip, chips, first, scale):
    heads = mine.shape[0]
    per = heads // CHUNKS
    keeps, gives, before = [], [], None

    def chunk(index):
        place = jnp.clip(index, 0, CHUNKS - 1) * per
        cut = [
            lax.dynamic_slice_in_dim(a, place, per, 0)
            for a in (mine, partner, decay, decay_partner)
        ]
        state0, state1 = jnp.where(first, cut[0], cut[1]), jnp.where(first, cut[1], cut[0])
        decay0, decay1 = jnp.where(first, cut[2], cut[3]), jnp.where(first, cut[3], cut[2])
        return state0, state1, decay0[:, None, :], decay1[:, None, :]

    for step in range(CHUNKS + chips - 2):
        state0, state1, decay0, decay1 = chunk(step - chip)
        gone = (decay1 * state0 + state1) * scale
        if before is not None:
            gone = (decay0 * decay1) * before.astype(F32) + gone
        pairs = [
            (2 * z + core, 2 * z + 2 + core)
            for z in range(chips - 1)
            if 0 <= step - z < CHUNKS
            for core in range(2)
        ]
        gone = gone.astype(jnp.float16)
        if step >= 2:
            gone, keeps[-1], gives[-1] = lax.optimization_barrier((gone, keeps[-1], gives[-1]))
        before = lax.ppermute(gone, "ctx", pairs)
        state0, _, decay0, _ = chunk(step - jnp.maximum(chip - 1, 0))
        prefix = lax.optimization_barrier(before).astype(F32) * (1.0 / scale)
        after0 = decay0 * prefix + state0
        keeps.append(jnp.where(first, prefix, after0))
        gives.append(jnp.where(first, after0, prefix))
    return keeps, [swapped(give) for give in gives]


def local(
    resid,
    queries,
    keys,
    values,
    log_decay,
    attn_gain,
    moe_gain,
    experts,
    combine_weight,
    w_up,
    w_down,
):
    return layer(
        resid[0], queries[0], keys[0], values[0], log_decay[0], attn_gain, moe_gain,
        experts[0], combine_weight[0], w_up[0], w_down[0],
    )


def layer(resid, queries, keys, values, rate, attn_gain, moe_gain, experts, weight, up, down):
    length, width = queries.shape
    count = lax.axis_size("ctx")
    me = lax.axis_index("ctx")
    chips, chip, core = count // 2, me // 2, me % 2
    half = width // HEAD // 2
    first = core == 0
    core1 = core.astype(jnp.int32)[None]
    turned = rate.T

    other, decay = half_state(1 - core1, turned, keys, values)
    partner, decay_partner = swapped(other), swapped(decay)
    mine, _ = half_state(core1, turned, keys, values)
    decay, decay_partner = (
        lax.dynamic_slice_in_dim(a, core * half, half, 0) for a in (decay, decay_partner)
    )
    scale = 1.0
    while 36.0 * count * length * scale > 65000.0:
        scale = scale / 2
    keeps, gots = chain_prefix(
        mine, partner, decay, decay_partner, chip, chips, first, scale
    )
    late_by = jnp.maximum(chip - 1, 0)
    intra = []
    for part in range(PARTS):
        intra = [intra_attention(part, PARTS, turned, queries, keys, values, intra)]
    intra = intra[0]
    flying = count // SHARDS
    if flying > 1:
        keep, got = (
            lax.dynamic_slice_in_dim(jnp.concatenate(a), late_by * (half // CHUNKS), half, 0)
            for a in (keeps, gots)
        )
        prefix = jnp.where(first, jnp.concatenate([keep, got]), jnp.concatenate([got, keep]))
        return many_experts(
            flying, rate, queries, intra, prefix, resid,
            attn_gain, moe_gain, experts, weight, up, down,
        )
    where = jnp.stack([core, late_by]).astype(jnp.int32)
    wcol, token, growth, q_rows, resid_rows, intra_rows = select(
        experts.T, weight.T, turned, queries, resid, intra
    )
    outbox, picked = selected_rows(
        where, growth, q_rows, resid_rows, intra_rows, keeps, gots, attn_gain, moe_gain
    )
    own = [outbox] + [
        lax.ppermute(outbox, "ctx", [(i, i ^ (2 * d)) for i in range(count)])
        for d in range(1, chips)
    ]
    early = finish(where, turned, queries, intra, keeps, gots, resid, attn_gain)
    early = passed_along(early, "section", 1)
    up, down = fetch(up, down)
    others = [swapped(r) for r in own]
    mine, other = expert_rows(own + others, up, down)
    pair = (mine.astype(F32) + swapped(other).astype(F32)).astype(BF16)
    pair = pair.reshape(chips, CAP_SRC, width)
    backs = [
        lax.ppermute(pair[d], "ctx", [(i, i ^ (2 * d)) for i in range(count)])
        for d in range(1, chips)
    ]
    late = passed_along(late_rows(picked, wcol, token, [pair[0], *backs]), "section", 1)
    return merged(early, late)[None]


def rms_scale(values_in, gain):
    return (
        values_in
        * lax.rsqrt(jnp.mean(values_in * values_in, axis=-1, keepdims=True) + 1e-06)
        * gain
    )


def many_experts(
    flying, rate, queries, intra, prefix, resid, attn_gain, moe_gain, experts, weight, up, down
):
    length, width = queries.shape
    heads = width // HEAD
    count = lax.axis_size("ctx")
    inter = jnp.exp(jnp.cumsum(rate, axis=0))[:, :, None] * jnp.einsum(
        "thd,hde->the",
        queries.astype(F32).reshape(length, heads, HEAD),
        prefix,
        precision=lax.Precision.HIGHEST,
    )
    hres = resid.astype(F32) + rms_scale(intra + inter.reshape(length, width), attn_gain)
    normed = rms_scale(hres, moe_gain).astype(BF16)
    slots = flying * CAP_SRC
    chosen = experts.reshape(-1)
    onehot = (chosen[:, None] == jnp.arange(flying)[None, :]).astype(jnp.int32)
    slot = jnp.sum((jnp.cumsum(onehot, axis=0) - onehot) * onehot, axis=1)
    target = jnp.where(chosen < flying, chosen * CAP_SRC + slot, -1)
    hot = (target[None, :] == jnp.arange(slots)[:, None]).reshape(slots, length, 2)
    outbox = dot(hot.any(axis=2).astype(BF16), normed).astype(BF16)
    outbox = outbox.reshape(1, flying, CAP_SRC, width)
    mine = lax.dynamic_index_in_dim(
        lax.all_gather(outbox, "ctx", axis=0, tiled=True), lax.axis_index("ctx") // SHARDS, 1, False
    )
    hidden = jax.nn.gelu(dot(mine.reshape(count * CAP_SRC, width), up), approximate=True)
    part = dot(hidden.astype(BF16), down).astype(BF16).reshape(count, CAP_SRC, width)
    returned = lax.all_to_all(part, "ctx", split_axis=0, concat_axis=0, tiled=True)
    summed = returned.reshape(flying, SHARDS, CAP_SRC, width).astype(F32).sum(axis=1)
    mixed = lax.dot_general(
        jnp.where(hot, weight[None], 0.0).sum(axis=2),
        summed.reshape(slots, width),
        (((0,), (0,)), ((), ())),
        precision=lax.Precision.HIGHEST,
    )
    return passed_along((hres + mixed).astype(BF16)[None], "section", 1)


def solution(mesh):
    return jax.shard_map(
        local,
        mesh=mesh,
        in_specs=(
            P("section", "ctx", None),
            P("section", "ctx", None),
            P("section", "ctx", None),
            P("section", "ctx", None),
            P("section", "ctx", None),
            P("section", None),
            P("section", None),
            P("section", "ctx", None),
            P("section", "ctx", None),
            P("section", None, "ctx"),
            P("section", "ctx", None),
        ),
        out_specs=P("section", "ctx", None),
        check_vma=False,
    )
```

```python
import jax
import jax.numpy as jnp
from jax import lax
from jax.experimental import pallas as pl
from jax.experimental.pallas import tpu as pltpu
from jax.sharding import PartitionSpec as P

HEAD = 128
SHARDS = 8
CAP_SRC = 16
GROUP = 8
CHUNKS = 3
PARTS = 1
FETCH_MIB = 42

F32, BF16 = jnp.float32, jnp.bfloat16


def dot(a, b, dims=((1,), (0,))):
    return lax.dot_general(a, b, (dims, ((), ())), preferred_element_type=F32)


def split(a):
    hi = a.astype(BF16)
    return hi, (a - hi.astype(F32)).astype(BF16)


def cumul_rows(rate_ref):
    length = rate_ref.shape[1]
    upper = (
        lax.broadcasted_iota(jnp.int32, (length, length), 0)
        <= lax.broadcasted_iota(jnp.int32, (length, length), 1)
    ).astype(F32)
    return lax.dot_general(
        rate_ref[...], upper, (((1,), (0,)), ((), ())), precision=lax.Precision.HIGHEST,
        preferred_element_type=F32,
    )


def in_vmem(x):
    return pltpu.with_memory_space_constraint(x, pltpu.VMEM)


VMEM_SPEC = pl.BlockSpec(memory_space=pltpu.VMEM)
HBM_SPEC = pl.BlockSpec(memory_space=pltpu.HBM)
ANY_SPEC = pl.BlockSpec(memory_space=pl.ANY)
SMEM_SPEC = pl.BlockSpec(memory_space=pltpu.SMEM)


def state_kernel(
    half_ref, rate_hbm, k_hbm, v_hbm, state_hbm, decay_hbm,
    rate_ref, k_ref, v_ref, state_ref, decay_ref, cum_ref, sems,
):
    groups = k_ref.shape[0]
    length = rate_ref.shape[1]
    span = GROUP * HEAD
    rates = pltpu.make_async_copy(rate_hbm, rate_ref, sems.at[3, 0])
    rates.start()

    def fetch(kind, g):
        source, target = ((k_hbm, k_ref), (v_hbm, v_ref))[kind]
        column = pl.multiple_of((half_ref[0] * groups + g) * span, span)
        return pltpu.make_async_copy(
            source.at[:, pl.ds(column, span)], target.at[g], sems.at[kind, g]
        )

    def store(g):
        at = pl.ds(g * GROUP, GROUP)
        return pltpu.make_async_copy(state_ref.at[at], state_hbm.at[at], sems.at[2, g])

    for g in range(groups):
        for kind in range(2):
            fetch(kind, g).start()
    rates.wait()
    cum_ref[...] = cumul_rows(rate_ref)
    decay_ref[...] = jnp.broadcast_to(jnp.exp(cum_ref[:, length - 1 :]), decay_ref.shape)
    decays = pltpu.make_async_copy(decay_ref, decay_hbm, sems.at[3, 1])
    decays.start()
    for g in range(groups):
        row = pl.multiple_of((half_ref[0] * groups + g) * GROUP, GROUP)
        cum = cum_ref[pl.ds(row, GROUP), :]
        tail = jnp.exp(cum[:, length - 1 :] - cum)
        for kind in range(2):
            fetch(kind, g).wait()
        for j in range(GROUP):
            cols = slice(j * HEAD, (j + 1) * HEAD)
            turned = k_ref[g, :, cols].T.astype(F32) * tail[j : j + 1, :]
            hi, lo = split(turned)
            v = v_ref[g, :, cols]
            state_ref[g * GROUP + j] = dot(hi, v) + dot(lo, v)
        store(g).start()
    for g in range(groups):
        store(g).wait()
    decays.wait()


def half_state(half, rate, keys, values):
    length, width = keys.shape
    heads = width // HEAD
    groups = heads // 2 // GROUP
    return pl.pallas_call(
        state_kernel,
        in_specs=[SMEM_SPEC, HBM_SPEC, HBM_SPEC, HBM_SPEC],
        out_specs=[HBM_SPEC, HBM_SPEC],
        out_shape=[
            jax.ShapeDtypeStruct((heads // 2, HEAD, HEAD), F32),
            jax.ShapeDtypeStruct((heads, HEAD), F32),
        ],
        scratch_shapes=[
            pltpu.VMEM((heads, length), F32),
            pltpu.VMEM((groups, length, GROUP * HEAD), BF16),
            pltpu.VMEM((groups, length, GROUP * HEAD), BF16),
            pltpu.VMEM((heads // 2, HEAD, HEAD), F32),
            pltpu.VMEM((heads, HEAD), F32),
            pltpu.VMEM((heads, length), F32),
            pltpu.SemaphoreType.DMA((4, max(groups, 2))),
        ],
        name="half_state",
    )(half, rate, keys, values)


def intra_kernel(first, rate_ref, q_hbm, k_hbm, v_hbm, *refs):
    out_hbm, q_ref, k_ref, v_ref, out_ref, sems = refs[-6:]
    groups = sems.shape[1]
    length = rate_ref.shape[1]
    span = GROUP * HEAD

    def fetch(kind, g):
        source, target = ((q_hbm, q_ref), (k_hbm, k_ref), (v_hbm, v_ref))[kind]
        return pltpu.make_async_copy(
            source.at[:, pl.ds((first + g) * span, span)], target.at[g], sems.at[kind, g]
        )

    def store(g):
        at = pl.ds((first + g) * span, span)
        return pltpu.make_async_copy(out_ref.at[g], out_hbm.at[:, at], sems.at[3, g])

    for g in range(groups):
        for kind in range(3):
            fetch(kind, g).start()
    cumul = cumul_rows(rate_ref)
    lower = lax.broadcasted_iota(jnp.int32, (length, length), 0) >= lax.broadcasted_iota(
        jnp.int32, (length, length), 1
    )
    for g in range(groups):
        for kind in range(3):
            fetch(kind, g).wait()
        for j in range(GROUP):
            head = (first + g) * GROUP + j
            cols = slice(j * HEAD, (j + 1) * HEAD)
            across = jnp.broadcast_to(cumul[head : head + 1, :], (length, length))
            weights = jnp.exp(jnp.where(lower, across.T - across, -1e30))
            scores = dot(q_ref[g, :, cols], k_ref[g, :, cols], ((1,), (1,)))
            hi, lo = split(scores * weights)
            v = v_ref[g, :, cols]
            out_ref[g, :, cols] = dot(hi, v) + dot(lo, v)
        store(g).start()
    for g in range(groups):
        store(g).wait()


def intra_attention(part, parts, rate, queries, keys, values, out):
    length, width = keys.shape
    groups = width // HEAD // GROUP // parts
    piece = (groups, length, GROUP * HEAD)
    return pl.pallas_call(
        lambda *refs: intra_kernel(part * groups, *refs),
        in_specs=[VMEM_SPEC] + [HBM_SPEC] * (3 + len(out)),
        out_specs=HBM_SPEC,
        out_shape=jax.ShapeDtypeStruct((length, width), F32),
        scratch_shapes=[pltpu.VMEM(piece, BF16)] * 3
        + [pltpu.VMEM(piece, F32), pltpu.SemaphoreType.DMA((4, groups))],
        input_output_aliases={4: 0} if out else {},
        name="intra_attention",
    )(rate, queries, keys, values, *out)


def select_kernel(
    experts_ref, weight_ref, rate_ref, q_ref, resid_ref, intra_ref,
    wcol_ref, token_ref, growth_ref, q_out, resid_out, intra_out, at_ref, at_smem, sem,
):
    slots = wcol_ref.shape[0]
    length = experts_ref.shape[1]
    before = (
        lax.broadcasted_iota(jnp.int32, (length, length), 0)
        < lax.broadcasted_iota(jnp.int32, (length, length), 1)
    ).astype(BF16)
    named = experts_ref[...] == 0
    taken = jnp.max(named.astype(F32), axis=0, keepdims=True)
    slot = dot(jnp.broadcast_to(taken, (8, length)).astype(BF16), before)[0:1, :]
    slot = jnp.where(taken > 0, slot, -1.0)
    hot = lax.broadcasted_iota(jnp.int32, (slots, length), 0).astype(F32) == slot
    weight = jnp.sum(jnp.where(named, weight_ref[...], 0.0), axis=0, keepdims=True)
    weight = jnp.sum(jnp.where(hot, weight, 0.0), axis=1, keepdims=True)
    wcol_ref[...] = jnp.broadcast_to(weight, wcol_ref.shape)
    at = lax.broadcasted_iota(jnp.int32, (slots, length), 1).astype(F32) + 1.0
    token = jnp.sum(jnp.where(hot, at, 0.0), axis=1, keepdims=True) - 1.0
    token_ref[...] = jnp.broadcast_to(token, token_ref.shape)
    at_ref[...] = jnp.broadcast_to(jnp.maximum(token, 0.0), at_ref.shape).astype(jnp.int32)
    known = pltpu.make_async_copy(at_ref, at_smem, sem)
    known.start()
    growth = lax.dot_general(
        hot.astype(F32), jnp.exp(cumul_rows(rate_ref)), (((1,), (1,)), ((), ())),
        precision=lax.Precision.HIGHEST, preferred_element_type=F32,
    )
    for head in range(growth.shape[1]):
        growth_ref[:, head * HEAD : (head + 1) * HEAD] = jnp.broadcast_to(
            growth[:, head : head + 1], (slots, HEAD)
        )
    hot = hot.astype(BF16)
    q_out[...] = dot(hot, q_ref[...]).astype(BF16)
    resid_out[...] = dot(hot, resid_ref[...])
    known.wait()
    for s in range(slots):
        intra_out[s : s + 1, :] = intra_ref[pl.ds(at_smem[s, 0], 1), :]


def select(experts, weight, rate, queries, resid, intra):
    _, width = queries.shape
    return pl.pallas_call(
        select_kernel,
        in_specs=[VMEM_SPEC] * 6,
        out_specs=[VMEM_SPEC] * 6,
        out_shape=[
            jax.ShapeDtypeStruct((CAP_SRC, 128), F32),
            jax.ShapeDtypeStruct((CAP_SRC, 128), F32),
            jax.ShapeDtypeStruct((CAP_SRC, width), F32),
            jax.ShapeDtypeStruct((CAP_SRC, width), BF16),
            jax.ShapeDtypeStruct((CAP_SRC, width), F32),
            jax.ShapeDtypeStruct((CAP_SRC, width), F32),
        ],
        scratch_shapes=[
            pltpu.VMEM((CAP_SRC, 128), jnp.int32),
            pltpu.SMEM((CAP_SRC, 128), jnp.int32),
            pltpu.SemaphoreType.DMA,
        ],
        name="select",
    )(experts, weight, rate, queries, resid, intra)


def each_state(core_ref, keeps, gots, chunks, use):
    steps, per = len(keeps), keeps[0].shape[0]
    half = chunks * per
    for late in range(steps - chunks + 1):

        @pl.when(core_ref[1] == late)
        def _():
            for n in range(2):
                start = lax.rem(core_ref[0] + n, 2) * half
                for c in range(chunks):
                    for j in range(per):
                        column = pl.multiple_of((start + c * per + j) * HEAD, HEAD)
                        use(pl.ds(column, HEAD), (keeps, gots)[n][c + late][j])


def rows_kernel(chunks, steps, core_ref, growth_ref, q_ref, resid_ref, intra_ref, *refs):
    keeps, gots, refs = refs[:steps], refs[steps : 2 * steps], refs[2 * steps :]
    again_ref, mgain_ref, outbox_ref, picked_ref = refs

    def use(cols, state):
        hi, lo = split(state)
        q = q_ref[:, cols]
        picked_ref[:, cols] = intra_ref[:, cols] + growth_ref[:, cols] * (dot(q, hi) + dot(q, lo))

    each_state(core_ref, keeps, gots, chunks, use)
    x = picked_ref[...]
    scale = lax.rsqrt(jnp.mean(x * x, axis=-1, keepdims=True) + 1e-06)
    hres = resid_ref[...] + x * scale * again_ref[...]
    picked_ref[...] = hres
    scale = lax.rsqrt(jnp.mean(hres * hres, axis=-1, keepdims=True) + 1e-06)
    outbox_ref[...] = (hres * scale * mgain_ref[...]).astype(BF16)


def selected_rows(core, growth, queries, resid, intra, keeps, gots, attn_gain, moe_gain):
    slots, width = queries.shape
    steps = len(keeps)
    args = [growth, queries, resid, intra, *keeps, *gots, attn_gain, moe_gain]
    return pl.pallas_call(
        lambda *refs: rows_kernel(CHUNKS, steps, *refs),
        in_specs=[SMEM_SPEC] + [VMEM_SPEC] * len(args),
        out_specs=[VMEM_SPEC] * 2,
        out_shape=[pltpu.VMEM((slots, width), BF16), pltpu.VMEM((slots, width), F32)],
        compiler_params=pltpu.CompilerParams(vmem_limit_bytes=8 << 20),
        name="selected_rows",
    )(core, *[in_vmem(a) for a in args])


def finish_kernel(chunks, steps, core_ref, rate_ref, q_ref, intra_ref, *refs):
    keeps, gots, refs = refs[:steps], refs[steps : 2 * steps], refs[2 * steps :]
    resid_ref, again_ref, early_ref, attn_ref, scale_ref = refs
    length, width = resid_ref.shape
    growth = jnp.exp(cumul_rows(rate_ref)).T
    for head in range(width // HEAD):
        scale_ref[:, head * HEAD : (head + 1) * HEAD] = jnp.broadcast_to(
            growth[:, head : head + 1], (length, HEAD)
        )

    def use(cols, state):
        hi, lo = split(state)
        q = q_ref[:, cols]
        attn_ref[:, cols] = intra_ref[:, cols] + scale_ref[:, cols] * (dot(q, hi) + dot(q, lo))

    each_state(core_ref, keeps, gots, chunks, use)
    rows = 16

    def norm(r, carry):
        at = pl.ds(pl.multiple_of(r * rows, rows), rows)
        x = attn_ref[at, :]
        scale = lax.rsqrt(jnp.mean(x * x, axis=-1, keepdims=True) + 1e-06)
        hres = resid_ref[at, :].astype(F32) + x * scale * again_ref[...]
        early_ref[at, :] = hres.astype(BF16)
        return carry

    lax.fori_loop(0, length // rows, norm, 0)


def finish(core, rate, queries, intra, keeps, gots, resid, attn_gain):
    length, width = queries.shape
    steps = len(keeps)
    args = [rate, queries, intra, *keeps, *gots, resid, attn_gain]
    return pl.pallas_call(
        lambda *refs: finish_kernel(CHUNKS, steps, *refs),
        in_specs=[SMEM_SPEC] + [VMEM_SPEC] * len(args),
        out_specs=VMEM_SPEC,
        out_shape=pltpu.VMEM((length, width), BF16),
        scratch_shapes=[pltpu.VMEM((length, width), F32), pltpu.VMEM((length, width), F32)],
        compiler_params=pltpu.CompilerParams(vmem_limit_bytes=14 << 20),
        name="finish",
    )(core, *[in_vmem(a) for a in args])


def late_kernel(count, picked_ref, wcol_ref, token_ref, *refs):
    parts, out_ref = refs[:count], refs[count]
    width = picked_ref.shape[1]
    total = parts[0][...].astype(F32)
    for part in parts[1:]:
        total = total + part[...].astype(F32)
    out_ref[:, :width] = (picked_ref[...] + wcol_ref[:, :1] * total).astype(BF16)
    out_ref[:, width:] = token_ref[...].astype(BF16)


def late_rows(picked, wcol, token, parts):
    slots, width = picked.shape
    return pl.pallas_call(
        lambda *refs: late_kernel(len(parts), *refs),
        in_specs=[VMEM_SPEC] * (3 + len(parts)),
        out_specs=VMEM_SPEC,
        out_shape=pltpu.VMEM((slots, width + 128), BF16),
        compiler_params=pltpu.CompilerParams(vmem_limit_bytes=8 << 20),
        name="late_rows",
    )(in_vmem(picked), wcol, token, *[in_vmem(p) for p in parts])


def merge_kernel(early_ref, late_ref, out_hbm, out_ref, sems):
    length, width = early_ref.shape
    slots = late_ref.shape[0]
    parts = sems.shape[0]
    span = width // parts
    token = late_ref[:, width:].astype(F32)
    found = token == lax.broadcasted_iota(jnp.int32, (slots, length), 1).astype(F32)
    found = found.astype(BF16)
    down = ((0,), (0,))
    hit = dot(found, jnp.ones((slots, 128), BF16), down)[:, :1] > 0.5

    def store(i):
        at = pl.ds(i * span, span)
        return pltpu.make_async_copy(out_ref.at[:, at], out_hbm.at[:, at], sems.at[i])

    for i in range(parts):
        at = slice(i * span, (i + 1) * span)
        rows = dot(found, late_ref[:, at], down)
        out_ref[:, at] = jnp.where(hit, rows, early_ref[:, at].astype(F32)).astype(BF16)
        store(i).start()
    for i in range(parts):
        store(i).wait()


def merged(early, late):
    return pl.pallas_call(
        merge_kernel,
        in_specs=[VMEM_SPEC] * 2,
        out_specs=HBM_SPEC,
        out_shape=jax.ShapeDtypeStruct(early.shape, BF16),
        scratch_shapes=[pltpu.VMEM(early.shape, BF16), pltpu.SemaphoreType.DMA((4,))],
        compiler_params=pltpu.CompilerParams(vmem_limit_bytes=8 << 20),
        name="merged",
    )(in_vmem(early), in_vmem(late))


def fetch_kernel(up_hbm, down_hbm, up_ref, down_ref, sems):
    copies = [
        pltpu.make_async_copy(up_hbm, up_ref, sems.at[0]),
        pltpu.make_async_copy(down_hbm, down_ref, sems.at[1]),
    ]
    for copy in copies:
        copy.start()
    for copy in copies:
        copy.wait()


def fetch(up, down):
    return pl.pallas_call(
        fetch_kernel,
        in_specs=[HBM_SPEC] * 2,
        out_specs=[VMEM_SPEC] * 2,
        out_shape=[pltpu.VMEM(up.shape, BF16), pltpu.VMEM(down.shape, BF16)],
        scratch_shapes=[pltpu.SemaphoreType.DMA((2,))],
        compiler_params=pltpu.CompilerParams(vmem_limit_bytes=FETCH_MIB << 20),
        name="fetch",
    )(up, down)


def expert_kernel(count, *refs):
    row_refs = refs[:count]
    up_ref, down_ref, mine_ref, other_ref, rows_ref, hidden_ref = refs[count:]
    half = mine_ref.shape[0]
    each = row_refs[0].shape[0]
    for n, ref in enumerate(row_refs):
        rows_ref[n * each : (n + 1) * each, :] = ref[...]
    hidden = dot(rows_ref[...], up_ref[...])
    hidden_ref[...] = jax.nn.gelu(hidden, approximate=True).astype(BF16)
    parts = 4
    length = down_ref.shape[1] // parts
    for i in range(parts):
        at = slice(i * length, (i + 1) * length)
        part = dot(hidden_ref[...], down_ref[:, at]).astype(BF16)
        mine_ref[:, at] = part[:half]
        other_ref[:, at] = part[half:]


def expert_rows(rows, up, down):
    width, units = up.shape
    total = sum(r.shape[0] for r in rows)
    return pl.pallas_call(
        lambda *refs: expert_kernel(len(rows), *refs),
        in_specs=[VMEM_SPEC] * (len(rows) + 2),
        out_specs=[VMEM_SPEC] * 2,
        out_shape=[pltpu.VMEM((total // 2, width), BF16)] * 2,
        scratch_shapes=[pltpu.VMEM((total, width), BF16), pltpu.VMEM((total, units), BF16)],
        compiler_params=pltpu.CompilerParams(vmem_limit_bytes=12 << 20),
        name="expert_rows",
    )(*[in_vmem(r) for r in rows], up, down)


def passed_along(value, axis, steps):
    count = lax.axis_size(axis)
    pairs = [(source, (source + steps) % count) for source in range(count)]
    return lax.ppermute(value, axis, pairs)


def swapped(value):
    count = lax.axis_size("ctx")
    return lax.ppermute(value, "ctx", [(i, i ^ 1) for i in range(count)])


def chain_prefix(mine, partner, decay, decay_partner, chip, chips, first, scale):
    heads = mine.shape[0]
    per = heads // CHUNKS
    keeps, gives, before = [], [], None

    def chunk(index):
        place = jnp.clip(index, 0, CHUNKS - 1) * per
        cut = [
            lax.dynamic_slice_in_dim(a, place, per, 0)
            for a in (mine, partner, decay, decay_partner)
        ]
        state0, state1 = jnp.where(first, cut[0], cut[1]), jnp.where(first, cut[1], cut[0])
        decay0, decay1 = jnp.where(first, cut[2], cut[3]), jnp.where(first, cut[3], cut[2])
        return state0, state1, decay0[:, None, :], decay1[:, None, :]

    for step in range(CHUNKS + chips - 2):
        state0, state1, decay0, decay1 = chunk(step - chip)
        gone = (decay1 * state0 + state1) * scale
        if before is not None:
            gone = (decay0 * decay1) * before.astype(F32) + gone
        pairs = [
            (2 * z + core, 2 * z + 2 + core)
            for z in range(chips - 1)
            if 0 <= step - z < CHUNKS
            for core in range(2)
        ]
        gone = gone.astype(jnp.float16)
        if step >= 2:
            gone, keeps[-1], gives[-1] = lax.optimization_barrier((gone, keeps[-1], gives[-1]))
        before = lax.ppermute(gone, "ctx", pairs)
        state0, _, decay0, _ = chunk(step - jnp.maximum(chip - 1, 0))
        prefix = lax.optimization_barrier(before).astype(F32) * (1.0 / scale)
        after0 = decay0 * prefix + state0
        keeps.append(jnp.where(first, prefix, after0))
        gives.append(jnp.where(first, after0, prefix))
    return keeps, [swapped(give) for give in gives]


def local(
    resid,
    queries,
    keys,
    values,
    log_decay,
    attn_gain,
    moe_gain,
    experts,
    combine_weight,
    w_up,
    w_down,
):
    return layer(
        resid[0], queries[0], keys[0], values[0], log_decay[0], attn_gain, moe_gain,
        experts[0], combine_weight[0], w_up[0], w_down[0],
    )


def layer(resid, queries, keys, values, rate, attn_gain, moe_gain, experts, weight, up, down):
    length, width = queries.shape
    count = lax.axis_size("ctx")
    me = lax.axis_index("ctx")
    chips, chip, core = count // 2, me // 2, me % 2
    half = width // HEAD // 2
    first = core == 0
    core1 = core.astype(jnp.int32)[None]
    turned = rate.T

    other, decay = half_state(1 - core1, turned, keys, values)
    partner, decay_partner = swapped(other), swapped(decay)
    mine, _ = half_state(core1, turned, keys, values)
    decay, decay_partner = (
        lax.dynamic_slice_in_dim(a, core * half, half, 0) for a in (decay, decay_partner)
    )
    scale = 1.0
    while 36.0 * count * length * scale > 65000.0:
        scale = scale / 2
    keeps, gots = chain_prefix(
        mine, partner, decay, decay_partner, chip, chips, first, scale
    )
    late_by = jnp.maximum(chip - 1, 0)
    intra = []
    for part in range(PARTS):
        intra = [intra_attention(part, PARTS, turned, queries, keys, values, intra)]
    intra = intra[0]
    flying = count // SHARDS
    if flying > 1:
        keep, got = (
            lax.dynamic_slice_in_dim(jnp.concatenate(a), late_by * (half // CHUNKS), half, 0)
            for a in (keeps, gots)
        )
        prefix = jnp.where(first, jnp.concatenate([keep, got]), jnp.concatenate([got, keep]))
        return many_experts(
            flying, rate, queries, intra, prefix, resid,
            attn_gain, moe_gain, experts, weight, up, down,
        )
    where = jnp.stack([core, late_by]).astype(jnp.int32)
    wcol, token, growth, q_rows, resid_rows, intra_rows = select(
        experts.T, weight.T, turned, queries, resid, intra
    )
    outbox, picked = selected_rows(
        where, growth, q_rows, resid_rows, intra_rows, keeps, gots, attn_gain, moe_gain
    )
    own = [outbox] + [
        lax.ppermute(outbox, "ctx", [(i, i ^ (2 * d)) for i in range(count)])
        for d in range(1, chips)
    ]
    early = finish(where, turned, queries, intra, keeps, gots, resid, attn_gain)
    early = passed_along(early, "section", 1)
    up, down = fetch(up, down)
    others = [swapped(r) for r in own]
    mine, other = expert_rows(own + others, up, down)
    pair = (mine.astype(F32) + swapped(other).astype(F32)).astype(BF16)
    pair = pair.reshape(chips, CAP_SRC, width)
    backs = [
        lax.ppermute(pair[d], "ctx", [(i, i ^ (2 * d)) for i in range(count)])
        for d in range(1, chips)
    ]
    late = passed_along(late_rows(picked, wcol, token, [pair[0], *backs]), "section", 1)
    return merged(early, late)[None]


def rms_scale(values_in, gain):
    return (
        values_in
        * lax.rsqrt(jnp.mean(values_in * values_in, axis=-1, keepdims=True) + 1e-06)
        * gain
    )


def many_experts(
    flying, rate, queries, intra, prefix, resid, attn_gain, moe_gain, experts, weight, up, down
):
    length, width = queries.shape
    heads = width // HEAD
    count = lax.axis_size("ctx")
    inter = jnp.exp(jnp.cumsum(rate, axis=0))[:, :, None] * jnp.einsum(
        "thd,hde->the",
        queries.astype(F32).reshape(length, heads, HEAD),
        prefix,
        precision=lax.Precision.HIGHEST,
    )
    hres = resid.astype(F32) + rms_scale(intra + inter.reshape(length, width), attn_gain)
    normed = rms_scale(hres, moe_gain).astype(BF16)
    slots = flying * CAP_SRC
    chosen = experts.reshape(-1)
    onehot = (chosen[:, None] == jnp.arange(flying)[None, :]).astype(jnp.int32)
    slot = jnp.sum((jnp.cumsum(onehot, axis=0) - onehot) * onehot, axis=1)
    target = jnp.where(chosen < flying, chosen * CAP_SRC + slot, -1)
    hot = (target[None, :] == jnp.arange(slots)[:, None]).reshape(slots, length, 2)
    outbox = dot(hot.any(axis=2).astype(BF16), normed).astype(BF16)
    outbox = outbox.reshape(1, flying, CAP_SRC, width)
    mine = lax.dynamic_index_in_dim(
        lax.all_gather(outbox, "ctx", axis=0, tiled=True), lax.axis_index("ctx") // SHARDS, 1, False
    )
    hidden = jax.nn.gelu(dot(mine.reshape(count * CAP_SRC, width), up), approximate=True)
    part = dot(hidden.astype(BF16), down).astype(BF16).reshape(count, CAP_SRC, width)
    returned = lax.all_to_all(part, "ctx", split_axis=0, concat_axis=0, tiled=True)
    summed = returned.reshape(flying, SHARDS, CAP_SRC, width).astype(F32).sum(axis=1)
    mixed = lax.dot_general(
        jnp.where(hot, weight[None], 0.0).sum(axis=2),
        summed.reshape(slots, width),
        (((0,), (0,)), ((), ())),
        precision=lax.Precision.HIGHEST,
    )
    return passed_along((hres + mixed).astype(BF16)[None], "section", 1)


def solution(mesh):
    return jax.shard_map(
        local,
        mesh=mesh,
        in_specs=(
            P("section", "ctx", None),
            P("section", "ctx", None),
            P("section", "ctx", None),
            P("section", "ctx", None),
            P("section", "ctx", None),
            P("section", None),
            P("section", None),
            P("section", "ctx", None),
            P("section", "ctx", None),
            P("section", None, "ctx"),
            P("section", "ctx", None),
        ),
        out_specs=P("section", "ctx", None),
        check_vma=False,
    )
```
